32 devices in a mesh: dp: 8 (over z, core), seq: 4 (over y, x).
Axes of the slice: x: 2, y: 2, z: 4, core: 2. Of those that a mesh axis runs over, the one named last changes fastest.
Arguments:
- block_in: bfloat16 [3, 8, 2048, 512], P(None, 'dp', 'seq'), may hold values from -6 to 6
- routes: int32 [3, 8, 2048, 2], P(None, 'dp', 'seq'), may hold values from 0 to 7, all different within a row
- segments: int32 [3, 8, 2048], P(None, 'dp'), may hold values from 0 to 7, never falling along the last dimension, each value on 1 to 1536 neighbouring positions
- cotangent: bfloat16 [3, 8, 2048, 512], P(None, 'dp', 'seq'), may hold values from -6 to 6
- ln1_gain: bfloat16 [512], P(('dp', 'seq')), may hold values from 0.5 to 1.5
- ln1_bias: bfloat16 [512], P(('dp', 'seq')), may hold values from -0.5 to 0.5
- query_weight: bfloat16 [512, 512], P(('dp', 'seq')), may hold values from -0.25 to 0.25
- kv_weight: bfloat16 [512, 128], P(('dp', 'seq')), may hold values from -0.25 to 0.25
- router_weight: bfloat16 [512, 8], P(('dp', 'seq')), may hold values from -0.25 to 0.25
- out_weight: bfloat16 [512, 512], P(('dp', 'seq')), may hold values from -4 to 4
- ln2_gain: bfloat16 [512], P(('dp', 'seq')), may hold values from 0.5 to 1.5
- ln2_bias: bfloat16 [512], P(('dp', 'seq')), may hold values from -0.5 to 0.5
- up_weight: bfloat16 [512, 2048], P(('dp', 'seq')), may hold values from -0.25 to 0.25
- up_bias: bfloat16 [2048], P(('dp', 'seq')), may hold values from -0.5 to 0.5
- down_weight: bfloat16 [2048, 512], P(('dp', 'seq')), may hold values from -0.1875 to 0.1875
- down_bias: bfloat16 [512], P(('dp', 'seq')), may hold values from -0.5 to 0.5
Outputs:
- block_out: bfloat16 [3, 8, 2048, 512], P(None, 'dp', 'seq')
- grad_in: float32 [3, 8, 2048, 512], P(None, 'dp', 'seq')
- grad_ln1_gain: float32 [512], P(('dp', 'seq'))
- grad_ln1_bias: float32 [512], P(('dp', 'seq'))
- grad_query_weight: float32 [512, 512], P(('dp', 'seq'))
- grad_kv_weight: float32 [512, 128], P(('dp', 'seq'))
- grad_router_weight: float32 [512, 8], P(('dp', 'seq'))
- grad_out_weight: float32 [512, 512], P(('dp', 'seq'))
- grad_ln2_gain: float32 [512], P(('dp', 'seq'))
- grad_ln2_bias: float32 [512], P(('dp', 'seq'))
- grad_up_weight: float32 [512, 2048], P(('dp', 'seq'))
- grad_up_bias: float32 [2048], P(('dp', 'seq'))
- grad_down_weight: float32 [2048, 512], P(('dp', 'seq'))
- grad_down_bias: float32 [512], P(('dp', 'seq'))
The draws below stay inside these ranges and needn't reach their ends.
Inputs may be any that keep to these rules, and one draw needn't show every extreme that they name: `routes`: each token names two different experts; every expert is named by some token. `segments`: within a sequence the ids never fall; a document has 1 to 1536 tokens, and one has exactly 1536.
All inputs are finite; a program needn't handle non-finite values.
Results may differ from the reference program's by a relative error of at most 0.015.
Values may be sent and summed in bfloat16 or wider, within the bound.
No kernel may reach another device: no remote copies, remote signals or barrier semaphores. Data moves between devices by JAX's collectives and lax.ppermute only.
A program may use at most 192 MiB of HBM per device.

```python
import math
import jax
import jax.numpy as jnp
import numpy as np
from jax import lax

D = 512
FF = 2048
EXPERTS = 8
HEAD = 64
LEN = 2048
MICRO = 3
BATCH = 8
DOCS = 8
DOC_MOST = 1536


def block_levels(rng, extent, shards, low, top_value):
    level, own = 1.0, jax.random.fold_in(rng, 6)
    for axis_at, blocks in shards:
        steps = jnp.exp(jax.random.uniform(jax.random.fold_in(own, axis_at), (blocks,), jnp.float32, low / len(shards), top_value / len(shards)))
        level = level * jnp.repeat(steps, extent[axis_at] // blocks).reshape([-1 if axis == axis_at else 1 for axis in range(len(extent))])
    return level


def distinct(rng, rows, number_of, top, lift):
    sequence = jax.random.permutation(jax.random.fold_in(rng, 1), number_of)
    boost = sequence
    for power in range(3):
        boost = boost * boost // number_of
    boost = boost * lift // number_of
    tickets = jax.random.randint(jax.random.fold_in(rng, 2), (rows, number_of), 0, 4096) + boost
    fixed_rows = jax.random.permutation(jax.random.fold_in(rng, 3), rows)[jnp.arange(number_of) % rows]
    tickets = jnp.where(jnp.arange(rows)[:, None] == fixed_rows[None, :], 1 << 14, tickets)
    merit = tickets * number_of + jnp.arange(number_of)
    return lax.top_k(merit.astype(jnp.int32), top)[1].astype(jnp.int32)


def split_up(amount, total, limit, slope):
    weights = [(1 << 20) // math.isqrt(standing ** slope) + 1 for standing in range(2, amount + 1)]
    surplus, counts = total - limit - (amount - 1), [1] * (amount - 1)
    while surplus > 0:
        free = [i for i in range(amount - 1) if counts[i] < limit]
        mass, budget = sum([weights[i] for i in free]), surplus
        for i in free:
            extra = min(limit - counts[i], max(1, budget * weights[i] // mass), surplus)
            counts[i] = counts[i] + extra
            surplus = surplus - extra
    return np.array([limit] + counts)


def uneven_parts(key, number_of, total, most, slope):
    if number_of == 2:
        one = jax.random.randint(key, (), max(1, total - most), min(most, total - 1) + 1)
        return jnp.stack([one, total - one])
    tallies = jnp.asarray(split_up(number_of, total, most, slope), jnp.int32)
    couples = (number_of - 1) // 2
    source_of, sink = tallies[1:1 + 2 * couples:2], tallies[2:2 + 2 * couples:2]
    margin = jnp.minimum(source_of - 1, most - sink)
    shifted = jax.random.randint(jax.random.fold_in(key, 1), (couples,), 0, 1 << 20) % (margin + 1)
    tallies = tallies.at[1:1 + 2 * couples:2].set(source_of - shifted).at[2:2 + 2 * couples:2].set(sink + shifted)
    return tallies[jax.random.permutation(jax.random.fold_in(key, 2), number_of)]


def centred(key, dims, width, limit, cuts=(), held_as=jnp.bfloat16):
    entries = width * jax.random.normal(key, dims, jnp.float32)
    if cuts:
        entries = entries * block_levels(key, dims, cuts, -0.22, 0.18)
    return jnp.clip(entries, -limit, limit).astype(held_as)


def setup_inputs(seed: int = 0) -> dict:
    seeds = jax.random.split(jax.random.key(seed), 17)
    return {
        "block_in": centred(seeds[0], (MICRO, BATCH, LEN, D), 1.0, 6.0, ((1, 8), (2, 4))),
        "routes": distinct(seeds[1], MICRO * BATCH * LEN, EXPERTS, 2, 2048).reshape((MICRO, BATCH, LEN, 2)),
        "segments": jax.vmap(lambda own: jnp.searchsorted(jnp.cumsum(uneven_parts(own, DOCS, LEN, DOC_MOST, 1)), jnp.arange(LEN), side="right"))(jax.random.split(seeds[2], MICRO * BATCH)).reshape((MICRO, BATCH, LEN)).astype(jnp.int32),
        "cotangent": centred(seeds[3], (MICRO, BATCH, LEN, D), 1.0, 6.0, ((1, 8), (2, 4))),
        "ln1_gain": jnp.clip(1.0 + 0.1 * jax.random.normal(seeds[4], (D,), jnp.float32), 0.5, 1.5).astype(jnp.bfloat16),
        "ln1_bias": centred(seeds[5], (D,), 0.1, 0.5, ((0, 32),)),
        "query_weight": centred(seeds[6], (D, EXPERTS * HEAD), D ** -0.5, 0.25, ((0, 32),)),
        "kv_weight": centred(seeds[7], (D, 2 * HEAD), D ** -0.5, 0.25, ((0, 32),)),
        "router_weight": centred(seeds[8], (D, EXPERTS), D ** -0.5, 0.25, ((0, 32),)),
        "out_weight": centred(seeds[9], (EXPERTS * HEAD, D), 2 ** -0.5, 4.0, ((0, 32),)),
        "ln2_gain": jnp.clip(1.0 + 0.1 * jax.random.normal(seeds[10], (D,), jnp.float32), 0.5, 1.5).astype(jnp.bfloat16),
        "ln2_bias": centred(seeds[11], (D,), 0.1, 0.5, ((0, 32),)),
        "up_weight": centred(seeds[12], (D, FF), D ** -0.5, 0.25, ((0, 32),)),
        "up_bias": centred(seeds[13], (FF,), 0.1, 0.5, ((0, 32),)),
        "down_weight": centred(seeds[14], (FF, D), (FF // 2) ** -0.5, 0.1875, ((0, 32),)),
        "down_bias": centred(seeds[15], (D,), 0.1, 0.5, ((0, 32),)),
    }


EPS = 1e-05

@jax.custom_vjp
def low(v):
    return lax.optimization_barrier(v.astype(jnp.bfloat16)).astype(jnp.float32)

@jax.custom_vjp
def low_back(v):
    return v

def low_keep(v):
    return (low(v), None)

def low_pass(kept, grad):
    return (grad,)

def back_keep(v):
    return (v, None)

def back_low(kept, grad):
    return (low(grad),)
low.defvjp(low_keep, low_pass)
low_back.defvjp(back_keep, back_low)

def layer_norm(values, gain, shift):
    centered = values - lax.optimization_barrier(jnp.mean(values, -1, keepdims=True))
    inv_dev = lax.rsqrt(lax.optimization_barrier(jnp.mean(centered * centered, -1, keepdims=True)) + EPS)
    return centered * inv_dev * gain + shift

def project(left, right):
    return jnp.einsum('...d,de->...e', left, right, precision=lax.Precision.HIGHEST)

def widen(value):
    return value.astype(jnp.float32)

def reference(block_in, routes, segments, cotangent, ln1_gain, ln1_bias, query_weight, kv_weight, router_weight, out_weight, ln2_gain, ln2_bias, up_weight, up_bias, down_weight, down_bias):
    expert_ids = jnp.arange(EXPERTS, dtype=jnp.int32)
    pick_first = (routes[..., 0:1] == expert_ids).astype(jnp.float32)
    pick_second = (routes[..., 1:2] == expert_ids).astype(jnp.float32)
    query_block = min(512, LEN)
    block_count = LEN // query_block
    score_scale = HEAD ** (-0.5)
    key_pos = jnp.arange(LEN, dtype=jnp.int32)
    flat_count = MICRO * BATCH

    def attention(queries, keyvals, seg_ids):

        def one_sequence(item):
            seq_queries, seq_keyvals, seq_segs = item
            keys = seq_keyvals[:, :HEAD]
            values = seq_keyvals[:, HEAD:]

            def one_block(block_item):
                block_queries, start = block_item
                query_pos = start + jnp.arange(query_block, dtype=jnp.int32)
                query_segs = lax.dynamic_slice_in_dim(seq_segs, start, query_block)
                allowed = (query_segs[:, None] == seq_segs[None, :]) & (query_pos[:, None] >= key_pos[None, :])
                raw = jnp.einsum('qhd,kd->hqk', block_queries, keys, precision=lax.Precision.HIGHEST) * score_scale
                raw = low_back(raw)
                masked = jnp.where(allowed[None], raw, -1e+30)
                peak = lax.optimization_barrier(jnp.max(masked, -1, keepdims=True))
                expo = jnp.exp(masked - peak)
                probs = expo / lax.optimization_barrier(jnp.sum(expo, -1, keepdims=True))
                return low_back(jnp.einsum('hqk,kd->qhd', low(probs), values, precision=lax.Precision.HIGHEST))
            blocks = seq_queries.reshape(block_count, query_block, EXPERTS, HEAD)
            starts = jnp.arange(block_count, dtype=jnp.int32) * query_block
            return lax.map(jax.checkpoint(one_block), (blocks, starts)).reshape(LEN, EXPERTS, HEAD)
        return lax.map(one_sequence, (queries, keyvals, seg_ids))

    def forward(tokens_in, gain_one, shift_one, query_mat, keyval_mat, router_mat, output_mat, gain_two, shift_two, up_mat, up_shift, down_mat, down_shift):
        hidden_low = low(layer_norm(tokens_in, gain_one, shift_one))
        logits = project(hidden_low, router_mat)
        first = lax.optimization_barrier(jnp.sum(logits * pick_first, -1, keepdims=True))
        second = lax.optimization_barrier(jnp.sum(logits * pick_second, -1, keepdims=True))
        peak = jnp.maximum(first, second)
        exp_first = jnp.exp(first - peak)
        exp_second = jnp.exp(second - peak)
        gates = exp_first / (exp_first + exp_second) * pick_first + exp_second / (exp_first + exp_second) * pick_second
        queries = low_back(low(project(hidden_low, query_mat)))
        keyvals = low_back(low(project(hidden_low, keyval_mat)))
        mixed = attention(queries.reshape(flat_count, LEN, EXPERTS, HEAD), keyvals.reshape(flat_count, LEN, 2 * HEAD), segments.reshape(flat_count, LEN))
        mixed = mixed.reshape(MICRO, BATCH, LEN, EXPERTS, HEAD)
        routed = low_back(low(gates[..., None] * mixed)).reshape(MICRO, BATCH, LEN, EXPERTS * HEAD)
        attended = low_back(project(routed, output_mat))
        middle = tokens_in + attended
        second_low = low(layer_norm(middle, gain_two, shift_two))
        pre_act = low_back(project(second_low, up_mat) + up_shift)
        active = low_back(low(jax.nn.silu(pre_act)))
        branch = low_back(project(active, down_mat) + down_shift)
        return middle + branch
    weights = (widen(ln1_gain), widen(ln1_bias), widen(query_weight), widen(kv_weight), widen(router_weight), widen(out_weight), widen(ln2_gain), widen(ln2_bias), widen(up_weight), widen(up_bias), widen(down_weight), widen(down_bias))
    result, pullback = jax.vjp(forward, widen(block_in), *weights)
    grads = pullback(widen(cotangent))
    return (result.astype(jnp.bfloat16), grads[0], grads[1], grads[2], grads[3], grads[4], grads[5], grads[6], grads[7], grads[8], grads[9], grads[10], grads[11], grads[12])
```

```python
import functools

import jax
import jax.numpy as jnp
from jax import lax
from jax.experimental import pallas as pl
from jax.experimental.pallas import tpu as pltpu
from jax.sharding import PartitionSpec as P

EPS = 1e-05
LANES = 128
VMEM_LIMIT = 56 * 1024 * 1024
BF16 = jnp.bfloat16
F32 = jnp.float32


def call_params():
    return pltpu.CompilerParams(vmem_limit_bytes=VMEM_LIMIT)


def cost(flops, bytes_accessed, transcendentals=0):
    return pl.CostEstimate(
        flops=int(flops), bytes_accessed=int(bytes_accessed), transcendentals=int(transcendentals)
    )


def dot_nn(left, right):
    return lax.dot_general(left, right, (((1,), (0,)), ((), ())), preferred_element_type=F32)


def dot_nt(left, right):
    return lax.dot_general(left, right, (((1,), (1,)), ((), ())), preferred_element_type=F32)


def lanes_of(rows, width):
    return lax.broadcasted_iota(jnp.int32, (rows, width), 1)


def fold_matrix(width, head, shift):
    source = lax.broadcasted_iota(jnp.int32, (width, LANES), 0)
    target = lax.broadcasted_iota(jnp.int32, (width, LANES), 1)
    return jnp.where(target == shift + lax.rem(source, head), 1.0, 0.0).astype(BF16)


def unfold_matrix(width, head, shift):
    source = lax.broadcasted_iota(jnp.int32, (LANES, width), 1)
    target = lax.broadcasted_iota(jnp.int32, (LANES, width), 0)
    return jnp.where(target == shift + lax.rem(source, head), 1.0, 0.0).astype(BF16)


def rows_of(columns, picked):
    row = lax.broadcasted_iota(jnp.int32, (8, LANES), 0)
    lane = lax.broadcasted_iota(jnp.int32, (8, LANES), 1)
    chosen = jnp.zeros((8, LANES), F32)
    for at, column in enumerate(picked):
        chosen = jnp.where((row == at) & (lane == column), 1.0, chosen)
    return dot_nt(chosen.astype(BF16), columns)


def normalize(values):
    centered = values - jnp.mean(values, -1, keepdims=True)
    inv_dev = lax.rsqrt(jnp.mean(centered * centered, -1, keepdims=True) + EPS)
    return centered * inv_dev, inv_dev


def norm_back(grad, gain, normed, inv_dev):
    scaled = grad * gain
    return inv_dev * (
        scaled
        - jnp.mean(scaled, -1, keepdims=True)
        - normed * jnp.mean(scaled * normed, -1, keepdims=True)
    )


def pre_kernel(experts, head, x_ref, routes_ref, weight_ref, hidden_ref, kv_ref, q_ref, gate_ref):
    width = x_ref.shape[1]
    inner = experts * head
    extras = weight_ref[:, inner + LANES :]
    vectors = rows_of(extras, (experts, experts + 1))
    normed, _ = normalize(x_ref[...].astype(F32))
    hidden = (normed * vectors[0:1] + vectors[1:2]).astype(BF16)
    hidden_ref[...] = hidden
    big = dot_nn(hidden, weight_ref[...])
    rows = big.shape[0]
    kv_ref[...] = big[:, inner : inner + LANES].astype(BF16)
    logits = big[:, inner + LANES :]
    lane = lanes_of(rows, LANES)
    first, second = routes_ref[:, 0:1], routes_ref[:, 1:2]
    logit_one = jnp.sum(jnp.where(lane == first, logits, 0.0), -1, keepdims=True)
    logit_two = jnp.sum(jnp.where(lane == second, logits, 0.0), -1, keepdims=True)
    peak = jnp.maximum(logit_one, logit_two)
    exp_one = jnp.exp(logit_one - peak)
    exp_two = jnp.exp(logit_two - peak)
    total = exp_one + exp_two
    gate_ref[...] = jnp.where(lane == 0, exp_one / total, jnp.where(lane == 1, exp_two / total, 0.0))
    queries = (big[:, :inner] * (head**-0.5)).astype(BF16)
    owner = lax.div(lanes_of(rows, inner), head)
    fold = fold_matrix(inner, head, 0)
    zero = jnp.zeros_like(queries)
    q_ref[0] = dot_nn(jnp.where(owner == first, queries, zero), fold).astype(BF16)
    q_ref[1] = dot_nn(jnp.where(owner == second, queries, zero), fold).astype(BF16)


def masked(scores, start, key_at, query_at):
    keys = key_at + lax.broadcasted_iota(jnp.int32, scores.shape, 0)
    queries = query_at + lax.rem(
        lax.broadcasted_iota(jnp.int32, (1, scores.shape[1]), 1), scores.shape[1] // 2
    )
    return jnp.where((keys >= start) & (keys <= queries), scores, -1e30)


def attend_kernel(
    reach, chunk, head, low_ref, q_ref, start_ref, *rest
):
    pieces = rest[:reach]
    mixed_ref, lse_ref, kv_buf, vt_buf, peak_ref, total_ref, acc_ref = rest[reach:]
    seq, tile = pl.program_id(0), pl.program_id(1)
    local = pieces[0].shape[1]
    tokens = q_ref.shape[1]
    per_piece = local // chunk

    @pl.when(tile == 0)
    def _():
        for at in range(reach):
            for part in range(per_piece):
                block = pieces[at][0, part * chunk : (part + 1) * chunk, :]
                kv_buf[at * per_piece + part] = block
                row = lax.broadcasted_iota(jnp.int32, (LANES, chunk), 0)
                vt_buf[at * per_piece + part] = jnp.where(
                    row >= head, block.astype(F32).T, 0.0
                ).astype(BF16)

    queries = jnp.concatenate([q_ref[0], q_ref[1]], 0)
    start = start_ref[0]
    start = jnp.concatenate([start, start], 1)
    query_at = (reach - 1) * local + tile * tokens
    peak_ref[...] = jnp.full_like(peak_ref, -1e30)
    total_ref[...] = jnp.zeros_like(total_ref)
    acc_ref[...] = jnp.zeros_like(acc_ref)

    def step(at, carry):
        scores = masked(dot_nt(kv_buf[at], queries), start, at * chunk, query_at)
        peak = jnp.maximum(peak_ref[...], jnp.max(scores, 0, keepdims=True))
        fade = jnp.exp(peak_ref[...] - peak)
        expo = jnp.exp(scores - peak)
        total_ref[...] = total_ref[...] * fade + jnp.sum(expo, 0, keepdims=True)
        acc_ref[...] = acc_ref[...] * fade + dot_nn(vt_buf[at], expo.astype(BF16))
        peak_ref[...] = peak
        return carry

    low = low_ref[seq * pl.num_programs(1) + tile]
    high = (query_at + tokens - 1) // chunk + 1
    lax.fori_loop(low, high, step, 0)
    mixed = (acc_ref[...] / total_ref[...]).T
    mixed_ref[0] = mixed[:tokens]
    mixed_ref[1] = mixed[tokens:]
    lse_ref[0] = peak_ref[...] + jnp.log(total_ref[...])


def mid_kernel(
    experts,
    head,
    ff_chunk,
    x_ref,
    dy_ref,
    routes_ref,
    gate_ref,
    mixed_ref,
    weight_ref,
    down_ref,
    out_ref,
    grad_mid_ref,
    grad_mixed_ref,
    grad_logit_ref,
    d_weight_ref,
    d_down_ref,
    acc_out,
    acc_up,
    acc_down,
    acc_vec,
    acc_upb,
    branch_ref,
    gsec_ref,
):
    step, last = pl.program_id(0), pl.num_programs(0) - 1
    rows, width = x_ref.shape
    inner = experts * head
    ff = down_ref.shape[0]

    @pl.when(step == 0)
    def _():
        acc_out[...] = jnp.zeros_like(acc_out)
        acc_up[...] = jnp.zeros_like(acc_up)
        acc_down[...] = jnp.zeros_like(acc_down)
        acc_vec[...] = jnp.zeros_like(acc_vec)
        acc_upb[...] = jnp.zeros_like(acc_upb)

    vectors = rows_of(weight_ref[:, width + ff :], (0, 1, 2))
    gain, shift, down_bias = vectors[0:1], vectors[1:2], vectors[2:3]
    first, second = routes_ref[:, 0:1], routes_ref[:, 1:2]
    gate_one, gate_two = gate_ref[:, 0:1], gate_ref[:, 1:2]
    owner = lax.div(lanes_of(rows, inner), head)
    unfold = unfold_matrix(inner, head, head)
    fold = fold_matrix(inner, head, head)
    mixed_one, mixed_two = mixed_ref[0], mixed_ref[1]
    routed_one = dot_nn((gate_one * mixed_one).astype(BF16), unfold)
    routed_two = dot_nn((gate_two * mixed_two).astype(BF16), unfold)
    routed = jnp.where(
        owner == first, routed_one, jnp.where(owner == second, routed_two, 0.0)
    )
    middle = x_ref[...].astype(F32) + dot_nn(routed.astype(BF16), weight_ref[:, :width])
    normed, inv_dev = normalize(middle)
    second_low = (normed * gain + shift).astype(BF16)
    second_t = (normed * gain + shift).T.astype(BF16)
    dy = dy_ref[...]
    dy_wide = dy.astype(F32)
    dy_t = dy_wide.T.astype(BF16)
    branch_ref[...] = middle + down_bias
    gsec_ref[...] = jnp.zeros_like(gsec_ref)

    def ff_step(at, carry):
        lo = pl.multiple_of(at * ff_chunk, ff_chunk)
        up = weight_ref[:, pl.ds(width + lo, ff_chunk)]
        down = down_ref[pl.ds(lo, ff_chunk), :width]
        up_bias = rows_of(down_ref[pl.ds(lo, ff_chunk), width:], (0,))[0:1]
        pre_act = dot_nn(second_low, up) + up_bias
        sigma = 1.0 / (1.0 + jnp.exp(-pre_act))
        active = (pre_act * sigma).astype(BF16)
        branch_ref[...] += dot_nn(active, down)
        grad_active = dot_nt(dy, down).astype(BF16).astype(F32)
        grad_pre = grad_active * (sigma * (1.0 + pre_act * (1.0 - sigma)))
        grad_low = grad_pre.astype(BF16)
        gsec_ref[...] += dot_nt(grad_low, up)
        acc_down[:, pl.ds(lo, ff_chunk)] += dot_nn(dy_t, active)
        acc_up[:, pl.ds(lo, ff_chunk)] += dot_nn(second_t, grad_low)
        acc_upb[0:1, pl.ds(lo, ff_chunk)] += jnp.sum(grad_low.astype(F32), 0, keepdims=True)
        return carry

    lax.fori_loop(0, ff // ff_chunk, ff_step, 0)
    out_ref[...] = branch_ref[...].astype(BF16)
    gsec = gsec_ref[...]
    acc_vec[0:1] += jnp.sum(gsec * normed, 0, keepdims=True)
    acc_vec[1:2] += jnp.sum(gsec, 0, keepdims=True)
    acc_vec[2:3] += jnp.sum(dy_wide, 0, keepdims=True)
    grad_mid = dy_wide + norm_back(gsec, gain, normed, inv_dev)
    grad_mid_ref[...] = grad_mid
    grad_att = grad_mid.astype(BF16)
    acc_out[...] += dot_nn(routed.T.astype(BF16), grad_att)
    grad_routed = dot_nt(grad_att, weight_ref[:, :width]).astype(BF16)
    zero = jnp.zeros_like(grad_routed)
    picked_one = dot_nn(jnp.where(owner == first, grad_routed, zero), fold)
    picked_two = dot_nn(jnp.where(owner == second, grad_routed, zero), fold)
    grad_mixed_ref[0] = (gate_one * picked_one).astype(BF16)
    grad_mixed_ref[1] = (gate_two * picked_two).astype(BF16)
    grad_one = jnp.sum(picked_one * mixed_one, -1, keepdims=True)
    grad_two = jnp.sum(picked_two * mixed_two, -1, keepdims=True)
    common = gate_one * grad_one + gate_two * grad_two
    lane = lanes_of(rows, LANES)
    grad_logit_ref[...] = jnp.where(
        lane == first,
        gate_one * (grad_one - common),
        jnp.where(lane == second, gate_two * (grad_two - common), 0.0),
    )

    @pl.when(step == last)
    def _():
        d_weight_ref[:, :width] = acc_out[...].astype(BF16)
        d_weight_ref[:, width : width + ff] = acc_up[...].astype(BF16)
        d_weight_ref[:, width + ff :] = acc_vec[...].T.astype(BF16)
        for lo in range(0, ff, 512):
            d_down_ref[lo : lo + 512, :width] = acc_down[:, lo : lo + 512].T.astype(BF16)
            d_down_ref[lo : lo + 512, width:] = acc_upb[:, lo : lo + 512].T.astype(BF16)


def attend_back_kernel(
    reach, chunk, head, low_ref, q_ref, grad_ref, mixed_ref, lse_ref, start_ref, *rest
):
    pieces = rest[:reach]
    grad_q_ref = rest[reach]
    outs = rest[reach + 1 : 2 * reach + 1]
    kv_buf, kt_buf, acc_kv, acc_q = rest[2 * reach + 1 :]
    seq, tile = pl.program_id(0), pl.program_id(1)
    local = pieces[0].shape[1]
    tokens = q_ref.shape[1]
    per_piece = local // chunk

    @pl.when(tile == 0)
    def _():
        acc_kv[...] = jnp.zeros_like(acc_kv)
        for at in range(reach):
            for part in range(per_piece):
                block = pieces[at][0, part * chunk : (part + 1) * chunk, :]
                kv_buf[at * per_piece + part] = block
                kt_buf[at * per_piece + part] = block.astype(F32).T.astype(BF16)

    queries = jnp.concatenate([q_ref[0], q_ref[1]], 0)
    grads = jnp.concatenate([grad_ref[0], grad_ref[1]], 0)
    mixed = jnp.concatenate([mixed_ref[0], mixed_ref[1]], 0)
    inner = jnp.sum((grads.astype(F32) * mixed).T, 0, keepdims=True)
    start = start_ref[0]
    start = jnp.concatenate([start, start], 1)
    lse = lse_ref[0]
    query_at = (reach - 1) * local + tile * tokens
    acc_q[...] = jnp.zeros_like(acc_q)

    def step(at, carry):
        keyval = kv_buf[at]
        scores = masked(dot_nt(keyval, queries), start, at * chunk, query_at)
        probs = jnp.exp(scores - lse)
        grad_probs = dot_nt(keyval, grads)
        grad_scores = (probs * (grad_probs - inner)).astype(BF16)
        acc_kv[at] += dot_nn(grad_scores, queries) + dot_nn(probs.astype(BF16), grads)
        acc_q[...] += dot_nn(kt_buf[at], grad_scores)
        return carry

    low = low_ref[seq * pl.num_programs(1) + tile]
    high = (query_at + tokens - 1) // chunk + 1
    lax.fori_loop(low, high, step, 0)
    row = lax.broadcasted_iota(jnp.int32, acc_q.shape, 0)
    grad_q = (jnp.where(row < head, acc_q[...], 0.0) * (head**-0.5)).T.astype(BF16)
    grad_q_ref[0] = grad_q[:tokens]
    grad_q_ref[1] = grad_q[tokens:]

    @pl.when(tile == pl.num_programs(1) - 1)
    def _():
        for at in range(reach):
            for part in range(per_piece):
                block = acc_kv[at * per_piece + part]
                outs[at][0, part * chunk : (part + 1) * chunk, :] = block.astype(outs[at].dtype)


def last_kernel(
    experts,
    head,
    count,
    x_ref,
    hidden_ref,
    routes_ref,
    grad_q_ref,
    grad_logit_ref,
    grad_mid_ref,
    weight_ref,
    *rest,
):
    pieces = rest[:count]
    grad_in_ref, d_weight_ref, acc_ref, acc_vec = rest[count:]
    step, last = pl.program_id(0), pl.num_programs(0) - 1
    rows, width = x_ref.shape
    inner = experts * head

    @pl.when(step == 0)
    def _():
        acc_ref[...] = jnp.zeros_like(acc_ref)
        acc_vec[...] = jnp.zeros_like(acc_vec)

    gain = rows_of(weight_ref[:, inner + LANES :], (experts,))[0:1]
    normed, inv_dev = normalize(x_ref[...].astype(F32))
    first, second = routes_ref[:, 0:1], routes_ref[:, 1:2]
    owner = lax.div(lanes_of(rows, inner), head)
    unfold = unfold_matrix(inner, head, 0)
    grad_queries = jnp.where(
        owner == first,
        dot_nn(grad_q_ref[0], unfold),
        jnp.where(owner == second, dot_nn(grad_q_ref[1], unfold), 0.0),
    ).astype(BF16)
    summed = pieces[0][...]
    for piece in pieces[1:]:
        summed = summed + piece[...].astype(F32)
    grad_keyvals = summed.astype(BF16)
    grad_logits = grad_logit_ref[...]
    logit_high = grad_logits.astype(BF16)
    logit_low = (grad_logits - logit_high.astype(F32)).astype(BF16)
    router = weight_ref[:, inner + LANES :]
    grad_hidden = (
        dot_nt(grad_queries, weight_ref[:, :inner])
        + dot_nt(grad_keyvals, weight_ref[:, inner : inner + LANES])
        + dot_nt(logit_high, router)
        + dot_nt(logit_low, router)
    )
    grad_in_ref[...] = grad_mid_ref[...] + norm_back(grad_hidden, gain, normed, inv_dev)
    hidden_t = hidden_ref[...].astype(F32).T.astype(BF16)
    acc_ref[:, :inner] += dot_nn(hidden_t, grad_queries)
    acc_ref[:, inner : inner + LANES] += dot_nn(hidden_t, grad_keyvals)
    acc_ref[:, inner + LANES :] += dot_nn(hidden_t, logit_high) + dot_nn(hidden_t, logit_low)
    acc_vec[experts : experts + 1] += jnp.sum(grad_hidden * normed, 0, keepdims=True)
    acc_vec[experts + 1 : experts + 2] += jnp.sum(grad_hidden, 0, keepdims=True)

    @pl.when(step == last)
    def _():
        d_weight_ref[:, : inner + LANES] = acc_ref[:, : inner + LANES].astype(BF16)
        d_weight_ref[:, inner + LANES :] = (acc_ref[:, inner + LANES :] + acc_vec[...].T).astype(
            BF16
        )


def whole_spec(shape):
    zeros = (0,) * len(shape)
    return pl.BlockSpec(shape, lambda *_: zeros, pipeline_mode=pl.Buffered(1))


def row_spec(rows, columns):
    return pl.BlockSpec((rows, columns), lambda i, *_: (i, 0))


def pair_spec(rows):
    return pl.BlockSpec((2, rows, LANES), lambda i, *_: (0, i, 0))


def swapped(value, axis, mask):
    count = lax.axis_size(axis)
    return lax.ppermute(value, axis, [(at, at ^ mask) for at in range(count)])


def passed_along(value, axis, steps):
    count = lax.axis_size(axis)
    leading, last = (max(0, -steps), min(count, count - steps))
    return lax.ppermute(value, axis, [(source, source + steps) for source in range(leading, last)])


def gathered(shard):
    dp, seq = lax.axis_size("dp"), lax.axis_size("seq")
    along = [shard] + [swapped(shard, "dp", 2 * at) for at in range(1, dp // 2)]
    held = jnp.stack(along)
    across = [held] + [swapped(held, "seq", at) for at in range(1, seq)]
    held = jnp.stack(across)
    held = jnp.stack([held, swapped(held, "dp", 1)])
    dp_me, seq_me = lax.axis_index("dp"), lax.axis_index("seq")
    held = jnp.moveaxis(held, 2, 0)
    z_me, core_me = dp_me // 2, dp_me % 2
    for dim, me in ((0, z_me), (1, core_me), (2, seq_me)):
        size = held.shape[dim]
        order = jnp.arange(size, dtype=jnp.int32) ^ me
        held = jnp.take(held, order, axis=dim)
    return held.reshape((dp * seq * shard.shape[0],) + shard.shape[1:])


def halved(value, dim, bit, axis, mask):
    keep = lax.dynamic_index_in_dim(value, bit, dim, keepdims=False)
    send = lax.dynamic_index_in_dim(value, 1 - bit, dim, keepdims=False)
    return keep + swapped(send, axis, mask)


def scattered(value):
    dp, seq = lax.axis_size("dp"), lax.axis_size("seq")
    rows = value.shape[0] // (dp * seq)
    dp_bits, seq_bits = dp.bit_length() - 1, seq.bit_length() - 1
    bits = [("dp", 1 << at) for at in reversed(range(dp_bits))]
    bits += [("seq", 1 << at) for at in reversed(range(seq_bits))]
    held = value.reshape([2] * len(bits) + [rows, value.shape[1]])
    order = [("dp", 1)]
    order += [("seq", 1 << at) for at in range(seq_bits)]
    order += [("dp", 1 << at) for at in range(1, dp_bits)]
    for axis, mask in order:
        dim = bits.index((axis, mask))
        bit = (lax.axis_index(axis) // mask) % 2
        held = halved(held, dim, bit, axis, mask)
        bits.pop(dim)
    return held


def on_device(
    block_in,
    routes,
    segments,
    cotangent,
    ln1_gain,
    ln1_bias,
    query_weight,
    kv_weight,
    router_weight,
    out_weight,
    ln2_gain,
    ln2_bias,
    up_weight,
    up_bias,
    down_weight,
    down_bias,
):
    micro_count, seq_count, local_len, width = block_in.shape
    full_len = segments.shape[2]
    experts = router_weight.shape[1]
    head = kv_weight.shape[1] // 2
    inner = experts * head
    ff = up_weight.shape[1]
    shards = lax.axis_size("seq")
    batch = micro_count * seq_count
    rows_all = batch * local_len
    tile = 512
    longest = full_len * 3 // 4
    reach = min(shards, (longest - 2) // local_len + 2)
    own_shard = lax.axis_index("seq")
    start_pos = own_shard * local_len

    def column(vector):
        return vector[:, None]

    def padded(value, columns):
        return jnp.pad(value, ((0, 0), (0, columns - value.shape[1])))

    group_a = gathered(
        jnp.concatenate(
            [
                query_weight,
                kv_weight,
                padded(
                    jnp.concatenate([router_weight, column(ln1_gain), column(ln1_bias)], 1), LANES
                ),
            ],
            1,
        )
    )
    group_b = gathered(
        jnp.concatenate(
            [
                out_weight,
                up_weight,
                padded(
                    jnp.concatenate([column(ln2_gain), column(ln2_bias), column(down_bias)], 1),
                    LANES,
                ),
            ],
            1,
        )
    )
    group_c = gathered(jnp.concatenate([down_weight, padded(column(up_bias), LANES)], 1))

    tokens = block_in.reshape(rows_all, width)
    grad_out = cotangent.reshape(rows_all, width)
    route_rows = routes.reshape(rows_all, 2)

    seg_rows = segments.reshape(batch, full_len)
    seg_local = lax.dynamic_slice_in_dim(seg_rows, start_pos, local_len, 1)
    doc_start = jnp.sum(
        (seg_rows[:, None, :] < seg_local[:, :, None]).astype(jnp.int32), -1, dtype=jnp.int32
    )
    doc_start = jnp.maximum(doc_start - (own_shard - (reach - 1)) * local_len, 0)
    query_tile = min(local_len, 256)
    chunk = min(local_len, 256)
    tiles = local_len // query_tile
    low_chunks = (doc_start.reshape(batch * tiles, query_tile)[:, 0] // chunk).astype(jnp.int32)
    starts = doc_start.reshape(batch, 1, local_len)

    steps = rows_all // tile
    a_cols, b_cols, c_cols = inner + 2 * LANES, width + ff + LANES, width + LANES
    hidden, keyvals, queries, gates = pl.pallas_call(
        functools.partial(pre_kernel, experts, head),
        grid=(steps,),
        in_specs=[row_spec(tile, width), row_spec(tile, 2), whole_spec((width, a_cols))],
        out_specs=[
            row_spec(tile, width),
            row_spec(tile, LANES),
            pair_spec(tile),
            row_spec(tile, LANES),
        ],
        out_shape=[
            jax.ShapeDtypeStruct((rows_all, width), BF16),
            jax.ShapeDtypeStruct((rows_all, LANES), BF16),
            jax.ShapeDtypeStruct((2, rows_all, LANES), BF16),
            jax.ShapeDtypeStruct((rows_all, LANES), F32),
        ],
        compiler_params=call_params(),
        cost_estimate=cost(2 * rows_all * width * (a_cols + 512), rows_all * width * 8),
        name="pre",
    )(tokens, route_rows, group_a)

    own_pieces = keyvals.reshape(batch, local_len, LANES)
    pieces = [own_pieces] + [passed_along(own_pieces, "seq", back) for back in range(1, reach)]
    pieces = pieces[::-1]

    buffer_chunks = reach * local_len // chunk
    piece_spec = pl.BlockSpec((1, local_len, LANES), lambda b, t, *_: (b, 0, 0))
    q_spec = pl.BlockSpec((2, query_tile, LANES), lambda b, t, *_: (0, b * tiles + t, 0))
    start_spec = pl.BlockSpec((1, 1, query_tile), lambda b, t, *_: (b, 0, t))
    lse_spec = pl.BlockSpec((1, 1, 2 * query_tile), lambda b, t, *_: (b * tiles + t, 0, 0))
    lse_shape = jax.ShapeDtypeStruct((batch * tiles, 1, 2 * query_tile), F32)
    pairs = 2 * rows_all * full_len
    mixed, lse = pl.pallas_call(
        functools.partial(attend_kernel, reach, chunk, head),
        grid_spec=pltpu.PrefetchScalarGridSpec(
            num_scalar_prefetch=1,
            grid=(batch, tiles),
            in_specs=[q_spec, start_spec] + [piece_spec] * reach,
            out_specs=[q_spec, lse_spec],
            scratch_shapes=[
                pltpu.VMEM((buffer_chunks, chunk, LANES), BF16),
                pltpu.VMEM((buffer_chunks, LANES, chunk), BF16),
                pltpu.VMEM((1, 2 * query_tile), F32),
                pltpu.VMEM((1, 2 * query_tile), F32),
                pltpu.VMEM((LANES, 2 * query_tile), F32),
            ],
        ),
        out_shape=[jax.ShapeDtypeStruct((2, rows_all, LANES), F32), lse_shape],
        compiler_params=call_params(),
        cost_estimate=cost(4 * pairs * LANES, rows_all * LANES * 16, pairs),
        name="attend",
    )(low_chunks, queries, starts, *pieces)

    block_out, grad_mid, grad_mixed, grad_logits, d_b, d_c = pl.pallas_call(
        functools.partial(mid_kernel, experts, head, 512),
        grid=(steps,),
        in_specs=[
            row_spec(tile, width),
            row_spec(tile, width),
            row_spec(tile, 2),
            row_spec(tile, LANES),
            pair_spec(tile),
            whole_spec((width, b_cols)),
            whole_spec((ff, c_cols)),
        ],
        out_specs=[
            row_spec(tile, width),
            row_spec(tile, width),
            pair_spec(tile),
            row_spec(tile, LANES),
            whole_spec((width, b_cols)),
            whole_spec((ff, c_cols)),
        ],
        out_shape=[
            jax.ShapeDtypeStruct((rows_all, width), BF16),
            jax.ShapeDtypeStruct((rows_all, width), F32),
            jax.ShapeDtypeStruct((2, rows_all, LANES), BF16),
            jax.ShapeDtypeStruct((rows_all, LANES), F32),
            jax.ShapeDtypeStruct((width, b_cols), BF16),
            jax.ShapeDtypeStruct((ff, c_cols), BF16),
        ],
        scratch_shapes=[
            pltpu.VMEM((inner, width), F32),
            pltpu.VMEM((width, ff), F32),
            pltpu.VMEM((width, ff), F32),
            pltpu.VMEM((LANES, width), F32),
            pltpu.VMEM((LANES, ff), F32),
            pltpu.VMEM((tile, width), F32),
            pltpu.VMEM((tile, width), F32),
        ],
        compiler_params=call_params(),
        cost_estimate=cost(6 * rows_all * width * (2 * ff + width), rows_all * width * 16),
        name="mid",
    )(tokens, grad_out, route_rows, gates, mixed, group_b, group_c)
    own_b = scattered(d_b)
    own_c = scattered(d_c)

    grad_spec = pl.BlockSpec((1, local_len, LANES), lambda b, t, *_: (b, 0, 0))
    back = pl.pallas_call(
        functools.partial(attend_back_kernel, reach, chunk, head),
        grid_spec=pltpu.PrefetchScalarGridSpec(
            num_scalar_prefetch=1,
            grid=(batch, tiles),
            in_specs=[q_spec, q_spec, q_spec, lse_spec, start_spec] + [piece_spec] * reach,
            out_specs=[q_spec] + [grad_spec] * reach,
            scratch_shapes=[
                pltpu.VMEM((buffer_chunks, chunk, LANES), BF16),
                pltpu.VMEM((buffer_chunks, LANES, chunk), BF16),
                pltpu.VMEM((buffer_chunks, chunk, LANES), F32),
                pltpu.VMEM((LANES, 2 * query_tile), F32),
            ],
        ),
        out_shape=[jax.ShapeDtypeStruct((2, rows_all, LANES), BF16)]
        + [
            jax.ShapeDtypeStruct((batch, local_len, LANES), BF16 if at < reach - 1 else F32)
            for at in range(reach)
        ],
        compiler_params=call_params(),
        cost_estimate=cost(10 * pairs * LANES, rows_all * LANES * 32, pairs),
        name="attend_back",
    )(low_chunks, queries, grad_mixed, mixed, lse, starts, *pieces)
    grad_queries, grad_pieces = back[0], back[1:]
    returned = [grad_pieces[reach - 1].reshape(rows_all, LANES)]
    for steps_back in range(1, reach):
        piece = passed_along(grad_pieces[reach - 1 - steps_back], "seq", -steps_back)
        returned.append(piece.reshape(rows_all, LANES))

    grad_in, d_a = pl.pallas_call(
        functools.partial(last_kernel, experts, head, reach),
        grid=(steps,),
        in_specs=[
            row_spec(tile, width),
            row_spec(tile, width),
            row_spec(tile, 2),
            pair_spec(tile),
            row_spec(tile, LANES),
            row_spec(tile, width),
            whole_spec((width, a_cols)),
        ]
        + [row_spec(tile, LANES)] * reach,
        out_specs=[row_spec(tile, width), whole_spec((width, a_cols))],
        out_shape=[
            jax.ShapeDtypeStruct((rows_all, width), F32),
            jax.ShapeDtypeStruct((width, a_cols), BF16),
        ],
        scratch_shapes=[pltpu.VMEM((width, a_cols), F32), pltpu.VMEM((LANES, width), F32)],
        compiler_params=call_params(),
        cost_estimate=cost(4 * rows_all * width * a_cols, rows_all * width * 12),
        name="last",
    )(tokens, hidden, route_rows, grad_queries, grad_logits, grad_mid, group_a, *returned)
    own_a = scattered(d_a)

    own_a, own_b, own_c = (value.astype(F32) for value in (own_a, own_b, own_c))
    extra = own_a[:, inner + LANES :]
    return (
        block_out.reshape(block_in.shape),
        grad_in.reshape(block_in.shape),
        extra[:, experts],
        extra[:, experts + 1],
        own_a[:, :inner],
        own_a[:, inner : inner + 2 * head],
        extra[:, :experts],
        own_b[:, :width],
        own_b[:, width + ff],
        own_b[:, width + ff + 1],
        own_b[:, width : width + ff],
        own_c[:, width],
        own_c[:, :width],
        own_b[:, width + ff + 2],
    )


def solution(mesh):
    rows = P(("dp", "seq"), None)
    vector = P(("dp", "seq"))
    data = P(None, "dp", "seq", None)
    weights = (
        vector,
        vector,
        rows,
        rows,
        rows,
        rows,
        vector,
        vector,
        rows,
        vector,
        rows,
        vector,
    )
    return jax.shard_map(
        on_device,
        mesh=mesh,
        in_specs=(data, data, P(None, "dp", None), data) + weights,
        out_specs=(data, data) + weights,
        check_vma=False,
    )
```

```python
import functools

import jax
import jax.numpy as jnp
from jax import lax
from jax.experimental import pallas as pl
from jax.experimental.pallas import tpu as pltpu
from jax.sharding import PartitionSpec as P

EPS = 1e-05
LANES = 128
VMEM_LIMIT = 56 * 1024 * 1024
BF16 = jnp.bfloat16
F32 = jnp.float32


def call_params():
    return pltpu.CompilerParams(vmem_limit_bytes=VMEM_LIMIT)


def cost(flops, bytes_accessed, transcendentals=0):
    return pl.CostEstimate(
        flops=int(flops), bytes_accessed=int(bytes_accessed), transcendentals=int(transcendentals)
    )


def dot_nn(left, right):
    return lax.dot_general(left, right, (((1,), (0,)), ((), ())), preferred_element_type=F32)


def dot_nt(left, right):
    return lax.dot_general(left, right, (((1,), (1,)), ((), ())), preferred_element_type=F32)


def lanes_of(rows, width):
    return lax.broadcasted_iota(jnp.int32, (rows, width), 1)


def fold_matrix(width, head, shift):
    source = lax.broadcasted_iota(jnp.int32, (width, LANES), 0)
    target = lax.broadcasted_iota(jnp.int32, (width, LANES), 1)
    return jnp.where(target == shift + lax.rem(source, head), 1.0, 0.0).astype(BF16)


def unfold_matrix(width, head, shift):
    source = lax.broadcasted_iota(jnp.int32, (LANES, width), 1)
    target = lax.broadcasted_iota(jnp.int32, (LANES, width), 0)
    return jnp.where(target == shift + lax.rem(source, head), 1.0, 0.0).astype(BF16)


def rows_of(columns, picked):
    row = lax.broadcasted_iota(jnp.int32, (8, LANES), 0)
    lane = lax.broadcasted_iota(jnp.int32, (8, LANES), 1)
    chosen = jnp.zeros((8, LANES), F32)
    for at, column in enumerate(picked):
        chosen = jnp.where((row == at) & (lane == column), 1.0, chosen)
    return dot_nt(chosen.astype(BF16), columns)


def normalize(values):
    centered = values - jnp.mean(values, -1, keepdims=True)
    inv_dev = lax.rsqrt(jnp.mean(centered * centered, -1, keepdims=True) + EPS)
    return centered * inv_dev, inv_dev


def norm_back(grad, gain, normed, inv_dev):
    scaled = grad * gain
    return inv_dev * (
        scaled
        - jnp.mean(scaled, -1, keepdims=True)
        - normed * jnp.mean(scaled * normed, -1, keepdims=True)
    )


def pre_kernel(experts, head, x_ref, routes_ref, weight_ref, hidden_ref, kv_ref, q_ref, gate_ref):
    width = x_ref.shape[1]
    inner = experts * head
    extras = weight_ref[:, inner + LANES :]
    vectors = rows_of(extras, (experts, experts + 1))
    normed, _ = normalize(x_ref[...].astype(F32))
    hidden = (normed * vectors[0:1] + vectors[1:2]).astype(BF16)
    hidden_ref[...] = hidden
    big = dot_nn(hidden, weight_ref[...])
    rows = big.shape[0]
    kv_ref[...] = big[:, inner : inner + LANES].astype(BF16)
    logits = big[:, inner + LANES :]
    lane = lanes_of(rows, LANES)
    first, second = routes_ref[:, 0:1], routes_ref[:, 1:2]
    logit_one = jnp.sum(jnp.where(lane == first, logits, 0.0), -1, keepdims=True)
    logit_two = jnp.sum(jnp.where(lane == second, logits, 0.0), -1, keepdims=True)
    peak = jnp.maximum(logit_one, logit_two)
    exp_one = jnp.exp(logit_one - peak)
    exp_two = jnp.exp(logit_two - peak)
    total = exp_one + exp_two
    gate_ref[...] = jnp.where(lane == 0, exp_one / total, jnp.where(lane == 1, exp_two / total, 0.0))
    queries = (big[:, :inner] * (head**-0.5)).astype(BF16)
    owner = lax.div(lanes_of(rows, inner), head)
    fold = fold_matrix(inner, head, 0)
    zero = jnp.zeros_like(queries)
    q_ref[0] = dot_nn(jnp.where(owner == first, queries, zero), fold).astype(BF16)
    q_ref[1] = dot_nn(jnp.where(owner == second, queries, zero), fold).astype(BF16)


def masked(scores, start, key_at, query_at):
    keys = key_at + lax.broadcasted_iota(jnp.int32, scores.shape, 0)
    queries = query_at + lax.rem(
        lax.broadcasted_iota(jnp.int32, (1, scores.shape[1]), 1), scores.shape[1] // 2
    )
    return jnp.where((keys >= start) & (keys <= queries), scores, -1e30)


def over_chunks(step, bounds_ref, seq, chunk, query_at, tokens):
    low = bounds_ref[2 * seq] // chunk
    high = (query_at + tokens - 1) // chunk + 1
    clear_high = (query_at + 1) // chunk
    clear_low = jnp.minimum((bounds_ref[2 * seq + 1] + chunk - 1) // chunk, clear_high)

    def with_mask(at, carry):
        step(at, True)
        return carry

    def without_mask(at, carry):
        step(at, False)
        return carry

    lax.fori_loop(low, clear_low, with_mask, 0)
    lax.fori_loop(clear_low, clear_high, without_mask, 0)
    lax.fori_loop(clear_high, high, with_mask, 0)


def attend_kernel(reach, chunk, head, bounds_ref, q_ref, start_ref, *rest):
    pieces = rest[:reach]
    mixed_ref, lse_ref, kv_buf, vt_buf, peak_ref, total_ref, acc_ref = rest[reach:]
    seq = pl.program_id(0)
    local = pieces[0].shape[1]
    per_piece = local // chunk
    for at in range(reach):
        for part in range(per_piece):
            block = pieces[at][0, part * chunk : (part + 1) * chunk, :]
            kv_buf[at * per_piece + part] = block
            row = lax.broadcasted_iota(jnp.int32, (LANES, chunk), 0)
            vt_buf[at * per_piece + part] = jnp.where(
                row >= head, block.astype(F32).T, 0.0
            ).astype(BF16)

    queries = jnp.concatenate([q_ref[0], q_ref[1]], 0)
    start = start_ref[0]
    start = jnp.concatenate([start, start], 1)
    query_at = (reach - 1) * local
    peak_ref[...] = jnp.full_like(peak_ref, -1e30)
    total_ref[...] = jnp.zeros_like(total_ref)
    acc_ref[...] = jnp.zeros_like(acc_ref)

    def step(at, needs_mask):
        scores = dot_nt(kv_buf[at], queries)
        if needs_mask:
            scores = masked(scores, start, at * chunk, query_at)
        peak = jnp.maximum(peak_ref[...], jnp.max(scores, 0, keepdims=True))
        fade = jnp.exp(peak_ref[...] - peak)
        expo = jnp.exp(scores - peak)
        total_ref[...] = total_ref[...] * fade + jnp.sum(expo, 0, keepdims=True)
        acc_ref[...] = acc_ref[...] * fade + dot_nn(vt_buf[at], expo.astype(BF16))
        peak_ref[...] = peak

    over_chunks(step, bounds_ref, seq, chunk, query_at, local)
    mixed = (acc_ref[...] / total_ref[...]).T
    mixed_ref[0] = mixed[:local]
    mixed_ref[1] = mixed[local:]
    lse_ref[0] = peak_ref[...] + jnp.log(total_ref[...])


def mid_kernel(
    experts,
    head,
    x_ref,
    dy_ref,
    routes_ref,
    gate_ref,
    mixed_ref,
    vector_ref,
    down_ref,
    up_ref,
    wo_ref,
    out_ref,
    grad_mid_ref,
    grad_mixed_ref,
    grad_logit_ref,
    grads_ref,
    acc_out,
    acc_up,
    acc_down,
    acc_vec,
    acc_upb,
    branch_ref,
    gsec_ref,
):
    step, last = pl.program_id(0), pl.num_programs(0) - 1
    rows, width = x_ref.shape
    inner = experts * head
    owners, own_rows = wo_ref.shape[:2]
    ff_rows = down_ref.shape[1]
    ff = owners * ff_rows
    blocks = ff // width

    @pl.when(step == 0)
    def _():
        acc_out[...] = jnp.zeros_like(acc_out)
        acc_up[...] = jnp.zeros_like(acc_up)
        acc_down[...] = jnp.zeros_like(acc_down)
        acc_vec[...] = jnp.zeros_like(acc_vec)
        acc_upb[...] = jnp.zeros_like(acc_upb)

    gain, shift = vector_ref[1:2, :width], vector_ref[2:3, :width]
    down_bias = vector_ref[3:4, :width]
    first, second = routes_ref[:, 0:1], routes_ref[:, 1:2]
    gate_one, gate_two = gate_ref[:, 0:1], gate_ref[:, 1:2]
    owner = lax.div(lanes_of(rows, inner), head)
    unfold = unfold_matrix(inner, head, head)
    fold = fold_matrix(inner, head, head)
    wo = wo_ref[...].reshape(inner, width)
    mixed_one, mixed_two = mixed_ref[0], mixed_ref[1]
    routed_one = dot_nn((gate_one * mixed_one).astype(BF16), unfold)
    routed_two = dot_nn((gate_two * mixed_two).astype(BF16), unfold)
    routed = jnp.where(
        owner == first, routed_one, jnp.where(owner == second, routed_two, 0.0)
    )
    middle = x_ref[...].astype(F32) + dot_nn(routed.astype(BF16), wo)
    normed, inv_dev = normalize(middle)
    second_wide = normed * gain + shift
    second_low = second_wide.astype(BF16)
    second_t = second_wide.T.astype(BF16)
    dy = dy_ref[...]
    dy_wide = dy.astype(F32)
    dy_t = dy_wide.T.astype(BF16)
    branch_ref[...] = middle + down_bias
    gsec_ref[...] = jnp.zeros_like(gsec_ref)
    per_block = width // ff_rows if owners > 1 else 1

    def down_block(at):
        if owners > 1:
            return down_ref[at * per_block : (at + 1) * per_block].reshape(width, width)
        return down_ref[0, at * width : (at + 1) * width, :]

    for at in range(blocks):
        lo = at * width
        up = up_ref[:, at * own_rows : (at + 1) * own_rows, :].reshape(width, width)
        down = down_block(at)
        pre_act = dot_nn(second_low, up) + vector_ref[0:1, lo : lo + width]
        sigma = 1.0 / (1.0 + jnp.exp(-pre_act))
        active = (pre_act * sigma).astype(BF16)
        branch_ref[...] += dot_nn(active, down)
        grad_active = dot_nt(dy, down).astype(BF16).astype(F32)
        grad_pre = grad_active * (sigma * (1.0 + pre_act * (1.0 - sigma)))
        grad_low = grad_pre.astype(BF16)
        gsec_ref[...] += dot_nt(grad_low, up)
        acc_down[:, lo : lo + width] += dot_nn(dy_t, active)
        acc_up[:, lo : lo + width] += dot_nn(second_t, grad_low)
        acc_upb[8:9, lo : lo + width] += jnp.sum(grad_low.astype(F32), 0, keepdims=True)

    out_ref[...] = branch_ref[...].astype(BF16)
    gsec = gsec_ref[...]
    acc_vec[0:1] += jnp.sum(gsec * normed, 0, keepdims=True)
    acc_vec[1:2] += jnp.sum(gsec, 0, keepdims=True)
    acc_vec[2:3] += jnp.sum(dy_wide, 0, keepdims=True)
    grad_mid = dy_wide + norm_back(gsec, gain, normed, inv_dev)
    grad_mid_ref[...] = grad_mid
    grad_att = grad_mid.astype(BF16)
    acc_out[...] += dot_nn(routed.T.astype(BF16), grad_att)
    grad_routed = dot_nt(grad_att, wo).astype(BF16)
    zero = jnp.zeros_like(grad_routed)
    picked_one = dot_nn(jnp.where(owner == first, grad_routed, zero), fold)
    picked_two = dot_nn(jnp.where(owner == second, grad_routed, zero), fold)
    grad_mixed_ref[0] = (gate_one * picked_one).astype(BF16)
    grad_mixed_ref[1] = (gate_two * picked_two).astype(BF16)
    grad_one = jnp.sum(picked_one * mixed_one, -1, keepdims=True)
    grad_two = jnp.sum(picked_two * mixed_two, -1, keepdims=True)
    common = gate_one * grad_one + gate_two * grad_two
    lane = lanes_of(rows, LANES)
    grad_logit_ref[...] = jnp.where(
        lane == first,
        gate_one * (grad_one - common),
        jnp.where(lane == second, gate_two * (grad_two - common), 0.0),
    )

    @pl.when(step == last)
    def _():
        up_at, out_at = ff_rows, ff_rows + blocks * own_rows
        for at in range(blocks):
            lo = at * width
            turned = acc_down[:, lo : lo + width].T.astype(BF16)
            if owners > 1:
                grads_ref[at * per_block : (at + 1) * per_block, :ff_rows, :] = turned.reshape(
                    per_block, ff_rows, width
                )
            else:
                grads_ref[0, lo : lo + width, :] = turned
            grads_ref[:, up_at + at * own_rows : up_at + (at + 1) * own_rows, :] = (
                acc_up[:, lo : lo + width].astype(BF16).reshape(owners, own_rows, width)
            )
        grads_ref[:, out_at : out_at + own_rows, :] = (
            acc_out[...].astype(BF16).reshape(owners, own_rows, width)
        )
        extra = acc_upb[...].T.astype(BF16).reshape(owners, blocks, own_rows, LANES)
        for at in range(blocks):
            part = extra[:, at]
            if at == 0:
                part = part + acc_vec[...].T.astype(BF16).reshape(owners, own_rows, LANES)
            grads_ref[:, out_at + own_rows :, at * LANES : (at + 1) * LANES] = part


def attend_back_kernel(
    reach, chunk, head, micro, chained, bounds_ref, q_ref, grad_ref, mixed_ref, lse_ref, start_ref, *rest
):
    pieces = rest[:reach]
    rest = rest[reach + chained :]
    grad_q_ref = rest[0]
    outs = rest[1 : reach + 1]
    kv_buf, kt_buf, acc_kv, acc_q = rest[reach + 1 :]
    seq = micro * pl.num_programs(0) + pl.program_id(0)
    local = pieces[0].shape[1]
    per_piece = local // chunk
    acc_kv[...] = jnp.zeros_like(acc_kv)
    for at in range(reach):
        for part in range(per_piece):
            block = pieces[at][0, part * chunk : (part + 1) * chunk, :]
            kv_buf[at * per_piece + part] = block
            kt_buf[at * per_piece + part] = block.astype(F32).T.astype(BF16)

    queries = jnp.concatenate([q_ref[0], q_ref[1]], 0)
    grads = jnp.concatenate([grad_ref[0], grad_ref[1]], 0)
    mixed = jnp.concatenate([mixed_ref[0], mixed_ref[1]], 0)
    inner = jnp.sum((grads.astype(F32) * mixed).T, 0, keepdims=True)
    start = start_ref[0]
    start = jnp.concatenate([start, start], 1)
    lse = lse_ref[0]
    query_at = (reach - 1) * local
    acc_q[...] = jnp.zeros_like(acc_q)

    def step(at, needs_mask):
        keyval = kv_buf[at]
        scores = dot_nt(keyval, queries)
        if needs_mask:
            scores = masked(scores, start, at * chunk, query_at)
        probs = jnp.exp(scores - lse)
        grad_probs = dot_nt(keyval, grads)
        grad_scores = (probs * (grad_probs - inner)).astype(BF16)
        acc_kv[at] += dot_nn(grad_scores, queries) + dot_nn(probs.astype(BF16), grads)
        acc_q[...] += dot_nn(kt_buf[at], grad_scores)

    over_chunks(step, bounds_ref, seq, chunk, query_at, local)
    row = lax.broadcasted_iota(jnp.int32, acc_q.shape, 0)
    grad_q = (jnp.where(row < head, acc_q[...], 0.0) * (head**-0.5)).T.astype(BF16)
    grad_q_ref[0] = grad_q[:local]
    grad_q_ref[1] = grad_q[local:]
    for at in range(reach):
        for part in range(per_piece):
            block = acc_kv[at * per_piece + part]
            outs[at][0, part * chunk : (part + 1) * chunk, :] = block.astype(outs[at].dtype)


def query_grad_kernel(
    experts,
    head,
    hidden_ref,
    routes_ref,
    grad_q_ref,
    grad_logit_ref,
    weight_ref,
    partial_ref,
    d_query_ref,
    d_router_ref,
    acc_query,
    acc_router,
):
    step, last = pl.program_id(0), pl.num_programs(0) - 1
    rows, width = hidden_ref.shape
    inner = experts * head

    @pl.when(step == 0)
    def _():
        acc_query[...] = jnp.zeros_like(acc_query)
        acc_router[...] = jnp.zeros_like(acc_router)

    first, second = routes_ref[:, 0:1], routes_ref[:, 1:2]
    owner = lax.div(lanes_of(rows, inner), head)
    unfold = unfold_matrix(inner, head, 0)
    grad_queries = jnp.where(
        owner == first,
        dot_nn(grad_q_ref[0], unfold),
        jnp.where(owner == second, dot_nn(grad_q_ref[1], unfold), 0.0),
    ).astype(BF16)
    grad_logits = grad_logit_ref[...]
    logit_high = grad_logits.astype(BF16)
    logit_low = (grad_logits - logit_high.astype(F32)).astype(BF16)
    router = weight_ref[:, inner + LANES :]
    partial_ref[...] = (
        dot_nt(grad_queries, weight_ref[:, :inner])
        + dot_nt(logit_high, router)
        + dot_nt(logit_low, router)
    )
    hidden_t = hidden_ref[...].astype(F32).T.astype(BF16)
    acc_query[...] += dot_nn(hidden_t, grad_queries)
    acc_router[...] += dot_nn(hidden_t, logit_high) + dot_nn(hidden_t, logit_low)

    @pl.when(step == last)
    def _():
        d_query_ref[...] = acc_query[...].astype(BF16)
        d_router_ref[...] = acc_router[...]


def last_kernel(
    experts,
    head,
    reach,
    micro_count,
    x_ref,
    hidden_ref,
    partial_ref,
    grad_mid_ref,
    router_ref,
    weight_ref,
    *rest,
):
    pieces = rest[: reach * micro_count]
    grad_in_ref, d_small_ref, acc_kv, acc_vec, summed_ref = rest[reach * micro_count :]
    step, last = pl.program_id(0), pl.num_programs(0) - 1
    rows, width = x_ref.shape
    inner = experts * head

    @pl.when(step == 0)
    def _():
        acc_kv[...] = jnp.zeros_like(acc_kv)
        acc_vec[...] = jnp.zeros_like(acc_vec)

    for micro in range(micro_count):

        @pl.when(step == micro)
        def _():
            mine = pieces[micro * reach : (micro + 1) * reach]
            summed = mine[0][...]
            for piece in mine[1:]:
                summed = summed + piece[...].astype(F32)
            summed_ref[...] = summed.astype(BF16)

    gain = rows_of(weight_ref[:, inner + LANES :], (experts,))[0:1]
    normed, inv_dev = normalize(x_ref[...].astype(F32))
    grad_keyvals = summed_ref[...]
    grad_hidden = partial_ref[...] + dot_nt(grad_keyvals, weight_ref[:, inner : inner + LANES])
    grad_in_ref[...] = grad_mid_ref[...] + norm_back(grad_hidden, gain, normed, inv_dev)
    hidden_t = hidden_ref[...].astype(F32).T.astype(BF16)
    acc_kv[...] += dot_nn(hidden_t, grad_keyvals)
    acc_vec[experts : experts + 1] += jnp.sum(grad_hidden * normed, 0, keepdims=True)
    acc_vec[experts + 1 : experts + 2] += jnp.sum(grad_hidden, 0, keepdims=True)

    @pl.when(step == last)
    def _():
        d_small_ref[:, :LANES] = acc_kv[...].astype(BF16)
        d_small_ref[:, LANES:] = (router_ref[...] + acc_vec[...].T).astype(BF16)


def whole_spec(shape):
    zeros = (0,) * len(shape)
    return pl.BlockSpec(shape, lambda *_: zeros, pipeline_mode=pl.Buffered(1))


def row_spec(rows, columns):
    return pl.BlockSpec((rows, columns), lambda i, *_: (i, 0))


def pair_spec(rows):
    return pl.BlockSpec((2, rows, LANES), lambda i, *_: (0, i, 0))


def swapped(value, axis, mask):
    count = lax.axis_size(axis)
    return lax.ppermute(value, axis, [(at, at ^ mask) for at in range(count)])


def passed_along(value, axis, steps):
    count = lax.axis_size(axis)
    leading, last = (max(0, -steps), min(count, count - steps))
    return lax.ppermute(value, axis, [(source, source + steps) for source in range(leading, last)])


def gathered(shard):
    dp, seq = lax.axis_size("dp"), lax.axis_size("seq")
    along = [shard] + [swapped(shard, "dp", 2 * at) for at in range(1, dp // 2)]
    held = jnp.stack(along)
    across = [held] + [swapped(held, "seq", at) for at in range(1, seq)]
    held = jnp.stack(across)
    held = jnp.stack([held, swapped(held, "dp", 1)])
    dp_me, seq_me = lax.axis_index("dp"), lax.axis_index("seq")
    held = jnp.moveaxis(held, 2, 0)
    for dim, me in ((0, dp_me // 2), (1, dp_me % 2), (2, seq_me)):
        order = jnp.arange(held.shape[dim], dtype=jnp.int32) ^ me
        held = jnp.take(held, order, axis=dim)
    return held.reshape((dp * seq * shard.shape[0],) + shard.shape[1:])


def at_index(value, index, dim):
    return lax.dynamic_index_in_dim(value, index, dim, keepdims=False)


def core_halved(value):
    core = lax.axis_index("dp") % 2
    return at_index(value, core, 1) + swapped(at_index(value, 1 - core, 1), "dp", 1)


def seq_halved(value, dim, mask):
    bit = (lax.axis_index("seq") // mask) % 2
    return at_index(value, bit, dim) + swapped(at_index(value, 1 - bit, dim), "seq", mask)


def summed_direct(value, dim, axis, scale):
    me = lax.axis_index(axis) // scale
    total = at_index(value, me, dim).astype(F32)
    for at in range(1, value.shape[dim]):
        total = total + swapped(at_index(value, me ^ at, dim), axis, at * scale).astype(F32)
    return total


def small_scattered(value):
    dp, seq = lax.axis_size("dp"), lax.axis_size("seq")
    held = value.reshape(dp // 2, 2, seq, value.shape[0] // (dp * seq), value.shape[1])
    held = core_halved(held)
    held = summed_direct(held, 1, "seq", 1).astype(BF16)
    return summed_direct(held, 0, "dp", 2)


def together(*values):
    return lax.optimization_barrier(values)


def on_device(
    block_in,
    routes,
    segments,
    cotangent,
    ln1_gain,
    ln1_bias,
    query_weight,
    kv_weight,
    router_weight,
    out_weight,
    ln2_gain,
    ln2_bias,
    up_weight,
    up_bias,
    down_weight,
    down_bias,
):
    micro_count, seq_count, local_len, width = block_in.shape
    full_len = segments.shape[2]
    experts = router_weight.shape[1]
    head = kv_weight.shape[1] // 2
    inner = experts * head
    ff = up_weight.shape[1]
    dp, shards = lax.axis_size("dp"), lax.axis_size("seq")
    devices = dp * shards
    own_rows, ff_rows, blocks = width // devices, ff // devices, ff // width
    aligned = own_rows % 16 == 0
    batch = micro_count * seq_count
    rows_all = batch * local_len
    tile = seq_count * local_len
    longest = full_len * 3 // 4
    reach = min(shards, (longest - 2) // local_len + 2)
    own_shard = lax.axis_index("seq")
    start_pos = own_shard * local_len

    def column(vector):
        return vector[:, None]

    def padded(value, columns):
        return jnp.pad(value, ((0, 0), (0, columns - value.shape[1])))

    extra = [router_weight, column(ln1_gain), column(ln1_bias), column(ln2_gain)]
    extra += [column(ln2_bias), column(down_bias), up_bias.reshape(own_rows, blocks)]
    packed_a = jnp.concatenate(
        [query_weight, kv_weight, padded(jnp.concatenate(extra, 1), LANES)], 1
    )
    group_a = gathered(packed_a)
    packed_b = jnp.concatenate(
        [down_weight]
        + [up_weight[:, at * width : (at + 1) * width] for at in range(blocks)]
        + [out_weight],
        0,
    )
    group_b = lax.all_gather(packed_b, ("dp", "seq"), axis=0, tiled=False)
    up_at, out_at = ff_rows, ff_rows + blocks * own_rows
    if aligned:
        nb, rb, fb = devices, own_rows, ff_rows
        weights = [group_b, group_b, group_b]
        weight_specs = [
            pl.BlockSpec((nb, ff_rows, width), lambda *_: (0, 0, 0), pipeline_mode=pl.Buffered(1)),
            pl.BlockSpec(
                (nb, blocks * own_rows, width), lambda *_: (0, 1, 0), pipeline_mode=pl.Buffered(1)
            ),
            pl.BlockSpec(
                (nb, own_rows, width),
                lambda *_: (0, out_at // own_rows, 0),
                pipeline_mode=pl.Buffered(1),
            ),
        ]
    else:
        nb, rb, fb = 1, width, ff
        up_all = group_b[:, up_at:out_at].reshape(devices, blocks, own_rows, width)
        weights = [
            group_b[:, :ff_rows].reshape(1, ff, width),
            jnp.moveaxis(up_all, 0, 1).reshape(1, ff, width),
            group_b[:, out_at:].reshape(1, width, width),
        ]
        weight_specs = [whole_spec(value.shape) for value in weights]

    tokens = block_in.reshape(rows_all, width)
    grad_out = cotangent.reshape(rows_all, width)
    route_rows = routes.reshape(rows_all, 2)

    seg_rows = segments.reshape(batch, full_len)
    seg_local = lax.dynamic_slice_in_dim(seg_rows, start_pos, local_len, 1)
    doc_start = jnp.sum(
        (seg_rows[:, None, :] < seg_local[:, :, None]).astype(jnp.int32), -1, dtype=jnp.int32
    )
    doc_start = jnp.maximum(doc_start - (own_shard - (reach - 1)) * local_len, 0)
    chunk = min(local_len, 256)
    bounds = jnp.stack([doc_start[:, 0], doc_start[:, -1]], 1).reshape(2 * batch)
    starts = doc_start.reshape(batch, 1, local_len)

    steps = micro_count
    a_cols = inner + 2 * LANES
    hidden, keyvals, queries, gates = pl.pallas_call(
        functools.partial(pre_kernel, experts, head),
        grid=(steps,),
        in_specs=[row_spec(tile, width), row_spec(tile, 2), whole_spec((width, a_cols))],
        out_specs=[
            row_spec(tile, width),
            row_spec(tile, LANES),
            pair_spec(tile),
            row_spec(tile, LANES),
        ],
        out_shape=[
            jax.ShapeDtypeStruct((rows_all, width), BF16),
            jax.ShapeDtypeStruct((rows_all, LANES), BF16),
            jax.ShapeDtypeStruct((2, rows_all, LANES), BF16),
            jax.ShapeDtypeStruct((rows_all, LANES), F32),
        ],
        compiler_params=call_params(),
        cost_estimate=cost(2 * rows_all * width * (a_cols + 512), rows_all * width * 8),
        name="pre",
    )(tokens, route_rows, group_a)

    own_pieces = keyvals.reshape(batch, local_len, LANES)
    pieces = [own_pieces] + [passed_along(own_pieces, "seq", back) for back in range(1, reach)]
    pieces = pieces[::-1]

    columns = group_a[:, inner + LANES :].astype(F32)
    small = jnp.pad(columns[:, experts + 2 : experts + 5].T, ((0, 4), (0, ff - width)))
    up_row = columns[:, experts + 5 : experts + 5 + blocks].reshape(1, ff)
    vectors = jnp.concatenate([up_row, small], 0)

    buffer_chunks = reach * local_len // chunk
    piece_spec = pl.BlockSpec((1, local_len, LANES), lambda b, *_: (b, 0, 0))
    q_spec = pl.BlockSpec((2, local_len, LANES), lambda b, *_: (0, b, 0))
    start_spec = pl.BlockSpec((1, 1, local_len), lambda b, *_: (b, 0, 0))
    lse_spec = pl.BlockSpec((1, 1, 2 * local_len), lambda b, *_: (b, 0, 0))
    pairs = rows_all * full_len
    mixed, lse = pl.pallas_call(
        functools.partial(attend_kernel, reach, chunk, head),
        grid_spec=pltpu.PrefetchScalarGridSpec(
            num_scalar_prefetch=1,
            grid=(batch,),
            in_specs=[q_spec, start_spec] + [piece_spec] * reach,
            out_specs=[q_spec, lse_spec],
            scratch_shapes=[
                pltpu.VMEM((buffer_chunks, chunk, LANES), BF16),
                pltpu.VMEM((buffer_chunks, LANES, chunk), BF16),
                pltpu.VMEM((1, 2 * local_len), F32),
                pltpu.VMEM((1, 2 * local_len), F32),
                pltpu.VMEM((LANES, 2 * local_len), F32),
            ],
        ),
        out_shape=[
            jax.ShapeDtypeStruct((2, rows_all, LANES), F32),
            jax.ShapeDtypeStruct((batch, 1, 2 * local_len), F32),
        ],
        compiler_params=call_params(),
        cost_estimate=cost(4 * pairs * LANES, rows_all * LANES * 16, pairs),
        name="attend",
    )(bounds, queries, starts, *pieces)

    grad_rows = ff_rows + (blocks + 2) * own_rows if aligned else ff + (blocks + 2) * width
    block_out, grad_mid, grad_mixed, grad_logits, grads_b = pl.pallas_call(
        functools.partial(mid_kernel, experts, head),
        grid=(steps,),
        in_specs=[
            row_spec(tile, width),
            row_spec(tile, width),
            row_spec(tile, 2),
            row_spec(tile, LANES),
            pair_spec(tile),
            whole_spec((8, ff)),
        ]
        + weight_specs,
        out_specs=[
            row_spec(tile, width),
            row_spec(tile, width),
            pair_spec(tile),
            row_spec(tile, LANES),
            whole_spec((nb, grad_rows, width)),
        ],
        out_shape=[
            jax.ShapeDtypeStruct((rows_all, width), BF16),
            jax.ShapeDtypeStruct((rows_all, width), F32),
            jax.ShapeDtypeStruct((2, rows_all, LANES), BF16),
            jax.ShapeDtypeStruct((rows_all, LANES), F32),
            jax.ShapeDtypeStruct((nb, grad_rows, width), BF16),
        ],
        scratch_shapes=[
            pltpu.VMEM((inner, width), F32),
            pltpu.VMEM((width, ff), F32),
            pltpu.VMEM((width, ff), F32),
            pltpu.VMEM((LANES, width), F32),
            pltpu.VMEM((LANES, ff), F32),
            pltpu.VMEM((tile, width), F32),
            pltpu.VMEM((tile, width), F32),
        ],
        compiler_params=call_params(),
        cost_estimate=cost(6 * rows_all * width * (2 * ff + width), rows_all * width * 16),
        name="mid",
    )(tokens, grad_out, route_rows, gates, mixed, vectors, *weights)

    if not aligned:
        parts = grads_b[0]
        down_part = parts[:ff].reshape(devices, ff_rows, width)
        up_part = parts[ff : 2 * ff].reshape(blocks, devices, own_rows, width)
        up_part = jnp.moveaxis(up_part, 0, 1).reshape(devices, blocks * own_rows, width)
        out_part = parts[2 * ff : 2 * ff + width].reshape(devices, own_rows, width)
        tail = parts[2 * ff + width :]
        rows_up = tail.reshape(width, blocks, LANES)[:, :, 8].T.reshape(devices, own_rows, blocks)
        rows_vec = tail[:, :8].reshape(devices, own_rows, 8)
        rows_up = jnp.moveaxis(rows_up.reshape(devices, blocks, own_rows), 1, 2)
        tail = jnp.zeros((devices, own_rows, blocks, LANES), BF16)
        tail = tail.at[:, :, :, 8].set(rows_up).at[:, :, 0, :8].set(rows_vec)
        tail = tail.reshape(devices, own_rows, width)
        grads_b = jnp.concatenate([down_part, up_part, out_part, tail], 1)

    held = grads_b.reshape((dp // 2, 2, shards) + grads_b.shape[1:])
    held = core_halved(held)
    bits = shards.bit_length() - 1
    order = [1 << at for at in range(bits)]
    orders = (order, order[bits // 2 :] + order[: bits // 2])
    half_rows = held.shape[2] // 2
    halves = [
        held.reshape((dp // 2,) + (2,) * bits + held.shape[2:])[..., :half_rows, :],
        held.reshape((dp // 2,) + (2,) * bits + held.shape[2:])[..., half_rows:, :],
    ]
    remaining = [list(reversed(order)), list(reversed(order))]

    def halving(stage):
        for part in range(2):
            mask = orders[part][stage]
            dim = 1 + remaining[part].index(mask)
            remaining[part].remove(mask)
            halves[part] = seq_halved(halves[part], dim, mask)

    back_params = dict(compiler_params=call_params(), name="attend_back")
    grad_queries = None
    returned = []
    stage = 0
    for micro in range(micro_count):

        def at_micro(block, dims):
            base = micro * seq_count
            if dims == "b":
                return pl.BlockSpec(block, lambda b, *_: (base + b, 0, 0))
            return pl.BlockSpec(block, lambda b, *_: (0, base + b, 0))

        q_at = at_micro((2, local_len, LANES), "q")
        in_specs = [
            q_at,
            q_at,
            q_at,
            at_micro((1, 1, 2 * local_len), "b"),
            at_micro((1, 1, local_len), "b"),
        ]
        in_specs += [at_micro((1, local_len, LANES), "b")] * reach
        operands = [queries, grad_mixed, mixed, lse, starts, *pieces]
        bounds_now = bounds
        aliases = {}
        if micro:
            in_specs.append(pl.BlockSpec(memory_space=pl.ANY))
            if stage == 0:
                bounds_now, halves[0], halves[1] = together(bounds, halves[0], halves[1])
            if stage < bits:
                halving(stage)
                stage += 1
            operands.append(grad_queries)
            aliases = {len(operands): 0}
        back = pl.pallas_call(
            functools.partial(attend_back_kernel, reach, chunk, head, micro, int(micro > 0)),
            grid_spec=pltpu.PrefetchScalarGridSpec(
                num_scalar_prefetch=1,
                grid=(seq_count,),
                in_specs=in_specs,
                out_specs=[q_at] + [piece_spec] * reach,
                scratch_shapes=[
                    pltpu.VMEM((buffer_chunks, chunk, LANES), BF16),
                    pltpu.VMEM((buffer_chunks, LANES, chunk), BF16),
                    pltpu.VMEM((buffer_chunks, chunk, LANES), F32),
                    pltpu.VMEM((LANES, 2 * local_len), F32),
                ],
            ),
            out_shape=[jax.ShapeDtypeStruct((2, rows_all, LANES), BF16)]
            + [
                jax.ShapeDtypeStruct(
                    (seq_count, local_len, LANES), BF16 if at < reach - 1 else F32
                )
                for at in range(reach)
            ],
            input_output_aliases=aliases,
            cost_estimate=cost(
                10 * pairs * LANES // micro_count, tile * LANES * 32, pairs // micro_count
            ),
            **back_params,
        )(bounds_now, *operands)
        grad_queries, grad_pieces = back[0], back[1:]
        returned.append(grad_pieces[reach - 1].reshape(tile, LANES))
        for steps_back in range(1, reach):
            piece = passed_along(grad_pieces[reach - 1 - steps_back], "seq", -steps_back)
            returned.append(piece.reshape(tile, LANES))

    partial_hidden, d_query, d_router = pl.pallas_call(
        functools.partial(query_grad_kernel, experts, head),
        grid=(steps,),
        in_specs=[
            row_spec(tile, width),
            row_spec(tile, 2),
            pair_spec(tile),
            row_spec(tile, LANES),
            whole_spec((width, a_cols)),
        ],
        out_specs=[
            row_spec(tile, width),
            whole_spec((width, inner)),
            whole_spec((width, LANES)),
        ],
        out_shape=[
            jax.ShapeDtypeStruct((rows_all, width), F32),
            jax.ShapeDtypeStruct((width, inner), BF16),
            jax.ShapeDtypeStruct((width, LANES), F32),
        ],
        scratch_shapes=[pltpu.VMEM((width, inner), F32), pltpu.VMEM((width, LANES), F32)],
        compiler_params=call_params(),
        cost_estimate=cost(4 * rows_all * width * a_cols, rows_all * width * 12),
        name="query_grad",
    )(hidden, route_rows, grad_queries, grad_logits, group_a)

    while stage < bits:
        halving(stage)
        stage += 1
    own_b = jnp.concatenate(halves, 1)
    own_b = summed_direct(own_b, 0, "dp", 2)
    own_query = small_scattered(d_query)

    grad_in, d_small = pl.pallas_call(
        functools.partial(last_kernel, experts, head, reach, micro_count),
        grid=(steps,),
        in_specs=[
            row_spec(tile, width),
            row_spec(tile, width),
            row_spec(tile, width),
            row_spec(tile, width),
            whole_spec((width, LANES)),
            whole_spec((width, a_cols)),
        ]
        + [whole_spec((tile, LANES))] * (reach * micro_count),
        out_specs=[row_spec(tile, width), whole_spec((width, 2 * LANES))],
        out_shape=[
            jax.ShapeDtypeStruct((rows_all, width), F32),
            jax.ShapeDtypeStruct((width, 2 * LANES), BF16),
        ],
        scratch_shapes=[
            pltpu.VMEM((width, LANES), F32),
            pltpu.VMEM((LANES, width), F32),
            pltpu.VMEM((tile, LANES), BF16),
        ],
        compiler_params=call_params(),
        cost_estimate=cost(4 * rows_all * width * LANES, rows_all * width * 16),
        name="last",
    )(tokens, hidden, partial_hidden, grad_mid, d_router, group_a, *returned)
    own_small = small_scattered(d_small)

    tail = own_b[out_at + own_rows :]
    grad_up = jnp.concatenate(
        [own_b[up_at + at * own_rows : up_at + (at + 1) * own_rows] for at in range(blocks)], 1
    )
    grad_up_bias = jnp.concatenate([tail[:, at * LANES + 8] for at in range(blocks)])
    return (
        block_out.reshape(block_in.shape),
        grad_in.reshape(block_in.shape),
        own_small[:, LANES + experts],
        own_small[:, LANES + experts + 1],
        own_query,
        own_small[:, : 2 * head],
        own_small[:, LANES : LANES + experts],
        own_b[out_at : out_at + own_rows],
        tail[:, 0],
        tail[:, 1],
        grad_up,
        grad_up_bias,
        own_b[:ff_rows],
        tail[:, 2],
    )


def solution(mesh):
    rows = P(("dp", "seq"), None)
    vector = P(("dp", "seq"))
    data = P(None, "dp", "seq", None)
    weights = (
        vector,
        vector,
        rows,
        rows,
        rows,
        rows,
        vector,
        vector,
        rows,
        vector,
        rows,
        vector,
    )
    return jax.shard_map(
        on_device,
        mesh=mesh,
        in_specs=(data, data, P(None, "dp", None), data) + weights,
        out_specs=(data, data) + weights,
        check_vma=False,
    )
```

```python
import functools

import jax
import jax.numpy as jnp
from jax import lax
from jax.experimental import pallas as pl
from jax.experimental.pallas import tpu as pltpu
from jax.sharding import PartitionSpec as P

EPS = 1e-05
LANES = 128
MIB = 1024 * 1024
BF16 = jnp.bfloat16
F32 = jnp.float32


def call_params():
    return pltpu.CompilerParams(vmem_limit_bytes=56 * MIB)


def cost(flops, bytes_accessed, transcendentals=0):
    return pl.CostEstimate(
        flops=int(flops), bytes_accessed=int(bytes_accessed), transcendentals=int(transcendentals)
    )


def dot_nn(left, right):
    return lax.dot_general(left, right, (((1,), (0,)), ((), ())), preferred_element_type=F32)


def dot_nt(left, right):
    return lax.dot_general(left, right, (((1,), (1,)), ((), ())), preferred_element_type=F32)


def lanes_of(rows, width):
    return lax.broadcasted_iota(jnp.int32, (rows, width), 1)


def fold_matrix(width, head, shift):
    source = lax.broadcasted_iota(jnp.int32, (width, LANES), 0)
    target = lax.broadcasted_iota(jnp.int32, (width, LANES), 1)
    return jnp.where(target == shift + lax.rem(source, head), 1.0, 0.0).astype(BF16)


def unfold_matrix(width, head, shift):
    source = lax.broadcasted_iota(jnp.int32, (LANES, width), 1)
    target = lax.broadcasted_iota(jnp.int32, (LANES, width), 0)
    return jnp.where(target == shift + lax.rem(source, head), 1.0, 0.0).astype(BF16)


def rows_of(columns, picked):
    row = lax.broadcasted_iota(jnp.int32, (8, LANES), 0)
    lane = lax.broadcasted_iota(jnp.int32, (8, LANES), 1)
    chosen = jnp.zeros((8, LANES), F32)
    for at, column in enumerate(picked):
        chosen = jnp.where((row == at) & (lane == column), 1.0, chosen)
    return dot_nt(chosen.astype(BF16), columns)


def normalize(values):
    centered = values - jnp.mean(values, -1, keepdims=True)
    inv_dev = lax.rsqrt(jnp.mean(centered * centered, -1, keepdims=True) + EPS)
    return centered * inv_dev, inv_dev


def norm_back(grad, gain, normed, inv_dev):
    scaled = grad * gain
    return inv_dev * (
        scaled
        - jnp.mean(scaled, -1, keepdims=True)
        - normed * jnp.mean(scaled * normed, -1, keepdims=True)
    )


def pack_kernel(query_ref, kv_ref, router_ref, down_ref, up_ref, out_ref, *rest):
    *vector_refs, up_bias_ref, first_ref, second_ref = rest
    own_rows, width = query_ref.shape
    first_ref[:, :width] = query_ref[...]
    first_ref[:, width : width + LANES] = kv_ref[...]
    rows = [router_ref[...].astype(F32)]
    rows += [ref[...].astype(F32).reshape(1, own_rows) for ref in vector_refs]
    bias = up_bias_ref[...].astype(F32).reshape(1, up_bias_ref.shape[0])
    rows += [
        bias[:, at * own_rows : (at + 1) * own_rows] for at in range(bias.shape[1] // own_rows)
    ]
    count = router_ref.shape[0] + len(rows) - 1
    rows.append(jnp.zeros((32 - count, own_rows), F32))
    rows = jnp.concatenate(rows, 0).astype(BF16)
    row = lax.broadcasted_iota(jnp.int32, (32, LANES), 0)
    lane = lax.broadcasted_iota(jnp.int32, (32, LANES), 1)
    chosen = jnp.where(lane == row, 1.0, 0.0).astype(BF16)
    turned = lax.dot_general(rows, chosen, (((0,), (0,)), ((), ())), preferred_element_type=F32)
    first_ref[:, width + LANES :] = turned.astype(BF16)
    ff_rows = down_ref.shape[0]
    second_ref[:ff_rows] = down_ref[...]
    blocks = up_ref.shape[1] // width
    for at in range(blocks):
        low = ff_rows + at * own_rows
        second_ref[low : low + own_rows] = up_ref[:, at * width : (at + 1) * width]
    second_ref[ff_rows + blocks * own_rows :] = out_ref[...]


def in_order(place_ref, parts, put):
    z_me, core_me, seq_me = place_ref[0], place_ref[1], place_ref[2]
    for core, part in enumerate(parts):
        for seq in range(part.shape[0]):
            for z in range(part.shape[1]):
                dp_at = (z_me ^ z) * 2 + (core_me ^ core)
                put(dp_at * part.shape[0] + (seq_me ^ seq), part[seq, z])


def keyval_kernel(experts, head, place_ref, x_ref, mine_ref, mate_ref, *rest):
    hidden_ref, kv_ref, weight_ref, blocks_ref = rest

    @pl.when(pl.program_id(0) == 0)
    def _():
        def put(device, block):
            blocks_ref[device] = block

        in_order(place_ref, (mine_ref, mate_ref), put)
        weight_ref[...] = blocks_ref[...].reshape(weight_ref.shape)

    inner = experts * head
    vectors = rows_of(weight_ref[:, inner + LANES :], (experts, experts + 1))
    normed, _ = normalize(x_ref[...].astype(F32))
    hidden = (normed * vectors[0:1] + vectors[1:2]).astype(BF16)
    hidden_ref[...] = hidden
    kv_ref[...] = dot_nn(hidden, weight_ref[:, inner : inner + LANES]).astype(BF16)


def query_kernel(experts, head, hidden_ref, routes_ref, weight_ref, q_ref, gate_ref):
    inner = experts * head
    hidden = hidden_ref[...]
    rows = hidden.shape[0]
    logits = dot_nn(hidden, weight_ref[:, inner + LANES :])
    lane = lanes_of(rows, LANES)
    first, second = routes_ref[:, 0:1], routes_ref[:, 1:2]
    logit_one = jnp.sum(jnp.where(lane == first, logits, 0.0), -1, keepdims=True)
    logit_two = jnp.sum(jnp.where(lane == second, logits, 0.0), -1, keepdims=True)
    peak = jnp.maximum(logit_one, logit_two)
    exp_one = jnp.exp(logit_one - peak)
    exp_two = jnp.exp(logit_two - peak)
    total = exp_one + exp_two
    gates = jnp.where(lane == 0, exp_one / total, jnp.where(lane == 1, exp_two / total, 0.0))
    gates = jnp.where(lane == 2, first.astype(F32), gates)
    gate_ref[...] = jnp.where(lane == 3, second.astype(F32), gates)
    queries = (dot_nn(hidden, weight_ref[:, :inner]) * (head**-0.5)).astype(BF16)
    owner = lax.div(lanes_of(rows, inner), head)
    fold = fold_matrix(inner, head, 0)
    zero = jnp.zeros_like(queries)
    q_ref[0] = dot_nn(jnp.where(owner == first, queries, zero), fold).astype(BF16)
    q_ref[1] = dot_nn(jnp.where(owner == second, queries, zero), fold).astype(BF16)


def masked(scores, start, key_at, query_at=None):
    keys = key_at + lax.broadcasted_iota(jnp.int32, scores.shape, 0)
    seen = keys >= start
    if query_at is not None:
        lane = lax.broadcasted_iota(jnp.int32, (1, scores.shape[1]), 1)
        seen = seen & (keys <= query_at + lax.rem(lane, scores.shape[1] // 2))
    return jnp.where(seen, scores, -1e30)


def by_halves(ref):
    half = ref.shape[1] // 2
    return [
        jnp.concatenate([ref[0, at * half : (at + 1) * half], ref[1, at * half : (at + 1) * half]], 0)
        for at in range(2)
    ]


def from_halves(ref, groups):
    half = ref.shape[1] // 2
    for at, group in enumerate(groups):
        ref[0, at * half : (at + 1) * half] = group[:half]
        ref[1, at * half : (at + 1) * half] = group[half:]


def row_halves(row):
    half = row.shape[1] // 2
    return [
        jnp.concatenate([row[:, at * half : (at + 1) * half]] * 2, 1) for at in range(2)
    ]


def over_pieces(step, bounds_ref, seq, reach, local):
    low = jnp.minimum(bounds_ref[seq] // local, reach - 1)

    def body(at, carry):
        step(at)
        return carry

    lax.fori_loop(low, reach - 1, body, 0)


def attend_kernel(reach, head, bounds_ref, q_ref, start_ref, *rest):
    pieces = rest[:reach]
    mixed_ref, lse_ref, kv_buf, peak_ref, total_ref, acc_ref = rest[reach:]
    seq = pl.program_id(0)
    local = pieces[0].shape[1]
    half = local // 2
    for at in range(reach - 1):
        kv_buf[at] = pieces[at][0]
    queries = by_halves(q_ref)
    starts = row_halves(start_ref[0])
    peak_ref[...] = jnp.full_like(peak_ref, -1e30)
    total_ref[...] = jnp.zeros_like(total_ref)
    acc_ref[...] = jnp.zeros_like(acc_ref)

    def turned_values(keyval):
        return keyval.T[head:]

    def accumulate(group, scores, values):
        old = peak_ref[group : group + 1]
        peak = jnp.maximum(old, jnp.max(scores, 0, keepdims=True))
        fade = jnp.exp(old - peak)
        expo = jnp.exp(scores - peak)
        total_ref[group : group + 1] = total_ref[group : group + 1] * fade + jnp.sum(
            expo, 0, keepdims=True
        )
        acc_ref[group] = acc_ref[group] * fade + dot_nn(values, expo.astype(BF16))
        peak_ref[group : group + 1] = peak

    def step(at):
        keyval = kv_buf[at]
        values = turned_values(keyval)
        for group in range(2):
            scores = masked(dot_nt(keyval, queries[group]), starts[group], at * local)
            accumulate(group, scores, values)

    over_pieces(step, bounds_ref, seq, reach, local)
    own = pieces[reach - 1][0]
    own_at = (reach - 1) * local
    values = turned_values(own)
    for group in range(2):
        keys = half * (group + 1)
        scores = masked(
            dot_nt(own[:keys], queries[group]), starts[group], own_at, own_at + group * half
        )
        accumulate(group, scores, values[:, :keys])
    groups = []
    for group in range(2):
        mixed = acc_ref[group] / total_ref[group : group + 1]
        groups.append(jnp.concatenate([jnp.zeros_like(mixed), mixed], 0).T)
    from_halves(mixed_ref, groups)
    lse_ref[0] = peak_ref[...] + jnp.log(total_ref[...])


def mid_kernel(
    experts,
    head,
    x_ref,
    dy_ref,
    gate_ref,
    mixed_ref,
    vector_ref,
    core_ref,
    down_ref,
    up_ref,
    wo_ref,
    out_ref,
    grad_mid_ref,
    grad_mixed_ref,
    side_ref,
    *rest,
):
    *grads_refs, acc_out, acc_up, acc_down, acc_vec, acc_upb, branch_ref, gsec_ref = rest
    step, last = pl.program_id(0), pl.num_programs(0) - 1
    rows, width = x_ref.shape
    inner = experts * head
    owners, own_rows = wo_ref.shape[:2]
    ff_rows = down_ref.shape[1]
    ff = owners * ff_rows
    blocks = ff // width

    @pl.when(step == 0)
    def _():
        acc_out[...] = jnp.zeros_like(acc_out)
        acc_up[...] = jnp.zeros_like(acc_up)
        acc_down[...] = jnp.zeros_like(acc_down)
        acc_vec[...] = jnp.zeros_like(acc_vec)
        acc_upb[...] = jnp.zeros_like(acc_upb)

    gain, shift = vector_ref[1:2, :width], vector_ref[2:3, :width]
    down_bias = vector_ref[3:4, :width]
    gate_one, gate_two = gate_ref[:, 0:1], gate_ref[:, 1:2]
    first, second = gate_ref[:, 2:3].astype(jnp.int32), gate_ref[:, 3:4].astype(jnp.int32)
    owner = lax.div(lanes_of(rows, inner), head)
    unfold = unfold_matrix(inner, head, head)
    fold = fold_matrix(inner, head, head)
    wo = wo_ref[...].reshape(inner, width)
    mixed_one, mixed_two = mixed_ref[0], mixed_ref[1]
    routed_one = dot_nn((gate_one * mixed_one).astype(BF16), unfold)
    routed_two = dot_nn((gate_two * mixed_two).astype(BF16), unfold)
    routed = jnp.where(
        owner == first, routed_one, jnp.where(owner == second, routed_two, 0.0)
    )
    routed = routed.astype(BF16)
    middle = x_ref[...].astype(F32) + dot_nn(routed, wo)
    normed, inv_dev = normalize(middle)
    second_low = (normed * gain + shift).astype(BF16)
    second_t = second_low.T
    dy = dy_ref[...]
    dy_wide = dy.astype(F32)
    dy_t = dy.T
    branch_ref[...] = middle + down_bias
    gsec_ref[...] = jnp.zeros_like(gsec_ref)
    per_block = width // ff_rows if owners > 1 else 1

    def down_block(at):
        if owners > 1:
            return down_ref[at * per_block : (at + 1) * per_block].reshape(width, width)
        return down_ref[0, at * width : (at + 1) * width, :]

    def up_block(at):
        return up_ref[:, at * own_rows : (at + 1) * own_rows, :].reshape(width, width)

    def ahead(at):
        lo = at * width
        pre_act = dot_nn(second_low, up_block(at)) + vector_ref[0:1, lo : lo + width]
        return pre_act, dot_nt(dy, down_block(at)).astype(BF16)

    ready = ahead(0)
    for at in range(blocks):
        lo = at * width
        pre_act, grad_active = ready
        if at + 1 < blocks:
            ready = ahead(at + 1)
        sigma = jax.nn.sigmoid(pre_act)
        active = (pre_act * sigma).astype(BF16)
        slope = sigma * (1.0 + pre_act * (1.0 - sigma))
        grad_low = (grad_active.astype(F32) * slope).astype(BF16)
        branch_ref[...] += dot_nn(active, down_block(at))
        gsec_ref[...] += dot_nt(grad_low, up_block(at))
        acc_down[:, lo : lo + width] += dot_nn(dy_t, active)
        acc_up[:, lo : lo + width] += dot_nn(second_t, grad_low)
        acc_upb[8:9, lo : lo + width] += jnp.sum(grad_low.astype(F32), 0, keepdims=True)

    out_ref[...] = branch_ref[...].astype(BF16)
    gsec = gsec_ref[...]
    acc_vec[0:1] += jnp.sum(gsec * normed, 0, keepdims=True)
    acc_vec[1:2] += jnp.sum(gsec, 0, keepdims=True)
    acc_vec[2:3] += jnp.sum(dy_wide, 0, keepdims=True)
    grad_mid = dy_wide + norm_back(gsec, gain, normed, inv_dev)
    grad_mid_ref[...] = grad_mid
    grad_att = grad_mid.astype(BF16)
    acc_out[...] += dot_nn(routed.T, grad_att)
    grad_routed = dot_nt(grad_att, wo).astype(BF16)
    zero = jnp.zeros_like(grad_routed)
    picked_one = dot_nn(jnp.where(owner == first, grad_routed, zero), fold)
    picked_two = dot_nn(jnp.where(owner == second, grad_routed, zero), fold)
    grad_mixed_one = (gate_one * picked_one).astype(BF16)
    grad_mixed_two = (gate_two * picked_two).astype(BF16)
    grad_mixed_ref[0] = grad_mixed_one
    grad_mixed_ref[1] = grad_mixed_two
    inner_one = jnp.sum(grad_mixed_one.astype(F32) * mixed_one, -1, keepdims=True)
    inner_two = jnp.sum(grad_mixed_two.astype(F32) * mixed_two, -1, keepdims=True)
    grad_one = jnp.sum(picked_one * mixed_one, -1, keepdims=True)
    grad_two = jnp.sum(picked_two * mixed_two, -1, keepdims=True)
    common = gate_one * grad_one + gate_two * grad_two
    lane = lanes_of(rows, LANES)
    side = jnp.where(lane == first, gate_one * (grad_one - common), 0.0)
    side = jnp.where(lane == second, gate_two * (grad_two - common), side)
    side = jnp.where(lane == head, inner_one, side)
    side = jnp.where(lane == head + 1, inner_two, side)
    side = jnp.where(lane == head + 2, first.astype(F32), side)
    side_ref[...] = jnp.where(lane == head + 3, second.astype(F32), side)

    @pl.when(step == last)
    def _():
        up_at, out_at = ff_rows, ff_rows + blocks * own_rows

        def leave(value, columns, row, count, group):
            if owners == 1:
                grads_refs[0][0, row : row + value.shape[0], columns] = value
                return
            keep_ref, send_ref = grads_refs
            seqs = keep_ref.shape[1]
            parts = value.reshape(value.shape[0] // (2 * seqs * count), 2, seqs, count, -1)
            planes = parts.shape[0]
            other = core_ref[0] == 1
            low, high = parts[:, 0], parts[:, 1]
            where = (slice(group * planes, (group + 1) * planes), slice(None), slice(row, row + count), columns)
            keep_ref[where] = jnp.where(other, high, low)
            send_ref[where] = jnp.where(other, low, high)

        everything = slice(None)
        for at in range(blocks):
            lo = at * width
            turned = acc_down[:, lo : lo + width].T.astype(BF16)
            leave(turned, everything, lo if owners == 1 else 0, ff_rows, at)
            leave(
                acc_up[:, lo : lo + width].astype(BF16),
                everything,
                up_at + at * own_rows,
                own_rows,
                0,
            )
        leave(acc_out[...].astype(BF16), everything, out_at, own_rows, 0)
        vectors_turned = acc_vec[...].T
        extra = acc_upb[...].T
        if owners > 1:
            extra = extra.reshape(owners, blocks, own_rows, LANES)
        for at in range(blocks):
            if owners > 1:
                part = extra[:, at].reshape(width, LANES)
            else:
                part = extra[at * width : (at + 1) * width]
            if at == 0:
                part = part + vectors_turned
            columns = slice(at * LANES, (at + 1) * LANES)
            leave(part.astype(BF16), columns, out_at + own_rows, own_rows, 0)


def attend_back_kernel(
    reach, head, first_seq, chained, bounds_ref, q_ref, grad_ref, side_ref, lse_ref, start_ref, *rest
):
    pieces = rest[:reach]
    rest = rest[reach + chained :]
    grad_q_ref, leave_ref, kv_buf, acc_kv, acc_q = rest
    seq = first_seq + pl.program_id(0)
    local = pieces[0].shape[1]
    half = local // 2
    for at in range(reach - 1):
        kv_buf[at] = pieces[at][0]
    acc_kv[...] = jnp.zeros_like(acc_kv)
    acc_q[...] = jnp.zeros_like(acc_q)
    queries = by_halves(q_ref)
    grads = by_halves(grad_ref)
    side = side_ref[...].T
    inner_rows = [side[head + at : head + at + 1] for at in range(2)]
    starts = row_halves(start_ref[0])
    inners = [
        jnp.concatenate([row[:, at * half : (at + 1) * half] for row in inner_rows], 1)
        for at in range(2)
    ]
    log_sums = [lse_ref[0, at : at + 1] for at in range(2)]

    def one_group(group, keyval, keys_turned, mask):
        scores = mask(dot_nt(keyval, queries[group]))
        probs = jnp.exp(scores - log_sums[group])
        grad_probs = dot_nt(keyval, grads[group])
        grad_scores = (probs * (grad_probs - inners[group])).astype(BF16)
        acc_q[group] += dot_nn(keys_turned, grad_scores)
        return dot_nn(grad_scores, queries[group]) + dot_nn(probs.astype(BF16), grads[group])

    def turned_keys(keyval):
        return keyval.T[:head]

    def step(at):
        keyval = kv_buf[at]
        turned = turned_keys(keyval)
        added = []
        for group in range(2):

            def mask(scores):
                return masked(scores, starts[group], at * local)

            added.append(one_group(group, keyval, turned, mask))
        acc_kv[at] += added[0] + added[1]

    over_pieces(step, bounds_ref, seq, reach, local)
    own = pieces[reach - 1][0]
    own_at = (reach - 1) * local
    turned = turned_keys(own)
    for group in range(2):
        keys = half * (group + 1)
        added = one_group(
            group,
            own[:keys],
            turned[:, :keys],
            lambda scores: masked(scores, starts[group], own_at, own_at + group * half),
        )
        acc_kv[reach - 1, :keys] += added
    groups = []
    for group in range(2):
        grad_q = acc_q[group] * (head**-0.5)
        groups.append(jnp.concatenate([grad_q, jnp.zeros_like(grad_q)], 0).T.astype(BF16))
    from_halves(grad_q_ref, groups)
    shards = leave_ref.shape[0]
    me = bounds_ref[bounds_ref.shape[0] - 1]
    for at in range(shards):

        @pl.when((at > me) | (at <= me - reach))
        def _():
            leave_ref[at, 0] = jnp.zeros((local, LANES), BF16)

    for at in range(reach):
        target = me - (reach - 1) + at

        @pl.when(target >= 0)
        def _():
            leave_ref[target, 0] = acc_kv[at].astype(BF16)


def query_grad_kernel(
    experts,
    head,
    hidden_ref,
    grad_q_ref,
    grad_logit_ref,
    weight_ref,
    partial_ref,
    d_query_ref,
    d_router_ref,
    acc_query,
    acc_router,
):
    step, last = pl.program_id(0), pl.num_programs(0) - 1
    rows, width = hidden_ref.shape
    inner = experts * head

    @pl.when(step == 0)
    def _():
        acc_query[...] = jnp.zeros_like(acc_query)
        acc_router[...] = jnp.zeros_like(acc_router)

    side = grad_logit_ref[...]
    first = side[:, head + 2 : head + 3].astype(jnp.int32)
    second = side[:, head + 3 : head + 4].astype(jnp.int32)
    owner = lax.div(lanes_of(rows, inner), head)
    unfold = unfold_matrix(inner, head, 0)
    grad_queries = jnp.where(
        owner == first,
        dot_nn(grad_q_ref[0], unfold),
        jnp.where(owner == second, dot_nn(grad_q_ref[1], unfold), 0.0),
    ).astype(BF16)
    grad_logits = jnp.where(lanes_of(rows, LANES) < experts, side, 0.0)
    logit_high = grad_logits.astype(BF16)
    logit_low = (grad_logits - logit_high.astype(F32)).astype(BF16)
    router = weight_ref[:, inner + LANES :]
    partial_ref[...] = (
        dot_nt(grad_queries, weight_ref[:, :inner])
        + dot_nt(logit_high, router)
        + dot_nt(logit_low, router)
    )
    hidden_t = hidden_ref[...].T
    acc_query[...] += dot_nn(hidden_t, grad_queries)
    acc_router[...] += dot_nn(hidden_t, logit_high) + dot_nn(hidden_t, logit_low)

    @pl.when(step == last)
    def _():
        d_query_ref[...] = acc_query[...].astype(BF16)
        d_router_ref[...] = acc_router[...]


def last_kernel(
    experts,
    head,
    parts,
    core_ref,
    x_ref,
    hidden_ref,
    partial_ref,
    grad_mid_ref,
    query_ref,
    router_ref,
    weight_ref,
    *rest,
):
    pieces = rest[: len(parts)]
    grad_in_ref, *leaving, acc_kv, acc_vec, summed_ref = rest[len(parts) :]
    step, last = pl.program_id(0), pl.num_programs(0) - 1
    rows, width = x_ref.shape
    inner = experts * head

    @pl.when(step == 0)
    def _():
        acc_kv[...] = jnp.zeros_like(acc_kv)
        acc_vec[...] = jnp.zeros_like(acc_vec)

    for piece, (low, high) in zip(pieces, parts):

        @pl.when((step >= low) & (step < high))
        def _():
            per_step = piece.shape[1] // (high - low)
            base = (step - low) * per_step
            summed = piece[0, pl.ds(base, per_step)].astype(F32)
            for at in range(1, piece.shape[0]):
                summed = summed + piece[at, pl.ds(base, per_step)].astype(F32)
            summed_ref[...] = summed.astype(BF16).reshape(summed_ref.shape)

    gain = rows_of(weight_ref[:, inner + LANES :], (experts,))[0:1]
    normed, inv_dev = normalize(x_ref[...].astype(F32))
    grad_keyvals = summed_ref[...]
    grad_hidden = partial_ref[...] + dot_nt(grad_keyvals, weight_ref[:, inner : inner + LANES])
    grad_in_ref[...] = grad_mid_ref[...] + norm_back(grad_hidden, gain, normed, inv_dev)
    hidden_t = hidden_ref[...].T
    acc_kv[...] += dot_nn(hidden_t, grad_keyvals)
    acc_vec[experts : experts + 1] += jnp.sum(grad_hidden * normed, 0, keepdims=True)
    acc_vec[experts + 1 : experts + 2] += jnp.sum(grad_hidden, 0, keepdims=True)

    @pl.when(step == last)
    def _():
        extra = router_ref[...] + acc_vec[...].T
        for value, low in (
            (query_ref[...], 0),
            (acc_kv[...].astype(BF16), inner),
            (extra.astype(BF16), inner + LANES),
        ):
            columns = slice(low, low + value.shape[1])
            if len(leaving) == 1:
                leaving[0][:, columns] = value
                continue
            keep_ref, send_ref = leaving
            planes, seqs, own_rows = keep_ref.shape[:3]
            by_core = value.reshape(planes, 2, seqs, own_rows, value.shape[1])
            other = core_ref[0] == 1
            keep_ref[:, :, :, columns] = jnp.where(other, by_core[:, 1], by_core[:, 0])
            send_ref[:, :, :, columns] = jnp.where(other, by_core[:, 0], by_core[:, 1])


def finish_second_kernel(total_ref, down_ref, up_ref, out_ref, up_bias_ref, *vector_refs):
    ff_rows, width = down_ref.shape
    own_rows, ff = up_ref.shape
    blocks = ff // width
    down_ref[...] = total_ref[:ff_rows].astype(F32)
    for at in range(blocks):
        low = ff_rows + at * own_rows
        up_ref[:, at * width : (at + 1) * width] = total_ref[low : low + own_rows].astype(F32)
    low = ff_rows + blocks * own_rows
    out_ref[...] = total_ref[low : low + own_rows].astype(F32)
    turned = total_ref[low + own_rows :].astype(F32).T
    up_bias_ref[...] = jnp.concatenate([turned[at * LANES + 8] for at in range(blocks)], 0)
    for at, ref in enumerate(vector_refs):
        ref[...] = turned[at]


def finish_first_kernel(count, *refs):
    query_ref, kv_ref, router_ref, gain_ref, bias_ref = refs[count:]
    total = refs[0][...].astype(F32)
    for ref in refs[1:count]:
        total = total + ref[...].astype(F32)
    inner, pair, experts = query_ref.shape[1], kv_ref.shape[1], router_ref.shape[0]
    query_ref[...] = total[:, :inner]
    kv_ref[...] = total[:, inner : inner + pair]
    turned = total[:, inner + LANES :].T
    router_ref[...] = turned[:experts]
    gain_ref[...] = turned[experts]
    bias_ref[...] = turned[experts + 1]


def whole_spec(shape):
    zeros = (0,) * len(shape)
    return pl.BlockSpec(shape, lambda *_: zeros, pipeline_mode=pl.Buffered(1))


def row_spec(rows, columns):
    return pl.BlockSpec((rows, columns), lambda i, *_: (i, 0))


def pair_spec(rows):
    return pl.BlockSpec((2, rows, LANES), lambda i, *_: (0, i, 0))


def swapped(value, axis, mask):
    count = lax.axis_size(axis)
    return lax.ppermute(value, axis, [(at, at ^ mask) for at in range(count)])


def passed_along(value, axis, steps):
    count = lax.axis_size(axis)
    leading, last = (max(0, -steps), min(count, count - steps))
    return lax.ppermute(value, axis, [(source, source + steps) for source in range(leading, last)])


def spread(shard):
    dp, seq = lax.axis_size("dp"), lax.axis_size("seq")
    along = [shard] + [swapped(shard, "dp", 2 * at) for at in range(1, dp // 2)]
    held = jnp.stack(along)
    held = jnp.stack([held] + [swapped(held, "seq", at) for at in range(1, seq)])
    return held, swapped(held, "dp", 1)


def at_index(value, index, dim):
    return lax.dynamic_index_in_dim(value, index, dim, keepdims=False)


def core_halved(value):
    core = lax.axis_index("dp") % 2
    return at_index(value, core, 1) + swapped(at_index(value, 1 - core, 1), "dp", 1)


def summed_direct(value, dim, axis, scale):
    me = lax.axis_index(axis) // scale
    total = at_index(value, me, dim).astype(F32)
    for at in range(1, value.shape[dim]):
        total = total + swapped(at_index(value, me ^ at, dim), axis, at * scale).astype(F32)
    return total


def together(*values):
    return lax.optimization_barrier(values)


def on_device(
    block_in,
    routes,
    segments,
    cotangent,
    ln1_gain,
    ln1_bias,
    query_weight,
    kv_weight,
    router_weight,
    out_weight,
    ln2_gain,
    ln2_bias,
    up_weight,
    up_bias,
    down_weight,
    down_bias,
):
    micro_count, seq_count, local_len, width = block_in.shape
    full_len = segments.shape[2]
    experts = router_weight.shape[1]
    head = kv_weight.shape[1] // 2
    inner = experts * head
    ff = up_weight.shape[1]
    dp, shards = lax.axis_size("dp"), lax.axis_size("seq")
    devices = dp * shards
    own_rows, ff_rows, blocks = width // devices, ff // devices, ff // width
    aligned = own_rows % 16 == 0
    batch = micro_count * seq_count
    rows_all = batch * local_len
    tile = seq_count * local_len
    longest = full_len * 3 // 4
    reach = min(shards, (longest - 2) // local_len + 2)
    own_shard = lax.axis_index("seq")
    start_pos = own_shard * local_len

    def padded(value, columns):
        return jnp.pad(value, ((0, 0), (0, columns - value.shape[1])))

    a_cols = inner + 2 * LANES
    if aligned:
        packed_a, packed_b = pl.pallas_call(
            pack_kernel,
            out_shape=[
                jax.ShapeDtypeStruct((own_rows, a_cols), BF16),
                jax.ShapeDtypeStruct((ff_rows + (blocks + 1) * own_rows, width), BF16),
            ],
            compiler_params=call_params(),
            name="pack",
        )(
            query_weight,
            kv_weight,
            router_weight.T,
            down_weight,
            up_weight,
            out_weight,
            ln1_gain,
            ln1_bias,
            ln2_gain,
            ln2_bias,
            down_bias,
            up_bias,
        )
    else:
        rows = jnp.concatenate([ln1_gain, ln1_bias, ln2_gain, ln2_bias, down_bias, up_bias])
        rows = rows.reshape(5 + blocks, own_rows)
        extra = padded(jnp.concatenate([router_weight, rows.T], 1), LANES)
        packed_a = jnp.concatenate([query_weight, kv_weight, extra], 1)
        packed_b = jnp.concatenate(
            [down_weight]
            + [up_weight[:, at * width : (at + 1) * width] for at in range(blocks)]
            + [out_weight],
            0,
        )
    mine_a, mate_a = spread(packed_a)
    place = jnp.stack(
        [lax.axis_index("dp") // 2, lax.axis_index("dp") % 2, lax.axis_index("seq")]
    ).astype(jnp.int32)
    place_a = place
    if not aligned:
        held = jnp.moveaxis(jnp.stack([mine_a, mate_a]), 2, 0)
        for dim, at in ((0, 0), (1, 1), (2, 2)):
            order = jnp.arange(held.shape[dim], dtype=jnp.int32) ^ place[at]
            held = jnp.take(held, order, axis=dim)
        held = held.reshape(2, width // 2, a_cols)
        mine_a, mate_a = held[:1, None], held[1:, None]
        place_a = jnp.zeros_like(place)
    group_b = lax.all_gather(packed_b, ("dp", "seq"), axis=0, tiled=False)
    up_at, out_at = ff_rows, ff_rows + blocks * own_rows
    if aligned:
        nb, rb, fb = devices, own_rows, ff_rows
        weights = [group_b, group_b, group_b]
        weight_specs = [
            pl.BlockSpec((nb, ff_rows, width), lambda *_: (0, 0, 0), pipeline_mode=pl.Buffered(1)),
            pl.BlockSpec(
                (nb, blocks * own_rows, width), lambda *_: (0, 1, 0), pipeline_mode=pl.Buffered(1)
            ),
            pl.BlockSpec(
                (nb, own_rows, width),
                lambda *_: (0, out_at // own_rows, 0),
                pipeline_mode=pl.Buffered(1),
            ),
        ]
    else:
        nb, rb, fb = 1, width, ff
        up_all = group_b[:, up_at:out_at].reshape(devices, blocks, own_rows, width)
        weights = [
            group_b[:, :ff_rows].reshape(1, ff, width),
            jnp.moveaxis(up_all, 0, 1).reshape(1, ff, width),
            group_b[:, out_at:].reshape(1, width, width),
        ]
        weight_specs = [whole_spec(value.shape) for value in weights]

    tokens = block_in.reshape(rows_all, width)
    grad_out = cotangent.reshape(rows_all, width)
    route_rows = routes.reshape(rows_all, 2)

    seg_rows = segments.reshape(batch, full_len)
    seg_local = lax.dynamic_slice_in_dim(seg_rows, start_pos, local_len, 1)
    doc_start = jnp.sum(
        (seg_rows[:, None, :] < seg_local[:, :, None]).astype(jnp.int32), -1, dtype=jnp.int32
    )
    doc_start = jnp.maximum(doc_start - (own_shard - (reach - 1)) * local_len, 0)
    bounds = jnp.concatenate([doc_start[:, 0], own_shard.reshape(1).astype(jnp.int32)])
    starts = doc_start.reshape(batch, 1, local_len)

    steps = micro_count
    hidden, keyvals, group_a = pl.pallas_call(
        functools.partial(keyval_kernel, experts, head),
        grid=(steps,),
        in_specs=[
            pl.BlockSpec(memory_space=pltpu.SMEM),
            row_spec(tile, width),
            whole_spec(mine_a.shape),
            whole_spec(mate_a.shape),
        ],
        out_specs=[row_spec(tile, width), row_spec(tile, LANES), whole_spec((width, a_cols))],
        out_shape=[
            jax.ShapeDtypeStruct((rows_all, width), BF16),
            jax.ShapeDtypeStruct((rows_all, LANES), BF16),
            jax.ShapeDtypeStruct((width, a_cols), BF16),
        ],
        scratch_shapes=[
            pltpu.VMEM((2 * mine_a.shape[0] * mine_a.shape[1],) + mine_a.shape[2:], BF16)
        ],
        compiler_params=call_params(),
        cost_estimate=cost(2 * rows_all * width * LANES, rows_all * width * 4),
        name="keyval",
    )(place_a, tokens, mine_a, mate_a)

    own_pieces = keyvals.reshape(batch, local_len, LANES)
    pieces = [own_pieces] + [passed_along(own_pieces, "seq", back) for back in range(1, reach)]
    pieces = pieces[::-1]

    queries, gates = pl.pallas_call(
        functools.partial(query_kernel, experts, head),
        grid=(steps,),
        in_specs=[row_spec(tile, width), row_spec(tile, 2), whole_spec((width, a_cols))],
        out_specs=[pair_spec(tile), row_spec(tile, LANES)],
        out_shape=[
            jax.ShapeDtypeStruct((2, rows_all, LANES), BF16),
            jax.ShapeDtypeStruct((rows_all, LANES), F32),
        ],
        compiler_params=call_params(),
        cost_estimate=cost(2 * rows_all * width * (a_cols + 512), rows_all * width * 4),
        name="query",
    )(hidden, route_rows, group_a)

    columns = group_a[:, inner + LANES :].astype(F32)
    small = jnp.pad(columns[:, experts + 2 : experts + 5].T, ((0, 4), (0, ff - width)))
    up_row = columns[:, experts + 5 : experts + 5 + blocks]
    up_row = jnp.swapaxes(up_row.reshape(devices, own_rows, blocks), 1, 2).reshape(1, ff)
    vectors = jnp.concatenate([up_row, small], 0)

    piece_spec = pl.BlockSpec((1, local_len, LANES), lambda b, *_: (b, 0, 0))
    q_spec = pl.BlockSpec((2, local_len, LANES), lambda b, *_: (0, b, 0))
    start_spec = pl.BlockSpec((1, 1, local_len), lambda b, *_: (b, 0, 0))
    lse_spec = pl.BlockSpec((1, 2, local_len), lambda b, *_: (b, 0, 0))
    pairs = rows_all * full_len
    mixed, lse = pl.pallas_call(
        functools.partial(attend_kernel, reach, head),
        grid_spec=pltpu.PrefetchScalarGridSpec(
            num_scalar_prefetch=1,
            grid=(batch,),
            in_specs=[q_spec, start_spec] + [piece_spec] * reach,
            out_specs=[q_spec, lse_spec],
            scratch_shapes=[
                pltpu.VMEM((reach, local_len, LANES), BF16),
                pltpu.VMEM((2, local_len), F32),
                pltpu.VMEM((2, local_len), F32),
                pltpu.VMEM((2, head, local_len), F32),
            ],
        ),
        out_shape=[
            jax.ShapeDtypeStruct((2, rows_all, LANES), F32),
            jax.ShapeDtypeStruct((batch, 2, local_len), F32),
        ],
        compiler_params=call_params(),
        cost_estimate=cost(4 * pairs * LANES, rows_all * LANES * 16, pairs),
        name="attend",
    )(bounds, queries, starts, *pieces)

    grad_rows = ff_rows + (blocks + 2) * own_rows if aligned else ff + (blocks + 2) * width
    core_index = (lax.axis_index("dp") % 2).reshape(1).astype(jnp.int32)
    if aligned:
        leaving = [(dp // 2, shards, grad_rows, width)] * 2
    else:
        leaving = [(nb, grad_rows, width)]
    block_out, grad_mid, grad_mixed, side, *grads_b = pl.pallas_call(
        functools.partial(mid_kernel, experts, head),
        grid=(steps,),
        in_specs=[
            row_spec(tile, width),
            row_spec(tile, width),
            row_spec(tile, LANES),
            pair_spec(tile),
            whole_spec((8, ff)),
            pl.BlockSpec(memory_space=pltpu.SMEM),
        ]
        + weight_specs,
        out_specs=[
            row_spec(tile, width),
            row_spec(tile, width),
            pair_spec(tile),
            row_spec(tile, LANES),
        ]
        + [whole_spec(shape) for shape in leaving],
        out_shape=[
            jax.ShapeDtypeStruct((rows_all, width), BF16),
            jax.ShapeDtypeStruct((rows_all, width), F32),
            jax.ShapeDtypeStruct((2, rows_all, LANES), BF16),
            jax.ShapeDtypeStruct((rows_all, LANES), F32),
        ]
        + [jax.ShapeDtypeStruct(shape, BF16) for shape in leaving],
        scratch_shapes=[
            pltpu.VMEM((inner, width), F32),
            pltpu.VMEM((width, ff), F32),
            pltpu.VMEM((width, ff), F32),
            pltpu.VMEM((LANES, width), F32),
            pltpu.VMEM((LANES, ff), F32),
            pltpu.VMEM((tile, width), F32),
            pltpu.VMEM((tile, width), F32),
        ],
        compiler_params=call_params(),
        cost_estimate=cost(6 * rows_all * width * (2 * ff + width), rows_all * width * 16),
        name="mid",
    )(tokens, grad_out, gates, mixed, vectors, core_index, *weights)

    if not aligned:
        parts = grads_b[0][0]
        down_part = parts[:ff].reshape(devices, ff_rows, width)
        up_part = parts[ff : 2 * ff].reshape(blocks, devices, own_rows, width)
        up_part = jnp.moveaxis(up_part, 0, 1).reshape(devices, blocks * own_rows, width)
        out_part = parts[2 * ff : 2 * ff + width].reshape(devices, own_rows, width)
        tail = parts[2 * ff + width :]
        rows_up = tail.reshape(width, blocks, LANES)[:, :, 8].T.reshape(devices, own_rows, blocks)
        rows_vec = tail[:, :8].reshape(devices, own_rows, 8)
        rows_up = jnp.moveaxis(rows_up.reshape(devices, blocks, own_rows), 1, 2)
        tail = jnp.zeros((devices, own_rows, blocks, LANES), BF16)
        tail = tail.at[:, :, :, 8].set(rows_up).at[:, :, 0, :8].set(rows_vec)
        tail = tail.reshape(devices, own_rows, width)
        packed = jnp.concatenate([down_part, up_part, out_part, tail], 1)
        packed = packed.reshape((dp // 2, 2, shards) + packed.shape[1:])
        grads_b = [at_index(packed, core_index[0], 1), at_index(packed, 1 - core_index[0], 1)]

    keep, send = grads_b
    bits = shards.bit_length() - 1
    order = [1 << at for at in range(bits)]
    orders = (order, order[bits // 2 :] + order[: bits // 2])
    half_rows = keep.shape[2] // 2
    remaining = [list(reversed(order)), list(reversed(order))]
    halves = [None, None]
    arriving = swapped(send, "dp", 1)

    def core_step():
        held = keep + arriving
        held = held.reshape((dp // 2,) + (2,) * bits + held.shape[2:])
        halves[0] = held[..., :half_rows, :]
        halves[1] = held[..., half_rows:, :]

    leave_spec = pl.BlockSpec((shards, 1, local_len, LANES), lambda b, *_: (0, b, 0, 0))

    def send_halves(stage):
        for part in range(2):
            mask = orders[part][stage]
            dim = 1 + remaining[part].index(mask)
            remaining[part].remove(mask)
            bit = (own_shard // mask) % 2
            halves[part] = at_index(halves[part], bit, dim), at_index(halves[part], 1 - bit, dim)
        return [swapped(halves[part][1], "seq", orders[part][stage]) for part in range(2)]

    core_step()
    pending = send_halves(0)
    stage = 1
    bounds_now, *kept = together(bounds, halves[0][0], halves[1][0])
    grad_queries = None
    returned = []
    splits = [0, max(1, micro_count - 1), micro_count] if micro_count > 1 else [0, 1]
    for micro, stop in zip(splits[:-1], splits[1:]):
        count = (stop - micro) * seq_count

        def at_micro(block, dims, base=micro * seq_count):
            if dims == "b":
                return pl.BlockSpec(block, lambda b, *_: (base + b, 0, 0))
            return pl.BlockSpec(block, lambda b, *_: (0, base + b, 0))

        q_at = at_micro((2, local_len, LANES), "q")
        in_specs = [
            q_at,
            q_at,
            pl.BlockSpec(
                (local_len, LANES), lambda b, *_, base=micro * seq_count: (base + b, 0)
            ),
            at_micro((1, 2, local_len), "b"),
            at_micro((1, 1, local_len), "b"),
        ]
        in_specs += [at_micro((1, local_len, LANES), "b")] * reach
        operands = [queries, grad_mixed, side, lse, starts, *pieces]
        aliases = {}
        if micro:
            in_specs.append(pl.BlockSpec(memory_space=pl.ANY))
            operands.append(grad_queries)
            aliases = {len(operands): 0}
        grad_queries, leave = pl.pallas_call(
            functools.partial(
                attend_back_kernel, reach, head, micro * seq_count, int(micro > 0)
            ),
            grid_spec=pltpu.PrefetchScalarGridSpec(
                num_scalar_prefetch=1,
                grid=(count,),
                in_specs=in_specs,
                out_specs=[q_at, leave_spec],
                scratch_shapes=[
                    pltpu.VMEM((reach, local_len, LANES), BF16),
                    pltpu.VMEM((reach, local_len, LANES), F32),
                    pltpu.VMEM((2, head, local_len), F32),
                ],
            ),
            out_shape=[
                jax.ShapeDtypeStruct((2, rows_all, LANES), BF16),
                jax.ShapeDtypeStruct((shards, count, local_len, LANES), BF16),
            ],
            input_output_aliases=aliases,
            compiler_params=call_params(),
            cost_estimate=cost(
                10 * pairs * LANES * count // batch,
                count * local_len * LANES * 32,
                pairs * count // batch,
            ),
            name="attend_back",
        )(bounds_now, *operands)
        returned.append(lax.all_to_all(leave, "seq", 0, 0, tiled=True))
        if micro == 0 and stage < bits:
            pending[0], pending[1], grad_queries = together(*pending, grad_queries)
            halves[0], halves[1] = kept[0] + pending[0], kept[1] + pending[1]
            pending = send_halves(stage)
            stage += 1
            bounds_now, *kept = together(bounds, halves[0][0], halves[1][0])

    pending[0], pending[1], grad_queries = together(*pending, grad_queries)
    halves[0], halves[1] = kept[0] + pending[0], kept[1] + pending[1]
    while stage < bits:
        pending = send_halves(stage)
        halves[0], halves[1] = halves[0][0] + pending[0], halves[1][0] + pending[1]
        stage += 1
    own_b = jnp.concatenate(halves, 1)
    z_me = lax.axis_index("dp") // 2
    z_bits = (dp // 2).bit_length() - 1
    own_b = own_b.reshape((2,) * z_bits + own_b.shape[1:])
    z_stage = 0

    def z_split(value):
        bit = (z_me >> z_stage) & 1
        dim = z_bits - 1 - z_stage
        return at_index(value, bit, dim), at_index(value, 1 - bit, dim)

    arriving_b = None
    if z_bits:
        kept_b, send_b = z_split(own_b)
        side, kept_b = together(side, kept_b)
        arriving_b = swapped(send_b, "dp", 2)
        z_stage = 1
    partial_hidden, d_query, d_router = pl.pallas_call(
        functools.partial(query_grad_kernel, experts, head),
        grid=(steps,),
        in_specs=[
            row_spec(tile, width),
            pair_spec(tile),
            row_spec(tile, LANES),
            whole_spec((width, a_cols)),
        ],
        out_specs=[
            row_spec(tile, width),
            whole_spec((width, inner)),
            whole_spec((width, LANES)),
        ],
        out_shape=[
            jax.ShapeDtypeStruct((rows_all, width), F32),
            jax.ShapeDtypeStruct((width, inner), BF16),
            jax.ShapeDtypeStruct((width, LANES), F32),
        ],
        scratch_shapes=[pltpu.VMEM((width, inner), F32), pltpu.VMEM((width, LANES), F32)],
        compiler_params=call_params(),
        cost_estimate=cost(4 * rows_all * width * a_cols, rows_all * width * 12),
        name="query_grad",
    )(hidden, grad_queries, side, group_a)
    if z_bits > 1:
        arriving_b, partial_hidden = together(arriving_b, partial_hidden)
        kept_b, send_b = z_split(kept_b + arriving_b)
        partial_hidden, kept_b = together(partial_hidden, kept_b)
        arriving_b = swapped(send_b, "dp", 4)
        z_stage = 2
    if aligned:
        small_shapes = [(dp // 2, shards, own_rows, a_cols)] * 2
    else:
        small_shapes = [(width, a_cols)]
    grad_in, *small = pl.pallas_call(
        functools.partial(last_kernel, experts, head, tuple(zip(splits[:-1], splits[1:]))),
        grid=(steps,),
        in_specs=[
            pl.BlockSpec(memory_space=pltpu.SMEM),
            row_spec(tile, width),
            row_spec(tile, width),
            row_spec(tile, width),
            row_spec(tile, width),
            whole_spec((width, inner)),
            whole_spec((width, LANES)),
            whole_spec((width, a_cols)),
        ]
        + [whole_spec(piece.shape) for piece in returned],
        out_specs=[row_spec(tile, width)] + [whole_spec(shape) for shape in small_shapes],
        out_shape=[
            jax.ShapeDtypeStruct((rows_all, width), F32),
        ]
        + [jax.ShapeDtypeStruct(shape, BF16) for shape in small_shapes],
        scratch_shapes=[
            pltpu.VMEM((width, LANES), F32),
            pltpu.VMEM((LANES, width), F32),
            pltpu.VMEM((tile, LANES), BF16),
        ],
        compiler_params=call_params(),
        cost_estimate=cost(4 * rows_all * width * LANES, rows_all * width * 16),
        name="last",
    )(core_index, tokens, hidden, partial_hidden, grad_mid, d_query, d_router, group_a, *returned)
    if not aligned:
        by_core = small[0].reshape(dp // 2, 2, shards, own_rows, a_cols)
        small = [at_index(by_core, core_index[0], 1), at_index(by_core, 1 - core_index[0], 1)]
    keep_small, send_small = small
    if arriving_b is not None:
        send_small, arriving_b = together(send_small, arriving_b)
        own_b = kept_b + arriving_b
    while z_stage < z_bits:
        kept_b, send_b = z_split(own_b)
        own_b = kept_b + swapped(send_b, "dp", 2 << z_stage)
        z_stage += 1
    held = keep_small + swapped(send_small, "dp", 1)
    held = summed_direct(held, 1, "seq", 1).astype(BF16)
    ends = [at_index(held, z_me, 0)]
    ends += [swapped(at_index(held, z_me ^ at, 0), "dp", 2 * at) for at in range(1, dp // 2)]

    out_at_b, tail_at = ff_rows + blocks * own_rows, ff_rows + (blocks + 1) * own_rows
    if aligned:
        vector_shape = jax.ShapeDtypeStruct((own_rows,), F32)
        grad_down, grad_up, grad_out_weight, grad_up_bias, *second_vectors = pl.pallas_call(
            finish_second_kernel,
            out_shape=[
                jax.ShapeDtypeStruct((ff_rows, width), F32),
                jax.ShapeDtypeStruct((own_rows, ff), F32),
                jax.ShapeDtypeStruct((own_rows, width), F32),
                jax.ShapeDtypeStruct((ff_rows,), F32),
            ]
            + [vector_shape] * 3,
            compiler_params=call_params(),
            name="finish_second",
        )(own_b)
        grad_query, grad_kv, grad_router, *first_vectors = pl.pallas_call(
            functools.partial(finish_first_kernel, len(ends)),
            out_shape=[
                jax.ShapeDtypeStruct((own_rows, inner), F32),
                jax.ShapeDtypeStruct((own_rows, 2 * head), F32),
                jax.ShapeDtypeStruct((experts, own_rows), F32),
            ]
            + [vector_shape] * 2,
            compiler_params=call_params(),
            name="finish_first",
        )(*ends)
        grad_router = grad_router.T
    else:
        own_b = own_b.astype(F32)
        total = sum([piece.astype(F32) for piece in ends])
        ends = own_b[tail_at:]
        grad_up = jnp.concatenate(
            [
                own_b[ff_rows + at * own_rows : ff_rows + (at + 1) * own_rows]
                for at in range(blocks)
            ],
            1,
        )
        grad_up_bias = jnp.concatenate([ends[:, at * LANES + 8] for at in range(blocks)])
        grad_down, grad_out_weight = own_b[:ff_rows], own_b[out_at_b:tail_at]
        second_vectors = [ends[:, at] for at in range(3)]
        grad_query, grad_kv = total[:, :inner], total[:, inner : inner + 2 * head]
        total = total[:, inner + LANES :]
        grad_router = total[:, :experts]
        first_vectors = [total[:, experts], total[:, experts + 1]]
    return (
        block_out.reshape(block_in.shape),
        grad_in.reshape(block_in.shape),
        first_vectors[0],
        first_vectors[1],
        grad_query,
        grad_kv,
        grad_router,
        grad_out_weight,
        second_vectors[0],
        second_vectors[1],
        grad_up,
        grad_up_bias,
        grad_down,
        second_vectors[2],
    )


def solution(mesh):
    rows = P(("dp", "seq"), None)
    vector = P(("dp", "seq"))
    data = P(None, "dp", "seq", None)
    weights = (
        vector,
        vector,
        rows,
        rows,
        rows,
        rows,
        vector,
        vector,
        rows,
        vector,
        rows,
        vector,
    )
    return jax.shard_map(
        on_device,
        mesh=mesh,
        in_specs=(data, data, P(None, "dp", None), data) + weights,
        out_specs=(data, data) + weights,
        check_vma=False,
    )
```

```python
import functools

import jax
import jax.numpy as jnp
from jax import lax
from jax.experimental import pallas as pl
from jax.experimental.pallas import tpu as pltpu
from jax.sharding import PartitionSpec as P

EPS = 1e-05
LANES = 128
MIB = 1024 * 1024
BF16 = jnp.bfloat16
F32 = jnp.float32


def call_params():
    return pltpu.CompilerParams(vmem_limit_bytes=56 * MIB)


def cost(flops, bytes_accessed, transcendentals=0):
    return pl.CostEstimate(
        flops=int(flops), bytes_accessed=int(bytes_accessed), transcendentals=int(transcendentals)
    )


def dot_nn(left, right):
    return lax.dot_general(left, right, (((1,), (0,)), ((), ())), preferred_element_type=F32)


def dot_nt(left, right):
    return lax.dot_general(left, right, (((1,), (1,)), ((), ())), preferred_element_type=F32)


def lanes_of(rows, width):
    return lax.broadcasted_iota(jnp.int32, (rows, width), 1)


def fold_matrix(width, head, shift):
    source = lax.broadcasted_iota(jnp.int32, (width, LANES), 0)
    target = lax.broadcasted_iota(jnp.int32, (width, LANES), 1)
    return jnp.where(target == shift + lax.rem(source, head), 1.0, 0.0).astype(BF16)


def unfold_matrix(width, head, shift):
    source = lax.broadcasted_iota(jnp.int32, (LANES, width), 1)
    target = lax.broadcasted_iota(jnp.int32, (LANES, width), 0)
    return jnp.where(target == shift + lax.rem(source, head), 1.0, 0.0).astype(BF16)


def rows_of(columns, picked):
    row = lax.broadcasted_iota(jnp.int32, (8, LANES), 0)
    lane = lax.broadcasted_iota(jnp.int32, (8, LANES), 1)
    chosen = jnp.zeros((8, LANES), F32)
    for at, column in enumerate(picked):
        chosen = jnp.where((row == at) & (lane == column), 1.0, chosen)
    return dot_nt(chosen.astype(BF16), columns)


def normalize(values):
    centered = values - jnp.mean(values, -1, keepdims=True)
    inv_dev = lax.rsqrt(jnp.mean(centered * centered, -1, keepdims=True) + EPS)
    return centered * inv_dev, inv_dev


def norm_back(grad, gain, normed, inv_dev):
    scaled = grad * gain
    return inv_dev * (
        scaled
        - jnp.mean(scaled, -1, keepdims=True)
        - normed * jnp.mean(scaled * normed, -1, keepdims=True)
    )


def pack_kernel(query_ref, kv_ref, router_ref, down_ref, up_ref, out_ref, *rest):
    *vector_refs, up_bias_ref, first_ref, second_ref = rest
    own_rows, width = query_ref.shape
    first_ref[:, :width] = query_ref[...]
    first_ref[:, width : width + LANES] = kv_ref[...]
    rows = [router_ref[...].astype(F32)]
    rows += [ref[...].astype(F32).reshape(1, own_rows) for ref in vector_refs]
    bias = up_bias_ref[...].astype(F32).reshape(1, up_bias_ref.shape[0])
    rows += [
        bias[:, at * own_rows : (at + 1) * own_rows] for at in range(bias.shape[1] // own_rows)
    ]
    count = router_ref.shape[0] + len(rows) - 1
    rows.append(jnp.zeros((32 - count, own_rows), F32))
    rows = jnp.concatenate(rows, 0).astype(BF16)
    row = lax.broadcasted_iota(jnp.int32, (32, LANES), 0)
    lane = lax.broadcasted_iota(jnp.int32, (32, LANES), 1)
    chosen = jnp.where(lane == row, 1.0, 0.0).astype(BF16)
    turned = lax.dot_general(rows, chosen, (((0,), (0,)), ((), ())), preferred_element_type=F32)
    first_ref[:, width + LANES :] = turned.astype(BF16)
    ff_rows = down_ref.shape[0]
    second_ref[:ff_rows] = down_ref[...]
    blocks = up_ref.shape[1] // width
    for at in range(blocks):
        low = ff_rows + at * own_rows
        second_ref[low : low + own_rows] = up_ref[:, at * width : (at + 1) * width]
    second_ref[ff_rows + blocks * own_rows :] = out_ref[...]


def in_order(place_ref, parts, put):
    z_me, core_me, seq_me = place_ref[0], place_ref[1], place_ref[2]
    for core, part in enumerate(parts):
        for seq in range(part.shape[0]):
            for z in range(part.shape[1]):
                dp_at = (z_me ^ z) * 2 + (core_me ^ core)
                put(dp_at * part.shape[0] + (seq_me ^ seq), part[seq, z])


def keyval_kernel(experts, head, place_ref, x_ref, mine_ref, mate_ref, *rest):
    hidden_ref, kv_ref, weight_ref, blocks_ref = rest

    @pl.when(pl.program_id(0) == 0)
    def _():
        def put(device, block):
            blocks_ref[device] = block

        in_order(place_ref, (mine_ref, mate_ref), put)
        weight_ref[...] = blocks_ref[...].reshape(weight_ref.shape)

    inner = experts * head
    vectors = rows_of(weight_ref[:, inner + LANES :], (experts, experts + 1))
    normed, _ = normalize(x_ref[...].astype(F32))
    hidden = (normed * vectors[0:1] + vectors[1:2]).astype(BF16)
    hidden_ref[...] = hidden
    kv_ref[...] = dot_nn(hidden, weight_ref[:, inner : inner + LANES]).astype(BF16)


def query_kernel(experts, head, hidden_ref, routes_ref, weight_ref, q_ref, gate_ref):
    inner = experts * head
    hidden = hidden_ref[...]
    rows = hidden.shape[0]
    logits = dot_nn(hidden, weight_ref[:, inner + LANES :])
    lane = lanes_of(rows, LANES)
    first, second = routes_ref[:, 0:1], routes_ref[:, 1:2]
    logit_one = jnp.sum(jnp.where(lane == first, logits, 0.0), -1, keepdims=True)
    logit_two = jnp.sum(jnp.where(lane == second, logits, 0.0), -1, keepdims=True)
    peak = jnp.maximum(logit_one, logit_two)
    exp_one = jnp.exp(logit_one - peak)
    exp_two = jnp.exp(logit_two - peak)
    total = exp_one + exp_two
    gates = jnp.where(lane == 0, exp_one / total, jnp.where(lane == 1, exp_two / total, 0.0))
    gates = jnp.where(lane == 2, first.astype(F32), gates)
    gate_ref[...] = jnp.where(lane == 3, second.astype(F32), gates)
    queries = (dot_nn(hidden, weight_ref[:, :inner]) * (head**-0.5)).astype(BF16)
    owner = lax.div(lanes_of(rows, inner), head)
    fold = fold_matrix(inner, head, 0)
    zero = jnp.zeros_like(queries)
    q_ref[0] = dot_nn(jnp.where(owner == first, queries, zero), fold).astype(BF16)
    q_ref[1] = dot_nn(jnp.where(owner == second, queries, zero), fold).astype(BF16)


def masked(scores, start, key_at, query_at=None):
    keys = key_at + lax.broadcasted_iota(jnp.int32, scores.shape, 0)
    seen = keys >= start
    if query_at is not None:
        lane = lax.broadcasted_iota(jnp.int32, (1, scores.shape[1]), 1)
        seen = seen & (keys <= query_at + lax.rem(lane, scores.shape[1] // 2))
    return jnp.where(seen, scores, -1e30)


def by_halves(ref):
    half = ref.shape[1] // 2
    return [
        jnp.concatenate([ref[0, at * half : (at + 1) * half], ref[1, at * half : (at + 1) * half]], 0)
        for at in range(2)
    ]


def from_halves(ref, groups):
    half = ref.shape[1] // 2
    for at, group in enumerate(groups):
        ref[0, at * half : (at + 1) * half] = group[:half]
        ref[1, at * half : (at + 1) * half] = group[half:]


def row_halves(row):
    half = row.shape[1] // 2
    return [
        jnp.concatenate([row[:, at * half : (at + 1) * half]] * 2, 1) for at in range(2)
    ]


def over_pieces(step, bounds_ref, seq, reach, local):
    low = jnp.minimum(bounds_ref[seq] // local, reach - 1)

    def body(at, carry):
        step(at)
        return carry

    lax.fori_loop(low, reach - 1, body, 0)


def attend_kernel(reach, head, bounds_ref, q_ref, start_ref, *rest):
    pieces = rest[:reach]
    mixed_ref, lse_ref, kv_buf, peak_ref, total_ref, acc_ref = rest[reach:]
    seq = pl.program_id(0)
    local = pieces[0].shape[1]
    half = local // 2
    for at in range(reach - 1):
        kv_buf[at] = pieces[at][0]
    queries = by_halves(q_ref)
    starts = row_halves(start_ref[0])
    peak_ref[...] = jnp.full_like(peak_ref, -1e30)
    total_ref[...] = jnp.zeros_like(total_ref)
    acc_ref[...] = jnp.zeros_like(acc_ref)

    def turned_values(keyval):
        return keyval.T[head:]

    def accumulate(group, scores, values):
        old = peak_ref[group : group + 1]
        peak = jnp.maximum(old, jnp.max(scores, 0, keepdims=True))
        fade = jnp.exp(old - peak)
        expo = jnp.exp(scores - peak)
        total_ref[group : group + 1] = total_ref[group : group + 1] * fade + jnp.sum(
            expo, 0, keepdims=True
        )
        acc_ref[group] = acc_ref[group] * fade + dot_nn(values, expo.astype(BF16))
        peak_ref[group : group + 1] = peak

    def step(at):
        keyval = kv_buf[at]
        values = turned_values(keyval)
        for group in range(2):
            scores = masked(dot_nt(keyval, queries[group]), starts[group], at * local)
            accumulate(group, scores, values)

    over_pieces(step, bounds_ref, seq, reach, local)
    own = pieces[reach - 1][0]
    own_at = (reach - 1) * local
    values = turned_values(own)
    for group in range(2):
        keys = half * (group + 1)
        scores = masked(
            dot_nt(own[:keys], queries[group]), starts[group], own_at, own_at + group * half
        )
        accumulate(group, scores, values[:, :keys])
    groups = []
    for group in range(2):
        mixed = acc_ref[group] / total_ref[group : group + 1]
        groups.append(jnp.concatenate([jnp.zeros_like(mixed), mixed], 0).T)
    from_halves(mixed_ref, groups)
    lse_ref[0] = peak_ref[...] + jnp.log(total_ref[...])


def mid_kernel(
    experts,
    head,
    x_ref,
    dy_ref,
    gate_ref,
    mixed_ref,
    vector_ref,
    core_ref,
    down_ref,
    up_ref,
    wo_ref,
    out_ref,
    grad_mid_ref,
    grad_mixed_ref,
    side_ref,
    *rest,
):
    *grads_refs, acc_out, acc_up, acc_down, acc_vec, acc_upb, branch_ref, gsec_ref = rest
    step, last = pl.program_id(0), pl.num_programs(0) - 1
    rows, width = x_ref.shape
    inner = experts * head
    owners, own_rows = wo_ref.shape[:2]
    ff_rows = down_ref.shape[1]
    ff = owners * ff_rows
    blocks = ff // width

    @pl.when(step == 0)
    def _():
        acc_out[...] = jnp.zeros_like(acc_out)
        acc_up[...] = jnp.zeros_like(acc_up)
        acc_down[...] = jnp.zeros_like(acc_down)
        acc_vec[...] = jnp.zeros_like(acc_vec)
        acc_upb[...] = jnp.zeros_like(acc_upb)

    gain, shift = vector_ref[1:2, :width], vector_ref[2:3, :width]
    down_bias = vector_ref[3:4, :width]
    gate_one, gate_two = gate_ref[:, 0:1], gate_ref[:, 1:2]
    first, second = gate_ref[:, 2:3].astype(jnp.int32), gate_ref[:, 3:4].astype(jnp.int32)
    owner = lax.div(lanes_of(rows, inner), head)
    unfold = unfold_matrix(inner, head, head)
    fold = fold_matrix(inner, head, head)
    wo = wo_ref[...].reshape(inner, width)
    mixed_one, mixed_two = mixed_ref[0], mixed_ref[1]
    routed_one = dot_nn((gate_one * mixed_one).astype(BF16), unfold)
    routed_two = dot_nn((gate_two * mixed_two).astype(BF16), unfold)
    routed = jnp.where(
        owner == first, routed_one, jnp.where(owner == second, routed_two, 0.0)
    )
    routed = routed.astype(BF16)
    middle = x_ref[...].astype(F32) + dot_nn(routed, wo)
    normed, inv_dev = normalize(middle)
    second_low = (normed * gain + shift).astype(BF16)
    second_t = second_low.T
    dy = dy_ref[...]
    dy_wide = dy.astype(F32)
    dy_t = dy.T
    branch_ref[...] = middle + down_bias
    gsec_ref[...] = jnp.zeros_like(gsec_ref)
    per_block = width // ff_rows if owners > 1 else 1

    def down_block(at):
        if owners > 1:
            return down_ref[at * per_block : (at + 1) * per_block].reshape(width, width)
        return down_ref[0, at * width : (at + 1) * width, :]

    def up_block(at):
        return up_ref[:, at * own_rows : (at + 1) * own_rows, :].reshape(width, width)

    def ahead(at):
        lo = at * width
        pre_act = dot_nn(second_low, up_block(at)) + vector_ref[0:1, lo : lo + width]
        return pre_act, dot_nt(dy, down_block(at)).astype(BF16)

    ready = ahead(0)
    for at in range(blocks):
        lo = at * width
        pre_act, grad_active = ready
        if at + 1 < blocks:
            ready = ahead(at + 1)
        sigma = jax.nn.sigmoid(pre_act)
        active = (pre_act * sigma).astype(BF16)
        slope = sigma * (1.0 + pre_act * (1.0 - sigma))
        grad_low = (grad_active.astype(F32) * slope).astype(BF16)
        branch_ref[...] += dot_nn(active, down_block(at))
        gsec_ref[...] += dot_nt(grad_low, up_block(at))
        acc_down[:, lo : lo + width] += dot_nn(dy_t, active)
        acc_up[:, lo : lo + width] += dot_nn(second_t, grad_low)
        acc_upb[8:9, lo : lo + width] += jnp.sum(grad_low.astype(F32), 0, keepdims=True)

    out_ref[...] = branch_ref[...].astype(BF16)
    gsec = gsec_ref[...]
    acc_vec[0:1] += jnp.sum(gsec * normed, 0, keepdims=True)
    acc_vec[1:2] += jnp.sum(gsec, 0, keepdims=True)
    acc_vec[2:3] += jnp.sum(dy_wide, 0, keepdims=True)
    grad_mid = dy_wide + norm_back(gsec, gain, normed, inv_dev)
    grad_mid_ref[...] = grad_mid
    grad_att = grad_mid.astype(BF16)
    acc_out[...] += dot_nn(routed.T, grad_att)
    grad_routed = dot_nt(grad_att, wo).astype(BF16)
    zero = jnp.zeros_like(grad_routed)
    picked_one = dot_nn(jnp.where(owner == first, grad_routed, zero), fold)
    picked_two = dot_nn(jnp.where(owner == second, grad_routed, zero), fold)
    grad_mixed_one = (gate_one * picked_one).astype(BF16)
    grad_mixed_two = (gate_two * picked_two).astype(BF16)
    grad_mixed_ref[0] = grad_mixed_one
    grad_mixed_ref[1] = grad_mixed_two
    inner_one = jnp.sum(grad_mixed_one.astype(F32) * mixed_one, -1, keepdims=True)
    inner_two = jnp.sum(grad_mixed_two.astype(F32) * mixed_two, -1, keepdims=True)
    grad_one = jnp.sum(picked_one * mixed_one, -1, keepdims=True)
    grad_two = jnp.sum(picked_two * mixed_two, -1, keepdims=True)
    common = gate_one * grad_one + gate_two * grad_two
    lane = lanes_of(rows, LANES)
    side = jnp.where(lane == first, gate_one * (grad_one - common), 0.0)
    side = jnp.where(lane == second, gate_two * (grad_two - common), side)
    side = jnp.where(lane == head, inner_one, side)
    side = jnp.where(lane == head + 1, inner_two, side)
    side = jnp.where(lane == head + 2, first.astype(F32), side)
    side_ref[...] = jnp.where(lane == head + 3, second.astype(F32), side)

    @pl.when(step == last)
    def _():
        up_at, out_at = ff_rows, ff_rows + blocks * own_rows

        def leave(value, columns, row, count, group):
            if owners == 1:
                grads_refs[0][0, row : row + value.shape[0], columns] = value
                return
            keep_ref, send_ref = grads_refs
            seqs = keep_ref.shape[1]
            parts = value.reshape(value.shape[0] // (2 * seqs * count), 2, seqs, count, -1)
            planes = parts.shape[0]
            other = core_ref[0] == 1
            low, high = parts[:, 0], parts[:, 1]
            where = (slice(group * planes, (group + 1) * planes), slice(None), slice(row, row + count), columns)
            keep_ref[where] = jnp.where(other, high, low)
            send_ref[where] = jnp.where(other, low, high)

        everything = slice(None)
        for at in range(blocks):
            lo = at * width
            turned = acc_down[:, lo : lo + width].T.astype(BF16)
            leave(turned, everything, lo if owners == 1 else 0, ff_rows, at)
            leave(
                acc_up[:, lo : lo + width].astype(BF16),
                everything,
                up_at + at * own_rows,
                own_rows,
                0,
            )
        leave(acc_out[...].astype(BF16), everything, out_at, own_rows, 0)
        vectors_turned = acc_vec[...].T
        extra = acc_upb[...].T
        if owners > 1:
            extra = extra.reshape(owners, blocks, own_rows, LANES)
        for at in range(blocks):
            if owners > 1:
                part = extra[:, at].reshape(width, LANES)
            else:
                part = extra[at * width : (at + 1) * width]
            if at == 0:
                part = part + vectors_turned
            columns = slice(at * LANES, (at + 1) * LANES)
            leave(part.astype(BF16), columns, out_at + own_rows, own_rows, 0)


def attend_back_kernel(
    reach, head, first_seq, chained, bounds_ref, q_ref, grad_ref, side_ref, lse_ref, start_ref, *rest
):
    pieces = rest[:reach]
    rest = rest[reach + chained :]
    grad_q_ref, leave_ref, kv_buf, acc_kv, acc_q = rest
    seq = first_seq + pl.program_id(0)
    local = pieces[0].shape[1]
    half = local // 2
    for at in range(reach - 1):
        kv_buf[at] = pieces[at][0]
    acc_kv[...] = jnp.zeros_like(acc_kv)
    acc_q[...] = jnp.zeros_like(acc_q)
    queries = by_halves(q_ref)
    grads = by_halves(grad_ref)
    side = side_ref[...].T
    inner_rows = [side[head + at : head + at + 1] for at in range(2)]
    starts = row_halves(start_ref[0])
    inners = [
        jnp.concatenate([row[:, at * half : (at + 1) * half] for row in inner_rows], 1)
        for at in range(2)
    ]
    log_sums = [lse_ref[0, at : at + 1] for at in range(2)]

    def one_group(group, keyval, keys_turned, mask):
        scores = mask(dot_nt(keyval, queries[group]))
        probs = jnp.exp(scores - log_sums[group])
        grad_probs = dot_nt(keyval, grads[group])
        grad_scores = (probs * (grad_probs - inners[group])).astype(BF16)
        acc_q[group] += dot_nn(keys_turned, grad_scores)
        return dot_nn(grad_scores, queries[group]) + dot_nn(probs.astype(BF16), grads[group])

    def turned_keys(keyval):
        return keyval.T[:head]

    def step(at):
        keyval = kv_buf[at]
        turned = turned_keys(keyval)
        added = []
        for group in range(2):

            def mask(scores):
                return masked(scores, starts[group], at * local)

            added.append(one_group(group, keyval, turned, mask))
        acc_kv[at] += added[0] + added[1]

    over_pieces(step, bounds_ref, seq, reach, local)
    own = pieces[reach - 1][0]
    own_at = (reach - 1) * local
    turned = turned_keys(own)
    for group in range(2):
        keys = half * (group + 1)
        added = one_group(
            group,
            own[:keys],
            turned[:, :keys],
            lambda scores: masked(scores, starts[group], own_at, own_at + group * half),
        )
        acc_kv[reach - 1, :keys] += added
    groups = []
    for group in range(2):
        grad_q = acc_q[group] * (head**-0.5)
        groups.append(jnp.concatenate([grad_q, jnp.zeros_like(grad_q)], 0).T.astype(BF16))
    from_halves(grad_q_ref, groups)
    shards = leave_ref.shape[0]
    me = bounds_ref[bounds_ref.shape[0] - 1]
    for at in range(shards):

        @pl.when((at > me) | (at <= me - reach))
        def _():
            leave_ref[at, 0] = jnp.zeros((local, LANES), BF16)

    for at in range(reach):
        target = me - (reach - 1) + at

        @pl.when(target >= 0)
        def _():
            leave_ref[target, 0] = acc_kv[at].astype(BF16)


def query_grad_kernel(
    experts,
    head,
    hidden_ref,
    grad_q_ref,
    grad_logit_ref,
    weight_ref,
    partial_ref,
    d_query_ref,
    d_router_ref,
    acc_query,
    acc_router,
):
    step, last = pl.program_id(0), pl.num_programs(0) - 1
    rows, width = hidden_ref.shape
    inner = experts * head

    @pl.when(step == 0)
    def _():
        acc_query[...] = jnp.zeros_like(acc_query)
        acc_router[...] = jnp.zeros_like(acc_router)

    side = grad_logit_ref[...]
    first = side[:, head + 2 : head + 3].astype(jnp.int32)
    second = side[:, head + 3 : head + 4].astype(jnp.int32)
    owner = lax.div(lanes_of(rows, inner), head)
    unfold = unfold_matrix(inner, head, 0)
    grad_queries = jnp.where(
        owner == first,
        dot_nn(grad_q_ref[0], unfold),
        jnp.where(owner == second, dot_nn(grad_q_ref[1], unfold), 0.0),
    ).astype(BF16)
    grad_logits = jnp.where(lanes_of(rows, LANES) < experts, side, 0.0)
    logit_high = grad_logits.astype(BF16)
    logit_low = (grad_logits - logit_high.astype(F32)).astype(BF16)
    router = weight_ref[:, inner + LANES :]
    partial_ref[...] = (
        dot_nt(grad_queries, weight_ref[:, :inner])
        + dot_nt(logit_high, router)
        + dot_nt(logit_low, router)
    )
    hidden_t = hidden_ref[...].T
    acc_query[...] += dot_nn(hidden_t, grad_queries)
    acc_router[...] += dot_nn(hidden_t, logit_high) + dot_nn(hidden_t, logit_low)

    @pl.when(step == last)
    def _():
        d_query_ref[...] = acc_query[...].astype(BF16)
        d_router_ref[...] = acc_router[...]


def last_kernel(
    experts,
    head,
    parts,
    core_ref,
    x_ref,
    hidden_ref,
    partial_ref,
    grad_mid_ref,
    query_ref,
    router_ref,
    weight_ref,
    *rest,
):
    pieces = rest[: len(parts)]
    grad_in_ref, *leaving, acc_kv, acc_vec, summed_ref = rest[len(parts) :]
    step, last = pl.program_id(0), pl.num_programs(0) - 1
    rows, width = x_ref.shape
    inner = experts * head

    @pl.when(step == 0)
    def _():
        acc_kv[...] = jnp.zeros_like(acc_kv)
        acc_vec[...] = jnp.zeros_like(acc_vec)

    for piece, (low, high) in zip(pieces, parts):

        @pl.when((step >= low) & (step < high))
        def _():
            per_step = piece.shape[1] // (high - low)
            base = (step - low) * per_step
            summed = piece[0, pl.ds(base, per_step)].astype(F32)
            for at in range(1, piece.shape[0]):
                summed = summed + piece[at, pl.ds(base, per_step)].astype(F32)
            summed_ref[...] = summed.astype(BF16).reshape(summed_ref.shape)

    gain = rows_of(weight_ref[:, inner + LANES :], (experts,))[0:1]
    normed, inv_dev = normalize(x_ref[...].astype(F32))
    grad_keyvals = summed_ref[...]
    grad_hidden = partial_ref[...] + dot_nt(grad_keyvals, weight_ref[:, inner : inner + LANES])
    grad_in_ref[...] = grad_mid_ref[...] + norm_back(grad_hidden, gain, normed, inv_dev)
    hidden_t = hidden_ref[...].T
    acc_kv[...] += dot_nn(hidden_t, grad_keyvals)
    acc_vec[experts : experts + 1] += jnp.sum(grad_hidden * normed, 0, keepdims=True)
    acc_vec[experts + 1 : experts + 2] += jnp.sum(grad_hidden, 0, keepdims=True)

    @pl.when(step == last)
    def _():
        extra = router_ref[...] + acc_vec[...].T
        for value, low in (
            (query_ref[...], 0),
            (acc_kv[...].astype(BF16), inner),
            (extra.astype(BF16), inner + LANES),
        ):
            columns = slice(low, low + value.shape[1])
            if len(leaving) == 1:
                leaving[0][:, columns] = value
                continue
            keep_ref, send_ref = leaving
            planes, seqs, own_rows = keep_ref.shape[:3]
            by_core = value.reshape(planes, 2, seqs, own_rows, value.shape[1])
            other = core_ref[0] == 1
            keep_ref[:, :, :, columns] = jnp.where(other, by_core[:, 1], by_core[:, 0])
            send_ref[:, :, :, columns] = jnp.where(other, by_core[:, 0], by_core[:, 1])


def finish_second_kernel(total_ref, down_ref, up_ref, out_ref, up_bias_ref, *vector_refs):
    ff_rows, width = down_ref.shape
    own_rows, ff = up_ref.shape
    blocks = ff // width
    down_ref[...] = total_ref[:ff_rows].astype(F32)
    for at in range(blocks):
        low = ff_rows + at * own_rows
        up_ref[:, at * width : (at + 1) * width] = total_ref[low : low + own_rows].astype(F32)
    low = ff_rows + blocks * own_rows
    out_ref[...] = total_ref[low : low + own_rows].astype(F32)
    turned = total_ref[low + own_rows :].astype(F32).T
    up_bias_ref[...] = jnp.concatenate([turned[at * LANES + 8] for at in range(blocks)], 0)
    for at, ref in enumerate(vector_refs):
        ref[...] = turned[at]


def finish_first_kernel(count, *refs):
    query_ref, kv_ref, router_ref, gain_ref, bias_ref = refs[count:]
    total = refs[0][...].astype(F32)
    for ref in refs[1:count]:
        total = total + ref[...].astype(F32)
    inner, pair, experts = query_ref.shape[1], kv_ref.shape[1], router_ref.shape[0]
    query_ref[...] = total[:, :inner]
    kv_ref[...] = total[:, inner : inner + pair]
    turned = total[:, inner + LANES :].T
    router_ref[...] = turned[:experts]
    gain_ref[...] = turned[experts]
    bias_ref[...] = turned[experts + 1]


def whole_spec(shape):
    zeros = (0,) * len(shape)
    return pl.BlockSpec(shape, lambda *_: zeros, pipeline_mode=pl.Buffered(1))


def row_spec(rows, columns):
    return pl.BlockSpec((rows, columns), lambda i, *_: (i, 0))


def pair_spec(rows):
    return pl.BlockSpec((2, rows, LANES), lambda i, *_: (0, i, 0))


def swapped(value, axis, mask):
    count = lax.axis_size(axis)
    return lax.ppermute(value, axis, [(at, at ^ mask) for at in range(count)])


def passed_along(value, axis, steps):
    count = lax.axis_size(axis)
    leading, last = (max(0, -steps), min(count, count - steps))
    return lax.ppermute(value, axis, [(source, source + steps) for source in range(leading, last)])


def spread(shard):
    dp, seq = lax.axis_size("dp"), lax.axis_size("seq")
    along = [shard] + [swapped(shard, "dp", 2 * at) for at in range(1, dp // 2)]
    held = jnp.stack(along)
    held = jnp.stack([held] + [swapped(held, "seq", at) for at in range(1, seq)])
    return held, swapped(held, "dp", 1)


def at_index(value, index, dim):
    return lax.dynamic_index_in_dim(value, index, dim, keepdims=False)


def core_halved(value):
    core = lax.axis_index("dp") % 2
    return at_index(value, core, 1) + swapped(at_index(value, 1 - core, 1), "dp", 1)


def summed_direct(value, dim, axis, scale):
    me = lax.axis_index(axis) // scale
    total = at_index(value, me, dim).astype(F32)
    for at in range(1, value.shape[dim]):
        total = total + swapped(at_index(value, me ^ at, dim), axis, at * scale).astype(F32)
    return total


def together(*values):
    return lax.optimization_barrier(values)


def on_device(
    block_in,
    routes,
    segments,
    cotangent,
    ln1_gain,
    ln1_bias,
    query_weight,
    kv_weight,
    router_weight,
    out_weight,
    ln2_gain,
    ln2_bias,
    up_weight,
    up_bias,
    down_weight,
    down_bias,
):
    micro_count, seq_count, local_len, width = block_in.shape
    full_len = segments.shape[2]
    experts = router_weight.shape[1]
    head = kv_weight.shape[1] // 2
    inner = experts * head
    ff = up_weight.shape[1]
    dp, shards = lax.axis_size("dp"), lax.axis_size("seq")
    devices = dp * shards
    own_rows, ff_rows, blocks = width // devices, ff // devices, ff // width
    aligned = own_rows % 16 == 0
    batch = micro_count * seq_count
    rows_all = batch * local_len
    tile = seq_count * local_len
    longest = full_len * 3 // 4
    reach = min(shards, (longest - 2) // local_len + 2)
    own_shard = lax.axis_index("seq")
    start_pos = own_shard * local_len

    def padded(value, columns):
        return jnp.pad(value, ((0, 0), (0, columns - value.shape[1])))

    a_cols = inner + 2 * LANES
    if aligned:
        packed_a, packed_b = pl.pallas_call(
            pack_kernel,
            out_shape=[
                jax.ShapeDtypeStruct((own_rows, a_cols), BF16),
                jax.ShapeDtypeStruct((ff_rows + (blocks + 1) * own_rows, width), BF16),
            ],
            compiler_params=call_params(),
            name="pack",
        )(
            query_weight,
            kv_weight,
            router_weight.T,
            down_weight,
            up_weight,
            out_weight,
            ln1_gain,
            ln1_bias,
            ln2_gain,
            ln2_bias,
            down_bias,
            up_bias,
        )
    else:
        rows = jnp.concatenate([ln1_gain, ln1_bias, ln2_gain, ln2_bias, down_bias, up_bias])
        rows = rows.reshape(5 + blocks, own_rows)
        extra = padded(jnp.concatenate([router_weight, rows.T], 1), LANES)
        packed_a = jnp.concatenate([query_weight, kv_weight, extra], 1)
        packed_b = jnp.concatenate(
            [down_weight]
            + [up_weight[:, at * width : (at + 1) * width] for at in range(blocks)]
            + [out_weight],
            0,
        )
    mine_a, mate_a = spread(packed_a)
    place = jnp.stack(
        [lax.axis_index("dp") // 2, lax.axis_index("dp") % 2, lax.axis_index("seq")]
    ).astype(jnp.int32)
    place_a = place
    if not aligned:
        held = jnp.moveaxis(jnp.stack([mine_a, mate_a]), 2, 0)
        for dim, at in ((0, 0), (1, 1), (2, 2)):
            order = jnp.arange(held.shape[dim], dtype=jnp.int32) ^ place[at]
            held = jnp.take(held, order, axis=dim)
        held = held.reshape(2, width // 2, a_cols)
        mine_a, mate_a = held[:1, None], held[1:, None]
        place_a = jnp.zeros_like(place)
    group_b = lax.all_gather(packed_b, ("dp", "seq"), axis=0, tiled=False)
    up_at, out_at = ff_rows, ff_rows + blocks * own_rows
    if aligned:
        nb, rb, fb = devices, own_rows, ff_rows
        weights = [group_b, group_b, group_b]
        weight_specs = [
            pl.BlockSpec((nb, ff_rows, width), lambda *_: (0, 0, 0), pipeline_mode=pl.Buffered(1)),
            pl.BlockSpec(
                (nb, blocks * own_rows, width), lambda *_: (0, 1, 0), pipeline_mode=pl.Buffered(1)
            ),
            pl.BlockSpec(
                (nb, own_rows, width),
                lambda *_: (0, out_at // own_rows, 0),
                pipeline_mode=pl.Buffered(1),
            ),
        ]
    else:
        nb, rb, fb = 1, width, ff
        up_all = group_b[:, up_at:out_at].reshape(devices, blocks, own_rows, width)
        weights = [
            group_b[:, :ff_rows].reshape(1, ff, width),
            jnp.moveaxis(up_all, 0, 1).reshape(1, ff, width),
            group_b[:, out_at:].reshape(1, width, width),
        ]
        weight_specs = [whole_spec(value.shape) for value in weights]

    tokens = block_in.reshape(rows_all, width)
    grad_out = cotangent.reshape(rows_all, width)
    route_rows = routes.reshape(rows_all, 2)

    seg_rows = segments.reshape(batch, full_len)
    seg_local = lax.dynamic_slice_in_dim(seg_rows, start_pos, local_len, 1)
    doc_start = jnp.sum(
        (seg_rows[:, None, :] < seg_local[:, :, None]).astype(jnp.int32), -1, dtype=jnp.int32
    )
    doc_start = jnp.maximum(doc_start - (own_shard - (reach - 1)) * local_len, 0)
    bounds = jnp.concatenate([doc_start[:, 0], own_shard.reshape(1).astype(jnp.int32)])
    starts = doc_start.reshape(batch, 1, local_len)

    steps = micro_count
    hidden, keyvals, group_a = pl.pallas_call(
        functools.partial(keyval_kernel, experts, head),
        grid=(steps,),
        in_specs=[
            pl.BlockSpec(memory_space=pltpu.SMEM),
            row_spec(tile, width),
            whole_spec(mine_a.shape),
            whole_spec(mate_a.shape),
        ],
        out_specs=[row_spec(tile, width), row_spec(tile, LANES), whole_spec((width, a_cols))],
        out_shape=[
            jax.ShapeDtypeStruct((rows_all, width), BF16),
            jax.ShapeDtypeStruct((rows_all, LANES), BF16),
            jax.ShapeDtypeStruct((width, a_cols), BF16),
        ],
        scratch_shapes=[
            pltpu.VMEM((2 * mine_a.shape[0] * mine_a.shape[1],) + mine_a.shape[2:], BF16)
        ],
        compiler_params=call_params(),
        cost_estimate=cost(2 * rows_all * width * LANES, rows_all * width * 4),
        name="keyval",
    )(place_a, tokens, mine_a, mate_a)

    own_pieces = keyvals.reshape(batch, local_len, LANES)
    pieces = [own_pieces] + [passed_along(own_pieces, "seq", back) for back in range(1, reach)]
    pieces = pieces[::-1]

    queries, gates = pl.pallas_call(
        functools.partial(query_kernel, experts, head),
        grid=(steps,),
        in_specs=[row_spec(tile, width), row_spec(tile, 2), whole_spec((width, a_cols))],
        out_specs=[pair_spec(tile), row_spec(tile, LANES)],
        out_shape=[
            jax.ShapeDtypeStruct((2, rows_all, LANES), BF16),
            jax.ShapeDtypeStruct((rows_all, LANES), F32),
        ],
        compiler_params=call_params(),
        cost_estimate=cost(2 * rows_all * width * (a_cols + 512), rows_all * width * 4),
        name="query",
    )(hidden, route_rows, group_a)

    columns = group_a[:, inner + LANES :].astype(F32)
    small = jnp.pad(columns[:, experts + 2 : experts + 5].T, ((0, 4), (0, ff - width)))
    up_row = columns[:, experts + 5 : experts + 5 + blocks]
    up_row = jnp.swapaxes(up_row.reshape(devices, own_rows, blocks), 1, 2).reshape(1, ff)
    vectors = jnp.concatenate([up_row, small], 0)

    piece_spec = pl.BlockSpec((1, local_len, LANES), lambda b, *_: (b, 0, 0))
    q_spec = pl.BlockSpec((2, local_len, LANES), lambda b, *_: (0, b, 0))
    start_spec = pl.BlockSpec((1, 1, local_len), lambda b, *_: (b, 0, 0))
    lse_spec = pl.BlockSpec((1, 2, local_len), lambda b, *_: (b, 0, 0))
    pairs = rows_all * full_len
    mixed, lse = pl.pallas_call(
        functools.partial(attend_kernel, reach, head),
        grid_spec=pltpu.PrefetchScalarGridSpec(
            num_scalar_prefetch=1,
            grid=(batch,),
            in_specs=[q_spec, start_spec] + [piece_spec] * reach,
            out_specs=[q_spec, lse_spec],
            scratch_shapes=[
                pltpu.VMEM((reach, local_len, LANES), BF16),
                pltpu.VMEM((2, local_len), F32),
                pltpu.VMEM((2, local_len), F32),
                pltpu.VMEM((2, head, local_len), F32),
            ],
        ),
        out_shape=[
            jax.ShapeDtypeStruct((2, rows_all, LANES), F32),
            jax.ShapeDtypeStruct((batch, 2, local_len), F32),
        ],
        compiler_params=call_params(),
        cost_estimate=cost(4 * pairs * LANES, rows_all * LANES * 16, pairs),
        name="attend",
    )(bounds, queries, starts, *pieces)

    grad_rows = ff_rows + (blocks + 2) * own_rows if aligned else ff + (blocks + 2) * width
    core_index = (lax.axis_index("dp") % 2).reshape(1).astype(jnp.int32)
    if aligned:
        leaving = [(dp // 2, shards, grad_rows, width)] * 2
    else:
        leaving = [(nb, grad_rows, width)]
    block_out, grad_mid, grad_mixed, side, *grads_b = pl.pallas_call(
        functools.partial(mid_kernel, experts, head),
        grid=(steps,),
        in_specs=[
            row_spec(tile, width),
            row_spec(tile, width),
            row_spec(tile, LANES),
            pair_spec(tile),
            whole_spec((8, ff)),
            pl.BlockSpec(memory_space=pltpu.SMEM),
        ]
        + weight_specs,
        out_specs=[
            row_spec(tile, width),
            row_spec(tile, width),
            pair_spec(tile),
            row_spec(tile, LANES),
        ]
        + [whole_spec(shape) for shape in leaving],
        out_shape=[
            jax.ShapeDtypeStruct((rows_all, width), BF16),
            jax.ShapeDtypeStruct((rows_all, width), F32),
            jax.ShapeDtypeStruct((2, rows_all, LANES), BF16),
            jax.ShapeDtypeStruct((rows_all, LANES), F32),
        ]
        + [jax.ShapeDtypeStruct(shape, BF16) for shape in leaving],
        scratch_shapes=[
            pltpu.VMEM((inner, width), F32),
            pltpu.VMEM((width, ff), F32),
            pltpu.VMEM((width, ff), F32),
            pltpu.VMEM((LANES, width), F32),
            pltpu.VMEM((LANES, ff), F32),
            pltpu.VMEM((tile, width), F32),
            pltpu.VMEM((tile, width), F32),
        ],
        compiler_params=call_params(),
        cost_estimate=cost(6 * rows_all * width * (2 * ff + width), rows_all * width * 16),
        name="mid",
    )(tokens, grad_out, gates, mixed, vectors, core_index, *weights)

    if not aligned:
        parts = grads_b[0][0]
        down_part = parts[:ff].reshape(devices, ff_rows, width)
        up_part = parts[ff : 2 * ff].reshape(blocks, devices, own_rows, width)
        up_part = jnp.moveaxis(up_part, 0, 1).reshape(devices, blocks * own_rows, width)
        out_part = parts[2 * ff : 2 * ff + width].reshape(devices, own_rows, width)
        tail = parts[2 * ff + width :]
        rows_up = tail.reshape(width, blocks, LANES)[:, :, 8].T.reshape(devices, own_rows, blocks)
        rows_vec = tail[:, :8].reshape(devices, own_rows, 8)
        rows_up = jnp.moveaxis(rows_up.reshape(devices, blocks, own_rows), 1, 2)
        tail = jnp.zeros((devices, own_rows, blocks, LANES), BF16)
        tail = tail.at[:, :, :, 8].set(rows_up).at[:, :, 0, :8].set(rows_vec)
        tail = tail.reshape(devices, own_rows, width)
        packed = jnp.concatenate([down_part, up_part, out_part, tail], 1)
        packed = packed.reshape((dp // 2, 2, shards) + packed.shape[1:])
        grads_b = [at_index(packed, core_index[0], 1), at_index(packed, 1 - core_index[0], 1)]

    keep, send = grads_b
    bits, z_bits = shards.bit_length() - 1, (dp // 2).bit_length() - 1
    along_x = [("seq", 1 << at) for at in range(bits // 2)]
    along_y = [("seq", 1 << at) for at in range(bits // 2, bits)]
    along_z = [("dp", 2 << at) for at in range(z_bits)]
    near, far = along_z[:1], along_z[1:]
    dims = along_z[::-1] + along_y[::-1] + along_x[::-1]
    orders = [along_x + along_y + near, along_y + near + along_x, near + along_x + along_y]
    third = -(-keep.shape[2] // 24) * 8 if keep.shape[2] % 8 == 0 else -(-keep.shape[2] // 3)
    cuts = [0, third, 2 * third, keep.shape[2]]
    held = keep + swapped(send, "dp", 1)
    held = held.reshape((2,) * len(dims) + held.shape[2:])
    parts = [
        (held[..., low:high, :], dims, order)
        for low, high, order in zip(cuts[:-1], cuts[1:], orders)
    ]

    def send_parts(parts):
        stays, arrives = [], []
        for value, left, order in parts:
            axis, mask = order[0]
            dim, bit = left.index(order[0]), (lax.axis_index(axis) // mask) % 2
            left = left[:dim] + left[dim + 1 :]
            stays.append((at_index(value, bit, dim), left, order[1:]))
            arrives.append(swapped(at_index(value, 1 - bit, dim), axis, mask))
        return stays, arrives

    def behind(parts, other):
        *values, other = together(*[value for value, _, _ in parts], other)
        return [(value,) + part[1:] for value, part in zip(values, parts)], other

    def joined(parts, arrives):
        return [(part[0] + piece,) + part[1:] for part, piece in zip(parts, arrives)]

    leave_spec = pl.BlockSpec((shards, 1, local_len, LANES), lambda b, *_: (0, b, 0, 0))

    parts, arrives = send_parts(parts)
    parts, bounds_now = behind(parts, bounds)
    grad_queries = None
    returned = []
    splits = [0, max(1, micro_count - 1), micro_count] if micro_count > 1 else [0, 1]
    for micro, stop in zip(splits[:-1], splits[1:]):
        count = (stop - micro) * seq_count

        def at_micro(block, dims, base=micro * seq_count):
            if dims == "b":
                return pl.BlockSpec(block, lambda b, *_: (base + b, 0, 0))
            return pl.BlockSpec(block, lambda b, *_: (0, base + b, 0))

        q_at = at_micro((2, local_len, LANES), "q")
        in_specs = [
            q_at,
            q_at,
            pl.BlockSpec(
                (local_len, LANES), lambda b, *_, base=micro * seq_count: (base + b, 0)
            ),
            at_micro((1, 2, local_len), "b"),
            at_micro((1, 1, local_len), "b"),
        ]
        in_specs += [at_micro((1, local_len, LANES), "b")] * reach
        operands = [queries, grad_mixed, side, lse, starts, *pieces]
        aliases = {}
        if micro:
            in_specs.append(pl.BlockSpec(memory_space=pl.ANY))
            operands.append(grad_queries)
            aliases = {len(operands): 0}
        grad_queries, leave = pl.pallas_call(
            functools.partial(
                attend_back_kernel, reach, head, micro * seq_count, int(micro > 0)
            ),
            grid_spec=pltpu.PrefetchScalarGridSpec(
                num_scalar_prefetch=1,
                grid=(count,),
                in_specs=in_specs,
                out_specs=[q_at, leave_spec],
                scratch_shapes=[
                    pltpu.VMEM((reach, local_len, LANES), BF16),
                    pltpu.VMEM((reach, local_len, LANES), F32),
                    pltpu.VMEM((2, head, local_len), F32),
                ],
            ),
            out_shape=[
                jax.ShapeDtypeStruct((2, rows_all, LANES), BF16),
                jax.ShapeDtypeStruct((shards, count, local_len, LANES), BF16),
            ],
            input_output_aliases=aliases,
            compiler_params=call_params(),
            cost_estimate=cost(
                10 * pairs * LANES * count // batch,
                count * local_len * LANES * 32,
                pairs * count // batch,
            ),
            name="attend_back",
        )(bounds_now, *operands)
        returned.append(lax.all_to_all(leave, "seq", 0, 0, tiled=True))
        if parts[0][2]:
            *arrives, grad_queries = together(*arrives, grad_queries)
            parts, arrives = send_parts(joined(parts, arrives))
            if stop < micro_count:
                parts, bounds_now = behind(parts, bounds)
            else:
                parts, side = behind(parts, side)

    partial_hidden, d_query, d_router = pl.pallas_call(
        functools.partial(query_grad_kernel, experts, head),
        grid=(steps,),
        in_specs=[
            row_spec(tile, width),
            pair_spec(tile),
            row_spec(tile, LANES),
            whole_spec((width, a_cols)),
        ],
        out_specs=[
            row_spec(tile, width),
            whole_spec((width, inner)),
            whole_spec((width, LANES)),
        ],
        out_shape=[
            jax.ShapeDtypeStruct((rows_all, width), F32),
            jax.ShapeDtypeStruct((width, inner), BF16),
            jax.ShapeDtypeStruct((width, LANES), F32),
        ],
        scratch_shapes=[pltpu.VMEM((width, inner), F32), pltpu.VMEM((width, LANES), F32)],
        compiler_params=call_params(),
        cost_estimate=cost(4 * rows_all * width * a_cols, rows_all * width * 12),
        name="query_grad",
    )(hidden, grad_queries, side, group_a)
    *arrives, partial_hidden = together(*arrives, partial_hidden)
    parts = joined(parts, arrives)
    while parts[0][2]:
        parts = joined(*send_parts(parts))
    whole = jnp.concatenate([value for value, _, _ in parts], -2)
    parts, arrives = send_parts([(whole, parts[0][1], far)])
    parts, partial_hidden = behind(parts, partial_hidden)
    if aligned:
        small_shapes = [(dp // 2, shards, own_rows, a_cols)] * 2
    else:
        small_shapes = [(width, a_cols)]
    grad_in, *small = pl.pallas_call(
        functools.partial(last_kernel, experts, head, tuple(zip(splits[:-1], splits[1:]))),
        grid=(steps,),
        in_specs=[
            pl.BlockSpec(memory_space=pltpu.SMEM),
            row_spec(tile, width),
            row_spec(tile, width),
            row_spec(tile, width),
            row_spec(tile, width),
            whole_spec((width, inner)),
            whole_spec((width, LANES)),
            whole_spec((width, a_cols)),
        ]
        + [whole_spec(piece.shape) for piece in returned],
        out_specs=[row_spec(tile, width)] + [whole_spec(shape) for shape in small_shapes],
        out_shape=[
            jax.ShapeDtypeStruct((rows_all, width), F32),
        ]
        + [jax.ShapeDtypeStruct(shape, BF16) for shape in small_shapes],
        scratch_shapes=[
            pltpu.VMEM((width, LANES), F32),
            pltpu.VMEM((LANES, width), F32),
            pltpu.VMEM((tile, LANES), BF16),
        ],
        compiler_params=call_params(),
        cost_estimate=cost(4 * rows_all * width * LANES, rows_all * width * 16),
        name="last",
    )(core_index, tokens, hidden, partial_hidden, grad_mid, d_query, d_router, group_a, *returned)
    if not aligned:
        by_core = small[0].reshape(dp // 2, 2, shards, own_rows, a_cols)
        small = [at_index(by_core, core_index[0], 1), at_index(by_core, 1 - core_index[0], 1)]
    keep_small, send_small = small
    *arrives, send_small = together(*arrives, send_small)
    parts = joined(parts, arrives)
    while parts[0][2]:
        parts = joined(*send_parts(parts))
    own_b = parts[0][0]
    held = keep_small + swapped(send_small, "dp", 1)
    held = summed_direct(held, 1, "seq", 1).astype(BF16)
    z_me = lax.axis_index("dp") // 2
    ends = [at_index(held, z_me, 0)]
    ends += [swapped(at_index(held, z_me ^ at, 0), "dp", 2 * at) for at in range(1, dp // 2)]

    out_at_b, tail_at = ff_rows + blocks * own_rows, ff_rows + (blocks + 1) * own_rows
    if aligned:
        vector_shape = jax.ShapeDtypeStruct((own_rows,), F32)
        grad_down, grad_up, grad_out_weight, grad_up_bias, *second_vectors = pl.pallas_call(
            finish_second_kernel,
            out_shape=[
                jax.ShapeDtypeStruct((ff_rows, width), F32),
                jax.ShapeDtypeStruct((own_rows, ff), F32),
                jax.ShapeDtypeStruct((own_rows, width), F32),
                jax.ShapeDtypeStruct((ff_rows,), F32),
            ]
            + [vector_shape] * 3,
            compiler_params=call_params(),
            name="finish_second",
        )(own_b)
        grad_query, grad_kv, grad_router, *first_vectors = pl.pallas_call(
            functools.partial(finish_first_kernel, len(ends)),
            out_shape=[
                jax.ShapeDtypeStruct((own_rows, inner), F32),
                jax.ShapeDtypeStruct((own_rows, 2 * head), F32),
                jax.ShapeDtypeStruct((experts, own_rows), F32),
            ]
            + [vector_shape] * 2,
            compiler_params=call_params(),
            name="finish_first",
        )(*ends)
        grad_router = grad_router.T
    else:
        own_b = own_b.astype(F32)
        total = sum([piece.astype(F32) for piece in ends])
        ends = own_b[tail_at:]
        grad_up = jnp.concatenate(
            [
                own_b[ff_rows + at * own_rows : ff_rows + (at + 1) * own_rows]
                for at in range(blocks)
            ],
            1,
        )
        grad_up_bias = jnp.concatenate([ends[:, at * LANES + 8] for at in range(blocks)])
        grad_down, grad_out_weight = own_b[:ff_rows], own_b[out_at_b:tail_at]
        second_vectors = [ends[:, at] for at in range(3)]
        grad_query, grad_kv = total[:, :inner], total[:, inner : inner + 2 * head]
        total = total[:, inner + LANES :]
        grad_router = total[:, :experts]
        first_vectors = [total[:, experts], total[:, experts + 1]]
    return (
        block_out.reshape(block_in.shape),
        grad_in.reshape(block_in.shape),
        first_vectors[0],
        first_vectors[1],
        grad_query,
        grad_kv,
        grad_router,
        grad_out_weight,
        second_vectors[0],
        second_vectors[1],
        grad_up,
        grad_up_bias,
        grad_down,
        second_vectors[2],
    )


def solution(mesh):
    rows = P(("dp", "seq"), None)
    vector = P(("dp", "seq"))
    data = P(None, "dp", "seq", None)
    weights = (
        vector,
        vector,
        rows,
        rows,
        rows,
        rows,
        vector,
        vector,
        rows,
        vector,
        rows,
        vector,
    )
    return jax.shard_map(
        on_device,
        mesh=mesh,
        in_specs=(data, data, P(None, "dp", None), data) + weights,
        out_specs=(data, data) + weights,
        check_vma=False,
    )
```

```python
import functools

import jax
import jax.numpy as jnp
from jax import lax
from jax.experimental import pallas as pl
from jax.experimental.pallas import tpu as pltpu
from jax.sharding import PartitionSpec as P

EPS = 1e-05
LANES = 128
MIB = 1024 * 1024
BF16 = jnp.bfloat16
F32 = jnp.float32


def call_params(mib=56):
    return pltpu.CompilerParams(vmem_limit_bytes=mib * MIB)


def in_hbm(*values):
    return [pltpu.with_memory_space_constraint(value, pltpu.HBM) for value in values]


def cost(flops, bytes_accessed, transcendentals=0):
    return pl.CostEstimate(
        flops=int(flops), bytes_accessed=int(bytes_accessed), transcendentals=int(transcendentals)
    )


def dot_nn(left, right):
    return lax.dot_general(left, right, (((1,), (0,)), ((), ())), preferred_element_type=F32)


def dot_nt(left, right):
    return lax.dot_general(left, right, (((1,), (1,)), ((), ())), preferred_element_type=F32)


def lanes_of(rows, width):
    return lax.broadcasted_iota(jnp.int32, (rows, width), 1)


def fold_matrix(width, head, shift):
    source = lax.broadcasted_iota(jnp.int32, (width, LANES), 0)
    target = lax.broadcasted_iota(jnp.int32, (width, LANES), 1)
    return jnp.where(target == shift + lax.rem(source, head), 1.0, 0.0).astype(BF16)


def unfold_matrix(width, head, shift):
    source = lax.broadcasted_iota(jnp.int32, (LANES, width), 1)
    target = lax.broadcasted_iota(jnp.int32, (LANES, width), 0)
    return jnp.where(target == shift + lax.rem(source, head), 1.0, 0.0).astype(BF16)


def rows_of(columns, picked):
    row = lax.broadcasted_iota(jnp.int32, (8, LANES), 0)
    lane = lax.broadcasted_iota(jnp.int32, (8, LANES), 1)
    chosen = jnp.zeros((8, LANES), F32)
    for at, column in enumerate(picked):
        chosen = jnp.where((row == at) & (lane == column), 1.0, chosen)
    return dot_nt(chosen.astype(BF16), columns)


def normalize(values):
    centered = values - jnp.mean(values, -1, keepdims=True)
    inv_dev = lax.rsqrt(jnp.mean(centered * centered, -1, keepdims=True) + EPS)
    return centered * inv_dev, inv_dev


def norm_back(grad, gain, normed, inv_dev):
    scaled = grad * gain
    return inv_dev * (
        scaled
        - jnp.mean(scaled, -1, keepdims=True)
        - normed * jnp.mean(scaled * normed, -1, keepdims=True)
    )


def pack_kernel(query_ref, kv_ref, router_ref, down_ref, up_ref, out_ref, *rest):
    *vector_refs, up_bias_ref, first_ref, second_ref = rest
    own_rows, width = query_ref.shape
    first_ref[:, :width] = query_ref[...]
    first_ref[:, width : width + LANES] = kv_ref[...]
    rows = [router_ref[...].astype(F32)]
    rows += [ref[...].astype(F32).reshape(1, own_rows) for ref in vector_refs]
    bias = up_bias_ref[...].astype(F32).reshape(1, up_bias_ref.shape[0])
    rows += [
        bias[:, at * own_rows : (at + 1) * own_rows] for at in range(bias.shape[1] // own_rows)
    ]
    count = router_ref.shape[0] + len(rows) - 1
    rows.append(jnp.zeros((32 - count, own_rows), F32))
    rows = jnp.concatenate(rows, 0).astype(BF16)
    row = lax.broadcasted_iota(jnp.int32, (32, LANES), 0)
    lane = lax.broadcasted_iota(jnp.int32, (32, LANES), 1)
    chosen = jnp.where(lane == row, 1.0, 0.0).astype(BF16)
    turned = lax.dot_general(rows, chosen, (((0,), (0,)), ((), ())), preferred_element_type=F32)
    first_ref[:, width + LANES :] = turned.astype(BF16)
    ff_rows = down_ref.shape[0]
    second_ref[:ff_rows] = down_ref[...]
    blocks = up_ref.shape[1] // width
    for at in range(blocks):
        low = ff_rows + at * own_rows
        second_ref[low : low + own_rows] = up_ref[:, at * width : (at + 1) * width]
    second_ref[ff_rows + blocks * own_rows :] = out_ref[...]


def in_order(place_ref, parts, put):
    z_me, core_me, seq_me = place_ref[0], place_ref[1], place_ref[2]
    for core, part in enumerate(parts):
        for seq in range(part.shape[0]):
            for z in range(part.shape[1]):
                dp_at = (z_me ^ z) * 2 + (core_me ^ core)
                put(dp_at * part.shape[0] + (seq_me ^ seq), part[seq, z])


def keyval_kernel(experts, head, place_ref, x_ref, mine_ref, mate_ref, *rest):
    hidden_ref, kv_ref, weight_ref, blocks_ref = rest

    @pl.when(pl.program_id(0) == 0)
    def _():
        def put(device, block):
            blocks_ref[device] = block

        in_order(place_ref, (mine_ref, mate_ref), put)
        weight_ref[...] = blocks_ref[...].reshape(weight_ref.shape)

    inner = experts * head
    vectors = rows_of(weight_ref[:, inner + LANES :], (experts, experts + 1))
    normed, _ = normalize(x_ref[...].astype(F32))
    hidden = (normed * vectors[0:1] + vectors[1:2]).astype(BF16)
    hidden_ref[...] = hidden
    kv_ref[...] = dot_nn(hidden, weight_ref[:, inner : inner + LANES]).astype(BF16)


def query_kernel(experts, head, hidden_ref, routes_ref, weight_ref, q_ref, gate_ref):
    inner = experts * head
    hidden = hidden_ref[...]
    rows = hidden.shape[0]
    logits = dot_nn(hidden, weight_ref[:, inner + LANES :])
    lane = lanes_of(rows, LANES)
    first, second = routes_ref[:, 0:1], routes_ref[:, 1:2]
    logit_one = jnp.sum(jnp.where(lane == first, logits, 0.0), -1, keepdims=True)
    logit_two = jnp.sum(jnp.where(lane == second, logits, 0.0), -1, keepdims=True)
    peak = jnp.maximum(logit_one, logit_two)
    exp_one = jnp.exp(logit_one - peak)
    exp_two = jnp.exp(logit_two - peak)
    total = exp_one + exp_two
    gates = jnp.where(lane == 0, exp_one / total, jnp.where(lane == 1, exp_two / total, 0.0))
    gates = jnp.where(lane == 2, first.astype(F32), gates)
    gate_ref[...] = jnp.where(lane == 3, second.astype(F32), gates)
    queries = (dot_nn(hidden, weight_ref[:, :inner]) * (head**-0.5)).astype(BF16)
    owner = lax.div(lanes_of(rows, inner), head)
    fold = fold_matrix(inner, head, 0)
    zero = jnp.zeros_like(queries)
    q_ref[0] = dot_nn(jnp.where(owner == first, queries, zero), fold).astype(BF16)
    q_ref[1] = dot_nn(jnp.where(owner == second, queries, zero), fold).astype(BF16)


def masked(scores, start, key_at, query_at=None):
    keys = key_at + lax.broadcasted_iota(jnp.int32, scores.shape, 0)
    seen = keys >= start
    if query_at is not None:
        lane = lax.broadcasted_iota(jnp.int32, (1, scores.shape[1]), 1)
        seen = seen & (keys <= query_at + lax.rem(lane, scores.shape[1] // 2))
    return jnp.where(seen, scores, -1e30)


def by_halves(ref):
    half = ref.shape[1] // 2
    return [
        jnp.concatenate([ref[0, at * half : (at + 1) * half], ref[1, at * half : (at + 1) * half]], 0)
        for at in range(2)
    ]


def from_halves(ref, groups):
    half = ref.shape[1] // 2
    for at, group in enumerate(groups):
        ref[0, at * half : (at + 1) * half] = group[:half]
        ref[1, at * half : (at + 1) * half] = group[half:]


def row_halves(row):
    half = row.shape[1] // 2
    return [
        jnp.concatenate([row[:, at * half : (at + 1) * half]] * 2, 1) for at in range(2)
    ]


def over_pieces(step, bounds_ref, seq, reach, local):
    low = jnp.minimum(bounds_ref[seq] // local, reach - 1)

    def body(at, carry):
        step(at)
        return carry

    lax.fori_loop(low, reach - 1, body, 0)


def attend_kernel(reach, head, bounds_ref, q_ref, start_ref, *rest):
    pieces = rest[:reach]
    mixed_ref, lse_ref, kv_buf, peak_ref, total_ref, acc_ref = rest[reach:]
    seq = pl.program_id(0)
    local = pieces[0].shape[1]
    half = local // 2
    for at in range(reach - 1):
        kv_buf[at] = pieces[at][0]
    queries = by_halves(q_ref)
    starts = row_halves(start_ref[0])
    peak_ref[...] = jnp.full_like(peak_ref, -1e30)
    total_ref[...] = jnp.zeros_like(total_ref)
    acc_ref[...] = jnp.zeros_like(acc_ref)

    def turned_values(keyval):
        return keyval.T[head:]

    def accumulate(group, scores, values):
        old = peak_ref[group : group + 1]
        peak = jnp.maximum(old, jnp.max(scores, 0, keepdims=True))
        fade = jnp.exp(old - peak)
        expo = jnp.exp(scores - peak)
        total_ref[group : group + 1] = total_ref[group : group + 1] * fade + jnp.sum(
            expo, 0, keepdims=True
        )
        acc_ref[group] = acc_ref[group] * fade + dot_nn(values, expo.astype(BF16))
        peak_ref[group : group + 1] = peak

    def step(at):
        keyval = kv_buf[at]
        values = turned_values(keyval)
        for group in range(2):
            scores = masked(dot_nt(keyval, queries[group]), starts[group], at * local)
            accumulate(group, scores, values)

    over_pieces(step, bounds_ref, seq, reach, local)
    own = pieces[reach - 1][0]
    own_at = (reach - 1) * local
    values = turned_values(own)
    for group in range(2):
        keys = half * (group + 1)
        scores = masked(
            dot_nt(own[:keys], queries[group]), starts[group], own_at, own_at + group * half
        )
        accumulate(group, scores, values[:, :keys])
    groups = []
    for group in range(2):
        mixed = acc_ref[group] / total_ref[group : group + 1]
        groups.append(jnp.concatenate([jnp.zeros_like(mixed), mixed], 0).T)
    from_halves(mixed_ref, groups)
    lse_ref[0] = peak_ref[...] + jnp.log(total_ref[...])


def summed_by(values, chosen):
    matrix = jnp.where(chosen, 1.0, 0.0).astype(BF16)
    high = values.astype(BF16)
    low = (values - high.astype(F32)).astype(BF16)
    return dot_nn(high, matrix) + dot_nn(low, matrix)


def mid_scratch(rows_all, width, ff, weights, leaving):
    return (
        [pltpu.VMEM((rows_all, ff), BF16)] * 2
        + [pltpu.VMEM((width, rows_all), BF16)] * 3
        + [pltpu.VMEM((rows_all, width), BF16)]
        + [pltpu.VMEM((LANES, width), F32), pltpu.VMEM((LANES, ff), F32)]
        + [pltpu.VMEM(weights, BF16)]
        + [pltpu.VMEM(shape, BF16) for shape in leaving]
        + [pltpu.SemaphoreType.DMA((3,)), pltpu.SemaphoreType.DMA((2 + 4 * ff // width,))]
    )


def mid_kernel(
    experts,
    head,
    x_ref,
    dy_ref,
    gate_ref,
    mixed_ref,
    vector_ref,
    core_ref,
    weight_ref,
    out_ref,
    grad_mid_ref,
    grad_mixed_ref,
    side_ref,
    *rest,
):
    owners = weight_ref.shape[0]
    count = 2 if owners > 1 else 1
    leaving, rest = rest[:count], rest[count:]
    active_ref, grad_ref, dy_t_ref, second_t_ref, routed_t_ref, att_ref = rest[:6]
    acc_vec, acc_upb, kept_ref = rest[6:9]
    staged, (in_sems, out_sems) = rest[9 : 9 + count], rest[9 + count :]
    step, last = pl.program_id(0), pl.num_programs(0) - 1
    rows, width = x_ref.shape
    inner = experts * head
    own_rows = width // owners
    ff = active_ref.shape[1]
    ff_rows = ff // owners
    blocks = ff // width
    up_at, out_at = ff_rows, ff_rows + blocks * own_rows

    spans = ((out_at, out_at + own_rows), (0, ff_rows), (up_at, out_at))
    loads = [
        pltpu.make_async_copy(
            weight_ref.at[:, low:high, :], kept_ref.at[:, low:high, :], in_sems.at[at]
        )
        for at, (low, high) in enumerate(spans)
    ]

    @pl.when(step == 0)
    def _():
        for load in loads:
            load.start()
        acc_vec[...] = jnp.zeros_like(acc_vec)
        acc_upb[...] = jnp.zeros_like(acc_upb)
        loads[0].wait()

    gain, shift = vector_ref[1:2, :width], vector_ref[2:3, :width]
    down_bias = vector_ref[3:4, :width]
    gate_one, gate_two = gate_ref[:, 0:1], gate_ref[:, 1:2]
    first, second = gate_ref[:, 2:3].astype(jnp.int32), gate_ref[:, 3:4].astype(jnp.int32)
    owner = lax.div(lanes_of(rows, inner), head)
    unfold = unfold_matrix(inner, head, head)
    fold = fold_matrix(inner, head, head)
    wo = kept_ref[:, out_at : out_at + own_rows, :].reshape(inner, width)
    mixed_one, mixed_two = mixed_ref[0], mixed_ref[1]
    routed_one = dot_nn((gate_one * mixed_one).astype(BF16), unfold)
    routed_two = dot_nn((gate_two * mixed_two).astype(BF16), unfold)
    routed = jnp.where(
        owner == first, routed_one, jnp.where(owner == second, routed_two, 0.0)
    )
    routed = routed.astype(BF16)
    middle = x_ref[...].astype(F32) + dot_nn(routed, wo)
    normed, inv_dev = normalize(middle)
    second_low = (normed * gain + shift).astype(BF16)
    dy = dy_ref[...]
    dy_wide = dy.astype(F32)
    here = pl.ds(pl.multiple_of(step * rows, rows), rows)
    second_t_ref[:, here] = second_low.T
    dy_t_ref[:, here] = dy.T
    routed_t_ref[:, here] = routed.T
    per_block = width // ff_rows if owners > 1 else 1

    @pl.when(step == 0)
    def _():
        loads[1].wait()
        loads[2].wait()

    def down_block(at):
        if owners > 1:
            block = kept_ref[at * per_block : (at + 1) * per_block, :ff_rows, :]
            return block.reshape(width, width)
        return kept_ref[0, at * width : (at + 1) * width, :]

    def up_block(at):
        low = up_at + at * own_rows
        return kept_ref[:, low : low + own_rows, :].reshape(width, width)

    def ahead(at):
        lo = at * width
        pre_act = dot_nn(second_low, up_block(at)) + vector_ref[0:1, lo : lo + width]
        return pre_act, dot_nt(dy, down_block(at)).astype(BF16)

    ready = ahead(0)
    for at in range(blocks):
        lo = at * width
        pre_act, grad_active = ready
        if at + 1 < blocks:
            ready = ahead(at + 1)
        sigma = jax.nn.sigmoid(pre_act)
        active = (pre_act * sigma).astype(BF16)
        slope = sigma * (1.0 + pre_act * (1.0 - sigma))
        grad_low = (grad_active.astype(F32) * slope).astype(BF16)
        active_ref[here, lo : lo + width] = active
        grad_ref[here, lo : lo + width] = grad_low
        acc_upb[8:9, lo : lo + width] += jnp.sum(grad_low.astype(F32), 0, keepdims=True)

    down_all = jnp.concatenate([down_block(at) for at in range(blocks)], 0)
    up_all = jnp.concatenate([up_block(at) for at in range(blocks)], 1)
    out_ref[...] = (middle + down_bias + dot_nn(active_ref[here, :], down_all)).astype(BF16)
    gsec = dot_nt(grad_ref[here, :], up_all)
    acc_vec[0:1] += jnp.sum(gsec * normed, 0, keepdims=True)
    acc_vec[1:2] += jnp.sum(gsec, 0, keepdims=True)
    acc_vec[2:3] += jnp.sum(dy_wide, 0, keepdims=True)
    grad_mid = dy_wide + norm_back(gsec, gain, normed, inv_dev)
    grad_att = grad_mid.astype(BF16)
    grad_mid_ref[...] = grad_att
    att_ref[here, :] = grad_att
    grad_routed = dot_nt(grad_att, wo).astype(BF16)
    zero = jnp.zeros_like(grad_routed)
    picked_one = dot_nn(jnp.where(owner == first, grad_routed, zero), fold)
    picked_two = dot_nn(jnp.where(owner == second, grad_routed, zero), fold)
    grad_mixed_one = (gate_one * picked_one).astype(BF16)
    grad_mixed_two = (gate_two * picked_two).astype(BF16)
    grad_mixed_ref[0] = grad_mixed_one
    grad_mixed_ref[1] = grad_mixed_two
    spread_one = lax.broadcasted_iota(jnp.int32, (2 * LANES, 2 * LANES), 0) // LANES
    spread_two = lax.broadcasted_iota(jnp.int32, (2 * LANES, 2 * LANES), 1) // LANES
    sums = summed_by(
        jnp.concatenate([picked_one * mixed_one, picked_two * mixed_two], 1),
        spread_one == spread_two,
    )
    grad_one, grad_two = sums[:, :LANES], sums[:, LANES:]
    source = lax.broadcasted_iota(jnp.int32, (2 * LANES, LANES), 0) // LANES
    target = lax.broadcasted_iota(jnp.int32, (2 * LANES, LANES), 1)
    inners = summed_by(
        jnp.concatenate(
            [grad_mixed_one.astype(F32) * mixed_one, grad_mixed_two.astype(F32) * mixed_two], 1
        ),
        target == head + source,
    )
    common = gate_one * grad_one + gate_two * grad_two
    lane = lanes_of(rows, LANES)
    side = jnp.where(lane == first, gate_one * (grad_one - common), inners)
    side = jnp.where(lane == second, gate_two * (grad_two - common), side)
    side = jnp.where(lane == head + 2, gate_ref[:, 2:3], side)
    side_ref[...] = jnp.where(lane == head + 3, gate_ref[:, 3:4], side)

    @pl.when(step == last)
    def _():
        leaves = []

        def put(value, columns, row, count, group):
            if owners == 1:
                staged[0][0, row : row + value.shape[0], columns] = value
                return
            seqs = staged[0].shape[1]
            by_core = value.reshape(value.shape[0] // (2 * seqs * count), 2, seqs, count, -1)
            planes = by_core.shape[0]
            other = core_ref[0] == 1
            low, high = by_core[:, 0], by_core[:, 1]
            where = (slice(group * planes, (group + 1) * planes), slice(None), slice(row, row + count))
            staged[0][where + (columns,)] = jnp.where(other, high, low)
            staged[1][where + (columns,)] = jnp.where(other, low, high)

        def leave(where):
            for source, target in zip(staged, leaving):
                copy = pltpu.make_async_copy(
                    source.at[where], target.at[where], out_sems.at[len(leaves)]
                )
                copy.start()
                leaves.append(copy)

        everything = slice(None)

        def weight_block(at, carry):
            columns = pl.ds(pl.multiple_of(at * width, width), width)
            turned = dot_nn(dy_t_ref[...], active_ref[:, columns]).T.astype(BF16)
            straight = dot_nn(second_t_ref[...], grad_ref[:, columns]).astype(BF16)
            low = up_at + at * own_rows
            if owners == 1:
                staged[0][0, pl.ds(at * width, width), :] = turned
                staged[0][0, pl.ds(low, width), :] = straight
                return carry
            seqs = staged[0].shape[1]
            other = core_ref[0] == 1
            for value, rows_each, planes in ((turned, ff_rows, 1), (straight, own_rows, blocks)):
                by_core = value.reshape(-1, 2, seqs, rows_each, width)
                first_half, second_half = by_core[:, 0], by_core[:, 1]
                if planes == 1:
                    count = by_core.shape[0]
                    where = (pl.ds(at * count, count), everything, slice(0, ff_rows))
                else:
                    low = pl.multiple_of(up_at + at * own_rows, own_rows)
                    where = (everything, everything, pl.ds(low, own_rows))
                staged[0][where] = jnp.where(other, second_half, first_half)
                staged[1][where] = jnp.where(other, first_half, second_half)
                for copy in block_copies(at, planes > 1):
                    copy.start()
            return carry

        def block_copies(at, straight):
            count = staged[0].shape[0] // blocks
            if straight:
                low = pl.multiple_of(up_at + at * own_rows, own_rows)
                where = (everything, everything, pl.ds(low, own_rows))
            else:
                where = (pl.ds(at * count, count), everything, slice(0, ff_rows))
            base = 2 + 4 * at + 2 * int(straight)
            return [
                pltpu.make_async_copy(source.at[where], target.at[where], out_sems.at[base + side])
                for side, (source, target) in enumerate(zip(staged, leaving))
            ]

        def block_waits(at, carry):
            for straight in (False, True):
                for copy in block_copies(at, straight):
                    copy.wait()
            return carry

        lax.fori_loop(0, blocks, weight_block, 0)
        if owners == 1:
            leave((slice(0, 1), slice(0, out_at)))
        d_out = dot_nn(routed_t_ref[...], att_ref[...])
        put(d_out.astype(BF16), everything, out_at, own_rows, 0)
        vectors_turned = acc_vec[...].T
        extra = acc_upb[...].T
        if owners > 1:
            extra = extra.reshape(owners, blocks, own_rows, LANES)
        for at in range(blocks):
            if owners > 1:
                part = extra[:, at].reshape(width, LANES)
            else:
                part = extra[at * width : (at + 1) * width]
            if at == 0:
                part = part + vectors_turned
            columns = slice(at * LANES, (at + 1) * LANES)
            put(part.astype(BF16), columns, out_at + own_rows, own_rows, 0)
        ending = slice(out_at, out_at + 2 * own_rows)
        leave((slice(0, 1), ending) if owners == 1 else (everything, everything, ending))
        for copy in leaves:
            copy.wait()
        if owners > 1:
            lax.fori_loop(0, blocks, block_waits, 0)


def attend_back_kernel(
    reach, head, first_seq, chained, bounds_ref, q_ref, grad_ref, side_ref, lse_ref, start_ref, *rest
):
    pieces = rest[:reach]
    rest = rest[reach + chained :]
    grad_q_ref, leave_ref, kv_buf, acc_kv, acc_q = rest
    seq = first_seq + pl.program_id(0)
    local = pieces[0].shape[1]
    half = local // 2
    for at in range(reach - 1):
        kv_buf[at] = pieces[at][0]
    acc_kv[...] = jnp.zeros_like(acc_kv)
    acc_q[...] = jnp.zeros_like(acc_q)
    queries = by_halves(q_ref)
    grads = by_halves(grad_ref)
    side = side_ref[...].T
    inner_rows = [side[head + at : head + at + 1] for at in range(2)]
    starts = row_halves(start_ref[0])
    inners = [
        jnp.concatenate([row[:, at * half : (at + 1) * half] for row in inner_rows], 1)
        for at in range(2)
    ]
    log_sums = [lse_ref[0, at : at + 1] for at in range(2)]

    def one_group(group, keyval, keys_turned, mask):
        scores = mask(dot_nt(keyval, queries[group]))
        probs = jnp.exp(scores - log_sums[group])
        grad_probs = dot_nt(keyval, grads[group])
        grad_scores = (probs * (grad_probs - inners[group])).astype(BF16)
        acc_q[group] += dot_nn(keys_turned, grad_scores)
        return dot_nn(grad_scores, queries[group]) + dot_nn(probs.astype(BF16), grads[group])

    def turned_keys(keyval):
        return keyval.T[:head]

    def step(at):
        keyval = kv_buf[at]
        turned = turned_keys(keyval)
        added = []
        for group in range(2):

            def mask(scores):
                return masked(scores, starts[group], at * local)

            added.append(one_group(group, keyval, turned, mask))
        acc_kv[at] += added[0] + added[1]

    over_pieces(step, bounds_ref, seq, reach, local)
    own = pieces[reach - 1][0]
    own_at = (reach - 1) * local
    turned = turned_keys(own)
    for group in range(2):
        keys = half * (group + 1)
        added = one_group(
            group,
            own[:keys],
            turned[:, :keys],
            lambda scores: masked(scores, starts[group], own_at, own_at + group * half),
        )
        acc_kv[reach - 1, :keys] += added
    groups = []
    for group in range(2):
        grad_q = acc_q[group] * (head**-0.5)
        groups.append(jnp.concatenate([grad_q, jnp.zeros_like(grad_q)], 0).T.astype(BF16))
    from_halves(grad_q_ref, groups)
    shards = leave_ref.shape[0]
    me = bounds_ref[bounds_ref.shape[0] - 1]
    for at in range(shards):

        @pl.when((at > me) | (at <= me - reach))
        def _():
            leave_ref[at, 0] = jnp.zeros((local, LANES), BF16)

    for at in range(reach):
        target = me - (reach - 1) + at

        @pl.when(target >= 0)
        def _():
            leave_ref[target, 0] = acc_kv[at].astype(BF16)


def query_grad_kernel(
    experts,
    head,
    hidden_ref,
    grad_q_ref,
    grad_logit_ref,
    weight_ref,
    partial_ref,
    d_query_ref,
    d_router_ref,
    acc_query,
    acc_router,
):
    step, last = pl.program_id(0), pl.num_programs(0) - 1
    rows, width = hidden_ref.shape
    inner = experts * head

    @pl.when(step == 0)
    def _():
        acc_query[...] = jnp.zeros_like(acc_query)
        acc_router[...] = jnp.zeros_like(acc_router)

    side = grad_logit_ref[...]
    first = side[:, head + 2 : head + 3].astype(jnp.int32)
    second = side[:, head + 3 : head + 4].astype(jnp.int32)
    owner = lax.div(lanes_of(rows, inner), head)
    unfold = unfold_matrix(inner, head, 0)
    grad_queries = jnp.where(
        owner == first,
        dot_nn(grad_q_ref[0], unfold),
        jnp.where(owner == second, dot_nn(grad_q_ref[1], unfold), 0.0),
    ).astype(BF16)
    grad_logits = jnp.where(lanes_of(rows, LANES) < experts, side, 0.0)
    logit_high = grad_logits.astype(BF16)
    logit_low = (grad_logits - logit_high.astype(F32)).astype(BF16)
    router = weight_ref[:, inner + LANES :]
    partial_ref[...] = (
        dot_nt(grad_queries, weight_ref[:, :inner])
        + dot_nt(logit_high, router)
        + dot_nt(logit_low, router)
    ).astype(BF16)
    hidden_t = hidden_ref[...].T
    acc_query[...] += dot_nn(hidden_t, grad_queries)
    acc_router[...] += dot_nn(hidden_t, logit_high) + dot_nn(hidden_t, logit_low)

    @pl.when(step == last)
    def _():
        d_query_ref[...] = acc_query[...].astype(BF16)
        d_router_ref[...] = acc_router[...]


def last_kernel(
    experts,
    head,
    parts,
    core_ref,
    x_ref,
    hidden_ref,
    partial_ref,
    grad_mid_ref,
    query_ref,
    router_ref,
    weight_ref,
    *rest,
):
    pieces = rest[: len(parts)]
    grad_in_ref, *leaving, acc_kv, acc_vec, summed_ref = rest[len(parts) :]
    step, last = pl.program_id(0), pl.num_programs(0) - 1
    rows, width = x_ref.shape
    inner = experts * head

    @pl.when(step == 0)
    def _():
        acc_kv[...] = jnp.zeros_like(acc_kv)
        acc_vec[...] = jnp.zeros_like(acc_vec)

    for piece, (low, high) in zip(pieces, parts):

        @pl.when((step >= low) & (step < high))
        def _():
            per_step = piece.shape[1] // (high - low)
            base = (step - low) * per_step
            summed = piece[0, pl.ds(base, per_step)].astype(F32)
            for at in range(1, piece.shape[0]):
                summed = summed + piece[at, pl.ds(base, per_step)].astype(F32)
            summed_ref[...] = summed.astype(BF16).reshape(summed_ref.shape)

    gain = rows_of(weight_ref[:, inner + LANES :], (experts,))[0:1]
    normed, inv_dev = normalize(x_ref[...].astype(F32))
    grad_keyvals = summed_ref[...]
    grad_hidden = partial_ref[...].astype(F32) + dot_nt(grad_keyvals, weight_ref[:, inner : inner + LANES])
    grad_in_ref[...] = grad_mid_ref[...].astype(F32) + norm_back(grad_hidden, gain, normed, inv_dev)
    hidden_t = hidden_ref[...].T
    acc_kv[...] += dot_nn(hidden_t, grad_keyvals)
    acc_vec[experts : experts + 1] += jnp.sum(grad_hidden * normed, 0, keepdims=True)
    acc_vec[experts + 1 : experts + 2] += jnp.sum(grad_hidden, 0, keepdims=True)

    @pl.when(step == last)
    def _():
        extra = router_ref[...] + acc_vec[...].T
        for value, low in (
            (query_ref[...], 0),
            (acc_kv[...].astype(BF16), inner),
            (extra.astype(BF16), inner + LANES),
        ):
            columns = slice(low, low + value.shape[1])
            if len(leaving) == 1:
                leaving[0][:, columns] = value
                continue
            keep_ref, send_ref = leaving
            planes, seqs, own_rows = keep_ref.shape[:3]
            by_core = value.reshape(planes, 2, seqs, own_rows, value.shape[1])
            other = core_ref[0] == 1
            keep_ref[:, :, :, columns] = jnp.where(other, by_core[:, 1], by_core[:, 0])
            send_ref[:, :, :, columns] = jnp.where(other, by_core[:, 0], by_core[:, 1])


def finish_second_kernel(total_ref, down_ref, up_ref, out_ref, up_bias_ref, *vector_refs):
    ff_rows, width = down_ref.shape
    own_rows, ff = up_ref.shape
    blocks = ff // width
    down_ref[...] = total_ref[:ff_rows].astype(F32)
    for at in range(blocks):
        low = ff_rows + at * own_rows
        up_ref[:, at * width : (at + 1) * width] = total_ref[low : low + own_rows].astype(F32)
    low = ff_rows + blocks * own_rows
    out_ref[...] = total_ref[low : low + own_rows].astype(F32)
    turned = total_ref[low + own_rows :].astype(F32).T
    up_bias_ref[...] = jnp.concatenate([turned[at * LANES + 8] for at in range(blocks)], 0)
    for at, ref in enumerate(vector_refs):
        ref[...] = turned[at]


def finish_first_kernel(count, *refs):
    query_ref, kv_ref, router_ref, gain_ref, bias_ref = refs[count:]
    total = refs[0][...].astype(F32)
    for ref in refs[1:count]:
        total = total + ref[...].astype(F32)
    inner, pair, experts = query_ref.shape[1], kv_ref.shape[1], router_ref.shape[0]
    query_ref[...] = total[:, :inner]
    kv_ref[...] = total[:, inner : inner + pair]
    turned = total[:, inner + LANES :].T
    router_ref[...] = turned[:experts]
    gain_ref[...] = turned[experts]
    bias_ref[...] = turned[experts + 1]


def whole_spec(shape):
    zeros = (0,) * len(shape)
    return pl.BlockSpec(shape, lambda *_: zeros, pipeline_mode=pl.Buffered(1))


def row_spec(rows, columns):
    return pl.BlockSpec((rows, columns), lambda i, *_: (i, 0))


def pair_spec(rows):
    return pl.BlockSpec((2, rows, LANES), lambda i, *_: (0, i, 0))


def swapped(value, axis, mask):
    count = lax.axis_size(axis)
    return lax.ppermute(value, axis, [(at, at ^ mask) for at in range(count)])


def passed_along(value, axis, steps):
    count = lax.axis_size(axis)
    leading, last = (max(0, -steps), min(count, count - steps))
    return lax.ppermute(value, axis, [(source, source + steps) for source in range(leading, last)])


def spread(shard):
    dp, seq = lax.axis_size("dp"), lax.axis_size("seq")
    along = [shard] + [swapped(shard, "dp", 2 * at) for at in range(1, dp // 2)]
    held = jnp.stack(along)
    held = jnp.stack([held] + [swapped(held, "seq", at) for at in range(1, seq)])
    return held, swapped(held, "dp", 1)


def at_index(value, index, dim):
    return lax.dynamic_index_in_dim(value, index, dim, keepdims=False)


def core_halved(value):
    core = lax.axis_index("dp") % 2
    return at_index(value, core, 1) + swapped(at_index(value, 1 - core, 1), "dp", 1)


def summed_direct(value, dim, axis, scale):
    me = lax.axis_index(axis) // scale
    total = at_index(value, me, dim).astype(F32)
    for at in range(1, value.shape[dim]):
        total = total + swapped(at_index(value, me ^ at, dim), axis, at * scale).astype(F32)
    return total


def together(*values):
    return lax.optimization_barrier(values)


def on_device(
    block_in,
    routes,
    segments,
    cotangent,
    ln1_gain,
    ln1_bias,
    query_weight,
    kv_weight,
    router_weight,
    out_weight,
    ln2_gain,
    ln2_bias,
    up_weight,
    up_bias,
    down_weight,
    down_bias,
):
    micro_count, seq_count, local_len, width = block_in.shape
    full_len = segments.shape[2]
    experts = router_weight.shape[1]
    head = kv_weight.shape[1] // 2
    inner = experts * head
    ff = up_weight.shape[1]
    dp, shards = lax.axis_size("dp"), lax.axis_size("seq")
    devices = dp * shards
    own_rows, ff_rows, blocks = width // devices, ff // devices, ff // width
    aligned = own_rows % 16 == 0
    batch = micro_count * seq_count
    rows_all = batch * local_len
    tile = seq_count * local_len
    longest = full_len * 3 // 4
    reach = min(shards, (longest - 2) // local_len + 2)
    own_shard = lax.axis_index("seq")
    start_pos = own_shard * local_len

    def padded(value, columns):
        return jnp.pad(value, ((0, 0), (0, columns - value.shape[1])))

    a_cols = inner + 2 * LANES
    if aligned:
        packed_a, packed_b = pl.pallas_call(
            pack_kernel,
            out_shape=[
                jax.ShapeDtypeStruct((own_rows, a_cols), BF16),
                jax.ShapeDtypeStruct((ff_rows + (blocks + 1) * own_rows, width), BF16),
            ],
            compiler_params=call_params(),
            name="pack",
        )(
            query_weight,
            kv_weight,
            router_weight.T,
            down_weight,
            up_weight,
            out_weight,
            ln1_gain,
            ln1_bias,
            ln2_gain,
            ln2_bias,
            down_bias,
            up_bias,
        )
    else:
        rows = jnp.concatenate([ln1_gain, ln1_bias, ln2_gain, ln2_bias, down_bias, up_bias])
        rows = rows.reshape(5 + blocks, own_rows)
        extra = padded(jnp.concatenate([router_weight, rows.T], 1), LANES)
        packed_a = jnp.concatenate([query_weight, kv_weight, extra], 1)
        packed_b = jnp.concatenate(
            [down_weight]
            + [up_weight[:, at * width : (at + 1) * width] for at in range(blocks)]
            + [out_weight],
            0,
        )
    mine_a, mate_a = spread(packed_a)
    place = jnp.stack(
        [lax.axis_index("dp") // 2, lax.axis_index("dp") % 2, lax.axis_index("seq")]
    ).astype(jnp.int32)
    place_a = place
    if not aligned:
        held = jnp.moveaxis(jnp.stack([mine_a, mate_a]), 2, 0)
        for dim, at in ((0, 0), (1, 1), (2, 2)):
            order = jnp.arange(held.shape[dim], dtype=jnp.int32) ^ place[at]
            held = jnp.take(held, order, axis=dim)
        held = held.reshape(2, width // 2, a_cols)
        mine_a, mate_a = held[:1, None], held[1:, None]
        place_a = jnp.zeros_like(place)
    group_b = lax.all_gather(packed_b, ("dp", "seq"), axis=0, tiled=False)
    up_at, out_at = ff_rows, ff_rows + blocks * own_rows
    if aligned:
        weights = group_b
    else:
        up_all = group_b[:, up_at:out_at].reshape(devices, blocks, own_rows, width)
        weights = jnp.concatenate(
            [
                group_b[:, :ff_rows].reshape(ff, width),
                jnp.moveaxis(up_all, 0, 1).reshape(ff, width),
                group_b[:, out_at:].reshape(width, width),
            ],
            0,
        )[None]

    tokens = block_in.reshape(rows_all, width)
    grad_out = cotangent.reshape(rows_all, width)
    route_rows = routes.reshape(rows_all, 2)

    seg_rows = segments.reshape(batch, full_len)
    seg_local = lax.dynamic_slice_in_dim(seg_rows, start_pos, local_len, 1)
    doc_start = jnp.sum(
        (seg_rows[:, None, :] < seg_local[:, :, None]).astype(jnp.int32), -1, dtype=jnp.int32
    )
    doc_start = jnp.maximum(doc_start - (own_shard - (reach - 1)) * local_len, 0)
    bounds = jnp.concatenate([doc_start[:, 0], own_shard.reshape(1).astype(jnp.int32)])
    starts = doc_start.reshape(batch, 1, local_len)

    steps = micro_count
    hidden, keyvals, group_a = pl.pallas_call(
        functools.partial(keyval_kernel, experts, head),
        grid=(steps,),
        in_specs=[
            pl.BlockSpec(memory_space=pltpu.SMEM),
            row_spec(tile, width),
            whole_spec(mine_a.shape),
            whole_spec(mate_a.shape),
        ],
        out_specs=[row_spec(tile, width), row_spec(tile, LANES), whole_spec((width, a_cols))],
        out_shape=[
            jax.ShapeDtypeStruct((rows_all, width), BF16),
            jax.ShapeDtypeStruct((rows_all, LANES), BF16),
            jax.ShapeDtypeStruct((width, a_cols), BF16),
        ],
        scratch_shapes=[
            pltpu.VMEM((2 * mine_a.shape[0] * mine_a.shape[1],) + mine_a.shape[2:], BF16)
        ],
        compiler_params=call_params(),
        cost_estimate=cost(2 * rows_all * width * LANES, rows_all * width * 4),
        name="keyval",
    )(place_a, tokens, mine_a, mate_a)

    own_pieces = keyvals.reshape(batch, local_len, LANES)
    pieces = [own_pieces] + [passed_along(own_pieces, "seq", back) for back in range(1, reach)]
    pieces = pieces[::-1]

    queries, gates = pl.pallas_call(
        functools.partial(query_kernel, experts, head),
        grid=(steps,),
        in_specs=[row_spec(tile, width), row_spec(tile, 2), whole_spec((width, a_cols))],
        out_specs=[pair_spec(tile), row_spec(tile, LANES)],
        out_shape=[
            jax.ShapeDtypeStruct((2, rows_all, LANES), BF16),
            jax.ShapeDtypeStruct((rows_all, LANES), F32),
        ],
        compiler_params=call_params(),
        cost_estimate=cost(2 * rows_all * width * (a_cols + 512), rows_all * width * 4),
        name="query",
    )(hidden, route_rows, group_a)

    columns = group_a[:, inner + LANES :].astype(F32)
    small = jnp.pad(columns[:, experts + 2 : experts + 5].T, ((0, 4), (0, ff - width)))
    up_row = columns[:, experts + 5 : experts + 5 + blocks]
    up_row = jnp.swapaxes(up_row.reshape(devices, own_rows, blocks), 1, 2).reshape(1, ff)
    vectors = jnp.concatenate([up_row, small], 0)

    piece_spec = pl.BlockSpec((1, local_len, LANES), lambda b, *_: (b, 0, 0))
    q_spec = pl.BlockSpec((2, local_len, LANES), lambda b, *_: (0, b, 0))
    start_spec = pl.BlockSpec((1, 1, local_len), lambda b, *_: (b, 0, 0))
    lse_spec = pl.BlockSpec((1, 2, local_len), lambda b, *_: (b, 0, 0))
    pairs = rows_all * full_len
    mixed, lse = pl.pallas_call(
        functools.partial(attend_kernel, reach, head),
        grid_spec=pltpu.PrefetchScalarGridSpec(
            num_scalar_prefetch=1,
            grid=(batch,),
            in_specs=[q_spec, start_spec] + [piece_spec] * reach,
            out_specs=[q_spec, lse_spec],
            scratch_shapes=[
                pltpu.VMEM((reach, local_len, LANES), BF16),
                pltpu.VMEM((2, local_len), F32),
                pltpu.VMEM((2, local_len), F32),
                pltpu.VMEM((2, head, local_len), F32),
            ],
        ),
        out_shape=[
            jax.ShapeDtypeStruct((2, rows_all, LANES), F32),
            jax.ShapeDtypeStruct((batch, 2, local_len), F32),
        ],
        compiler_params=call_params(),
        cost_estimate=cost(4 * pairs * LANES, rows_all * LANES * 16, pairs),
        name="attend",
    )(bounds, queries, starts, *pieces)

    grad_rows = ff_rows + (blocks + 2) * own_rows if aligned else ff + (blocks + 2) * width
    core_index = (lax.axis_index("dp") % 2).reshape(1).astype(jnp.int32)
    if aligned:
        leaving = [(dp // 2, shards, grad_rows, width)] * 2
    else:
        leaving = [(1, grad_rows, width)]
    block_out, grad_mid, grad_mixed, side, *grads_b = pl.pallas_call(
        functools.partial(mid_kernel, experts, head),
        grid=(steps,),
        in_specs=[
            row_spec(tile, width),
            row_spec(tile, width),
            row_spec(tile, LANES),
            pair_spec(tile),
            whole_spec((8, ff)),
            pl.BlockSpec(memory_space=pltpu.SMEM),
        ]
        + [pl.BlockSpec(memory_space=pl.ANY)],
        out_specs=[
            row_spec(tile, width),
            row_spec(tile, width),
            pair_spec(tile),
            row_spec(tile, LANES),
        ]
        + [pl.BlockSpec(memory_space=pl.ANY)] * len(leaving),
        out_shape=[
            jax.ShapeDtypeStruct((rows_all, width), BF16),
            jax.ShapeDtypeStruct((rows_all, width), BF16),
            jax.ShapeDtypeStruct((2, rows_all, LANES), BF16),
            jax.ShapeDtypeStruct((rows_all, LANES), F32),
        ]
        + [jax.ShapeDtypeStruct(shape, BF16) for shape in leaving],
        scratch_shapes=mid_scratch(rows_all, width, ff, weights.shape, leaving),
        compiler_params=call_params(),
        cost_estimate=cost(6 * rows_all * width * (2 * ff + width), rows_all * width * 16),
        name="mid",
    )(tokens, grad_out, gates, mixed, vectors, core_index, weights)

    if not aligned:
        parts = grads_b[0][0]
        down_part = parts[:ff].reshape(devices, ff_rows, width)
        up_part = parts[ff : 2 * ff].reshape(blocks, devices, own_rows, width)
        up_part = jnp.moveaxis(up_part, 0, 1).reshape(devices, blocks * own_rows, width)
        out_part = parts[2 * ff : 2 * ff + width].reshape(devices, own_rows, width)
        tail = parts[2 * ff + width :]
        rows_up = tail.reshape(width, blocks, LANES)[:, :, 8].T.reshape(devices, own_rows, blocks)
        rows_vec = tail[:, :8].reshape(devices, own_rows, 8)
        rows_up = jnp.moveaxis(rows_up.reshape(devices, blocks, own_rows), 1, 2)
        tail = jnp.zeros((devices, own_rows, blocks, LANES), BF16)
        tail = tail.at[:, :, :, 8].set(rows_up).at[:, :, 0, :8].set(rows_vec)
        tail = tail.reshape(devices, own_rows, width)
        packed = jnp.concatenate([down_part, up_part, out_part, tail], 1)
        packed = packed.reshape((dp // 2, 2, shards) + packed.shape[1:])
        grads_b = [at_index(packed, core_index[0], 1), at_index(packed, 1 - core_index[0], 1)]

    keep, send = grads_b
    bits, z_bits = shards.bit_length() - 1, (dp // 2).bit_length() - 1
    along_x = [("seq", 1 << at) for at in range(bits // 2)]
    along_y = [("seq", 1 << at) for at in range(bits // 2, bits)]
    along_z = [("dp", 2 << at) for at in range(z_bits)]
    near, far = along_z[:1], along_z[1:]
    dims = along_z[::-1] + along_y[::-1] + along_x[::-1]
    orders = [along_x + along_y + near, along_y + near + along_x, near + along_x + along_y]
    third = -(-keep.shape[2] // 24) * 8 if keep.shape[2] % 8 == 0 else -(-keep.shape[2] // 3)
    cuts = [0, third, 2 * third, keep.shape[2]]
    held = keep + swapped(send, "dp", 1)
    held = held.reshape((2,) * len(dims) + held.shape[2:])
    parts = [
        (held[..., low:high, :], dims, order)
        for low, high, order in zip(cuts[:-1], cuts[1:], orders)
    ]

    def send_parts(parts):
        stays, arrives = [], []
        for value, left, order in parts:
            axis, mask = order[0]
            dim, bit = left.index(order[0]), (lax.axis_index(axis) // mask) % 2
            left = left[:dim] + left[dim + 1 :]
            stays.append((at_index(value, bit, dim), left, order[1:]))
            arrives.append(swapped(at_index(value, 1 - bit, dim), axis, mask))
        return stays, arrives

    def behind(parts, other):
        *values, other = together(*[value for value, _, _ in parts], other)
        return [(value,) + part[1:] for value, part in zip(values, parts)], other

    def joined(parts, arrives):
        return [(part[0] + piece,) + part[1:] for part, piece in zip(parts, arrives)]

    leave_spec = pl.BlockSpec((shards, 1, local_len, LANES), lambda b, *_: (0, b, 0, 0))

    parts, arrives = send_parts(parts)
    parts, bounds_now = behind(parts, bounds)
    grad_queries = None
    returned = []
    splits = [0, max(1, micro_count - 1), micro_count] if micro_count > 1 else [0, 1]
    for micro, stop in zip(splits[:-1], splits[1:]):
        count = (stop - micro) * seq_count

        def at_micro(block, dims, base=micro * seq_count):
            if dims == "b":
                return pl.BlockSpec(block, lambda b, *_: (base + b, 0, 0))
            return pl.BlockSpec(block, lambda b, *_: (0, base + b, 0))

        q_at = at_micro((2, local_len, LANES), "q")
        in_specs = [
            q_at,
            q_at,
            pl.BlockSpec(
                (local_len, LANES), lambda b, *_, base=micro * seq_count: (base + b, 0)
            ),
            at_micro((1, 2, local_len), "b"),
            at_micro((1, 1, local_len), "b"),
        ]
        in_specs += [at_micro((1, local_len, LANES), "b")] * reach
        operands = in_hbm(queries, grad_mixed, side, lse, starts, *pieces)
        aliases = {}
        if micro:
            in_specs.append(pl.BlockSpec(memory_space=pl.ANY))
            operands.append(grad_queries)
            aliases = {len(operands): 0}
        grad_queries, leave = pl.pallas_call(
            functools.partial(
                attend_back_kernel, reach, head, micro * seq_count, int(micro > 0)
            ),
            grid_spec=pltpu.PrefetchScalarGridSpec(
                num_scalar_prefetch=1,
                grid=(count,),
                in_specs=in_specs,
                out_specs=[q_at, leave_spec],
                scratch_shapes=[
                    pltpu.VMEM((reach, local_len, LANES), BF16),
                    pltpu.VMEM((reach, local_len, LANES), F32),
                    pltpu.VMEM((2, head, local_len), F32),
                ],
            ),
            out_shape=[
                pltpu.HBM((2, rows_all, LANES), BF16),
                jax.ShapeDtypeStruct((shards, count, local_len, LANES), BF16),
            ],
            input_output_aliases=aliases,
            compiler_params=call_params(28),
            cost_estimate=cost(
                10 * pairs * LANES * count // batch,
                count * local_len * LANES * 32,
                pairs * count // batch,
            ),
            name="attend_back",
        )(bounds_now, *operands)
        returned.append(lax.all_to_all(leave, "seq", 0, 0, tiled=True))
        if parts[0][2]:
            *arrives, grad_queries = together(*arrives, grad_queries)
            parts, arrives = send_parts(joined(parts, arrives))
            if stop < micro_count:
                parts, bounds_now = behind(parts, bounds)
            else:
                parts, side = behind(parts, side)

    partial_hidden, d_query, d_router = pl.pallas_call(
        functools.partial(query_grad_kernel, experts, head),
        grid=(steps,),
        in_specs=[
            row_spec(tile, width),
            pair_spec(tile),
            row_spec(tile, LANES),
            whole_spec((width, a_cols)),
        ],
        out_specs=[
            row_spec(tile, width),
            whole_spec((width, inner)),
            whole_spec((width, LANES)),
        ],
        out_shape=[
            jax.ShapeDtypeStruct((rows_all, width), BF16),
            pltpu.HBM((width, inner), BF16),
            pltpu.HBM((width, LANES), F32),
        ],
        scratch_shapes=[pltpu.VMEM((width, inner), F32), pltpu.VMEM((width, LANES), F32)],
        compiler_params=call_params(28),
        cost_estimate=cost(4 * rows_all * width * a_cols, rows_all * width * 12),
        name="query_grad",
    )(*in_hbm(hidden, grad_queries, side, group_a))
    *arrives, d_router = together(*arrives, d_router)
    parts = joined(parts, arrives)
    while parts[0][2]:
        parts = joined(*send_parts(parts))
    whole = jnp.concatenate([value for value, _, _ in parts], -2)
    parts, arrives = send_parts([(whole, parts[0][1], far)])
    parts, d_router = behind(parts, d_router)
    if aligned:
        small_shapes = [(dp // 2, shards, own_rows, a_cols)] * 2
    else:
        small_shapes = [(width, a_cols)]
    grad_in, *small = pl.pallas_call(
        functools.partial(last_kernel, experts, head, tuple(zip(splits[:-1], splits[1:]))),
        grid=(steps,),
        in_specs=[
            pl.BlockSpec(memory_space=pltpu.SMEM),
            row_spec(tile, width),
            row_spec(tile, width),
            row_spec(tile, width),
            row_spec(tile, width),
            whole_spec((width, inner)),
            whole_spec((width, LANES)),
            whole_spec((width, a_cols)),
        ]
        + [whole_spec(piece.shape) for piece in returned],
        out_specs=[row_spec(tile, width)] + [whole_spec(shape) for shape in small_shapes],
        out_shape=[
            jax.ShapeDtypeStruct((rows_all, width), F32),
        ]
        + [jax.ShapeDtypeStruct(shape, BF16) for shape in small_shapes],
        scratch_shapes=[
            pltpu.VMEM((width, LANES), F32),
            pltpu.VMEM((LANES, width), F32),
            pltpu.VMEM((tile, LANES), BF16),
        ],
        compiler_params=call_params(28),
        cost_estimate=cost(4 * rows_all * width * LANES, rows_all * width * 16),
        name="last",
    )(
        core_index,
        *in_hbm(tokens, hidden),
        partial_hidden,
        *in_hbm(grad_mid, d_query, d_router, group_a),
        *returned,
    )
    if not aligned:
        by_core = small[0].reshape(dp // 2, 2, shards, own_rows, a_cols)
        small = [at_index(by_core, core_index[0], 1), at_index(by_core, 1 - core_index[0], 1)]
    keep_small, send_small = small
    *arrives, send_small = together(*arrives, send_small)
    parts = joined(parts, arrives)
    while parts[0][2]:
        parts = joined(*send_parts(parts))
    own_b = parts[0][0]
    held = keep_small + swapped(send_small, "dp", 1)
    held = summed_direct(held, 1, "seq", 1).astype(BF16)
    z_me = lax.axis_index("dp") // 2
    ends = [at_index(held, z_me, 0)]
    ends += [swapped(at_index(held, z_me ^ at, 0), "dp", 2 * at) for at in range(1, dp // 2)]

    out_at_b, tail_at = ff_rows + blocks * own_rows, ff_rows + (blocks + 1) * own_rows
    if aligned:
        vector_shape = jax.ShapeDtypeStruct((own_rows,), F32)
        grad_down, grad_up, grad_out_weight, grad_up_bias, *second_vectors = pl.pallas_call(
            finish_second_kernel,
            out_shape=[
                jax.ShapeDtypeStruct((ff_rows, width), F32),
                jax.ShapeDtypeStruct((own_rows, ff), F32),
                jax.ShapeDtypeStruct((own_rows, width), F32),
                jax.ShapeDtypeStruct((ff_rows,), F32),
            ]
            + [vector_shape] * 3,
            compiler_params=call_params(),
            name="finish_second",
        )(own_b)
        grad_query, grad_kv, grad_router, *first_vectors = pl.pallas_call(
            functools.partial(finish_first_kernel, len(ends)),
            out_shape=[
                jax.ShapeDtypeStruct((own_rows, inner), F32),
                jax.ShapeDtypeStruct((own_rows, 2 * head), F32),
                jax.ShapeDtypeStruct((experts, own_rows), F32),
            ]
            + [vector_shape] * 2,
            compiler_params=call_params(),
            name="finish_first",
        )(*ends)
        grad_router = grad_router.T
    else:
        own_b = own_b.astype(F32)
        total = sum([piece.astype(F32) for piece in ends])
        ends = own_b[tail_at:]
        grad_up = jnp.concatenate(
            [
                own_b[ff_rows + at * own_rows : ff_rows + (at + 1) * own_rows]
                for at in range(blocks)
            ],
            1,
        )
        grad_up_bias = jnp.concatenate([ends[:, at * LANES + 8] for at in range(blocks)])
        grad_down, grad_out_weight = own_b[:ff_rows], own_b[out_at_b:tail_at]
        second_vectors = [ends[:, at] for at in range(3)]
        grad_query, grad_kv = total[:, :inner], total[:, inner : inner + 2 * head]
        total = total[:, inner + LANES :]
        grad_router = total[:, :experts]
        first_vectors = [total[:, experts], total[:, experts + 1]]
    return (
        block_out.reshape(block_in.shape),
        grad_in.reshape(block_in.shape),
        first_vectors[0],
        first_vectors[1],
        grad_query,
        grad_kv,
        grad_router,
        grad_out_weight,
        second_vectors[0],
        second_vectors[1],
        grad_up,
        grad_up_bias,
        grad_down,
        second_vectors[2],
    )


def solution(mesh):
    rows = P(("dp", "seq"), None)
    vector = P(("dp", "seq"))
    data = P(None, "dp", "seq", None)
    weights = (
        vector,
        vector,
        rows,
        rows,
        rows,
        rows,
        vector,
        vector,
        rows,
        vector,
        rows,
        vector,
    )
    return jax.shard_map(
        on_device,
        mesh=mesh,
        in_specs=(data, data, P(None, "dp", None), data) + weights,
        out_specs=(data, data) + weights,
        check_vma=False,
    )
```

```python
import functools

import jax
import jax.numpy as jnp
from jax import lax
from jax.experimental import pallas as pl
from jax.experimental.pallas import tpu as pltpu
from jax.sharding import PartitionSpec as P

EPS = 1e-05
LANES = 128
MIB = 1024 * 1024
BF16 = jnp.bfloat16
F32 = jnp.float32


def call_params(mib=56):
    return pltpu.CompilerParams(vmem_limit_bytes=mib * MIB)


def in_hbm(*values):
    return [pltpu.with_memory_space_constraint(value, pltpu.HBM) for value in values]


def cost(flops, bytes_accessed, transcendentals=0):
    return pl.CostEstimate(
        flops=int(flops), bytes_accessed=int(bytes_accessed), transcendentals=int(transcendentals)
    )


def dot_nn(left, right):
    return lax.dot_general(left, right, (((1,), (0,)), ((), ())), preferred_element_type=F32)


def dot_nt(left, right):
    return lax.dot_general(left, right, (((1,), (1,)), ((), ())), preferred_element_type=F32)


def lanes_of(rows, width):
    return lax.broadcasted_iota(jnp.int32, (rows, width), 1)


def fold_matrix(width, head, shift):
    source = lax.broadcasted_iota(jnp.int32, (width, LANES), 0)
    target = lax.broadcasted_iota(jnp.int32, (width, LANES), 1)
    return jnp.where(target == shift + lax.rem(source, head), 1.0, 0.0).astype(BF16)


def unfold_matrix(width, head, shift):
    source = lax.broadcasted_iota(jnp.int32, (LANES, width), 1)
    target = lax.broadcasted_iota(jnp.int32, (LANES, width), 0)
    return jnp.where(target == shift + lax.rem(source, head), 1.0, 0.0).astype(BF16)


def rows_of(columns, picked):
    row = lax.broadcasted_iota(jnp.int32, (8, LANES), 0)
    lane = lax.broadcasted_iota(jnp.int32, (8, LANES), 1)
    chosen = jnp.zeros((8, LANES), F32)
    for at, column in enumerate(picked):
        chosen = jnp.where((row == at) & (lane == column), 1.0, chosen)
    return dot_nt(chosen.astype(BF16), columns)


def normalize(values):
    centered = values - jnp.mean(values, -1, keepdims=True)
    inv_dev = lax.rsqrt(jnp.mean(centered * centered, -1, keepdims=True) + EPS)
    return centered * inv_dev, inv_dev


def norm_back(grad, gain, normed, inv_dev):
    scaled = grad * gain
    return inv_dev * (
        scaled
        - jnp.mean(scaled, -1, keepdims=True)
        - normed * jnp.mean(scaled * normed, -1, keepdims=True)
    )


def pack_kernel(query_ref, kv_ref, router_ref, down_ref, up_ref, out_ref, *rest):
    *vector_refs, up_bias_ref, first_ref, second_ref = rest
    own_rows, width = query_ref.shape
    first_ref[:, :width] = query_ref[...]
    first_ref[:, width : width + LANES] = kv_ref[...]
    rows = [router_ref[...].astype(F32)]
    rows += [ref[...].astype(F32).reshape(1, own_rows) for ref in vector_refs]
    bias = up_bias_ref[...].astype(F32).reshape(1, up_bias_ref.shape[0])
    rows += [
        bias[:, at * own_rows : (at + 1) * own_rows] for at in range(bias.shape[1] // own_rows)
    ]
    count = router_ref.shape[0] + len(rows) - 1
    rows.append(jnp.zeros((32 - count, own_rows), F32))
    rows = jnp.concatenate(rows, 0).astype(BF16)
    row = lax.broadcasted_iota(jnp.int32, (32, LANES), 0)
    lane = lax.broadcasted_iota(jnp.int32, (32, LANES), 1)
    chosen = jnp.where(lane == row, 1.0, 0.0).astype(BF16)
    turned = lax.dot_general(rows, chosen, (((0,), (0,)), ((), ())), preferred_element_type=F32)
    first_ref[:, width + LANES :] = turned.astype(BF16)
    ff_rows = down_ref.shape[0]
    second_ref[:ff_rows] = down_ref[...]
    blocks = up_ref.shape[1] // width
    for at in range(blocks):
        low = ff_rows + at * own_rows
        second_ref[low : low + own_rows] = up_ref[:, at * width : (at + 1) * width]
    second_ref[ff_rows + blocks * own_rows :] = out_ref[...]


def in_order(place_ref, parts, put):
    z_me, core_me, seq_me = place_ref[0], place_ref[1], place_ref[2]
    for core, part in enumerate(parts):
        for seq in range(part.shape[0]):
            for z in range(part.shape[1]):
                dp_at = (z_me ^ z) * 2 + (core_me ^ core)
                put(dp_at * part.shape[0] + (seq_me ^ seq), part[seq, z])


def keyval_kernel(experts, head, place_ref, x_ref, mine_ref, mate_ref, *rest):
    hidden_ref, kv_ref, weight_ref, blocks_ref = rest

    @pl.when(pl.program_id(0) == 0)
    def _():
        def put(device, block):
            blocks_ref[device] = block

        in_order(place_ref, (mine_ref, mate_ref), put)
        weight_ref[...] = blocks_ref[...].reshape(weight_ref.shape)

    inner = experts * head
    vectors = rows_of(weight_ref[:, inner + LANES :], (experts, experts + 1))
    normed, _ = normalize(x_ref[...].astype(F32))
    hidden = (normed * vectors[0:1] + vectors[1:2]).astype(BF16)
    hidden_ref[...] = hidden
    kv_ref[...] = dot_nn(hidden, weight_ref[:, inner : inner + LANES]).astype(BF16)


def query_kernel(experts, head, hidden_ref, routes_ref, weight_ref, q_ref, gate_ref):
    inner = experts * head
    hidden = hidden_ref[...]
    rows = hidden.shape[0]
    logits = dot_nn(hidden, weight_ref[:, inner + LANES :])
    lane = lanes_of(rows, LANES)
    first, second = routes_ref[:, 0:1], routes_ref[:, 1:2]
    logit_one = jnp.sum(jnp.where(lane == first, logits, 0.0), -1, keepdims=True)
    logit_two = jnp.sum(jnp.where(lane == second, logits, 0.0), -1, keepdims=True)
    peak = jnp.maximum(logit_one, logit_two)
    exp_one = jnp.exp(logit_one - peak)
    exp_two = jnp.exp(logit_two - peak)
    total = exp_one + exp_two
    gates = jnp.where(lane == 0, exp_one / total, jnp.where(lane == 1, exp_two / total, 0.0))
    gates = jnp.where(lane == 2, first.astype(F32), gates)
    gate_ref[...] = jnp.where(lane == 3, second.astype(F32), gates)
    queries = (dot_nn(hidden, weight_ref[:, :inner]) * (head**-0.5)).astype(BF16)
    owner = lax.div(lanes_of(rows, inner), head)
    fold = fold_matrix(inner, head, 0)
    zero = jnp.zeros_like(queries)
    q_ref[0] = dot_nn(jnp.where(owner == first, queries, zero), fold).astype(BF16)
    q_ref[1] = dot_nn(jnp.where(owner == second, queries, zero), fold).astype(BF16)


def masked(scores, start, key_at, query_at=None):
    keys = key_at + lax.broadcasted_iota(jnp.int32, scores.shape, 0)
    seen = keys >= start
    if query_at is not None:
        lane = lax.broadcasted_iota(jnp.int32, (1, scores.shape[1]), 1)
        seen = seen & (keys <= query_at + lax.rem(lane, scores.shape[1] // 2))
    return jnp.where(seen, scores, -1e30)


def by_halves(ref):
    half = ref.shape[1] // 2
    return [
        jnp.concatenate([ref[0, at * half : (at + 1) * half], ref[1, at * half : (at + 1) * half]], 0)
        for at in range(2)
    ]


def from_halves(ref, groups):
    half = ref.shape[1] // 2
    for at, group in enumerate(groups):
        ref[0, at * half : (at + 1) * half] = group[:half]
        ref[1, at * half : (at + 1) * half] = group[half:]


def row_halves(row):
    half = row.shape[1] // 2
    return [
        jnp.concatenate([row[:, at * half : (at + 1) * half]] * 2, 1) for at in range(2)
    ]


def over_pieces(step, bounds_ref, seq, reach, local):
    low = jnp.minimum(bounds_ref[seq] // local, reach - 1)

    def body(at, carry):
        step(at)
        return carry

    lax.fori_loop(low, reach - 1, body, 0)


def attend_kernel(reach, head, bounds_ref, q_ref, start_ref, *rest):
    pieces = rest[:reach]
    mixed_ref, lse_ref, kv_buf, peak_ref, total_ref, acc_ref = rest[reach:]
    seq = pl.program_id(0)
    local = pieces[0].shape[1]
    half = local // 2
    for at in range(reach - 1):
        kv_buf[at] = pieces[at][0]
    queries = by_halves(q_ref)
    starts = row_halves(start_ref[0])
    peak_ref[...] = jnp.full_like(peak_ref, -1e30)
    total_ref[...] = jnp.zeros_like(total_ref)
    acc_ref[...] = jnp.zeros_like(acc_ref)

    def turned_values(keyval):
        return keyval.T[head:]

    def accumulate(group, scores, values):
        old = peak_ref[group : group + 1]
        peak = jnp.maximum(old, jnp.max(scores, 0, keepdims=True))
        fade = jnp.exp(old - peak)
        expo = jnp.exp(scores - peak)
        total_ref[group : group + 1] = total_ref[group : group + 1] * fade + jnp.sum(
            expo, 0, keepdims=True
        )
        acc_ref[group] = acc_ref[group] * fade + dot_nn(values, expo.astype(BF16))
        peak_ref[group : group + 1] = peak

    def step(at):
        keyval = kv_buf[at]
        values = turned_values(keyval)
        for group in range(2):
            scores = masked(dot_nt(keyval, queries[group]), starts[group], at * local)
            accumulate(group, scores, values)

    over_pieces(step, bounds_ref, seq, reach, local)
    own = pieces[reach - 1][0]
    own_at = (reach - 1) * local
    values = turned_values(own)
    for group in range(2):
        keys = half * (group + 1)
        scores = masked(
            dot_nt(own[:keys], queries[group]), starts[group], own_at, own_at + group * half
        )
        accumulate(group, scores, values[:, :keys])
    groups = []
    for group in range(2):
        mixed = acc_ref[group] / total_ref[group : group + 1]
        groups.append(jnp.concatenate([jnp.zeros_like(mixed), mixed], 0).T)
    from_halves(mixed_ref, groups)
    lse_ref[0] = peak_ref[...] + jnp.log(total_ref[...])


def summed_by(values, chosen):
    matrix = jnp.where(chosen, 1.0, 0.0).astype(BF16)
    high = values.astype(BF16)
    low = (values - high.astype(F32)).astype(BF16)
    return dot_nn(high, matrix) + dot_nn(low, matrix)


def mid_scratch(rows_all, width, ff, weights, leaving):
    return (
        [pltpu.VMEM((rows_all, ff), BF16)] * 2
        + [pltpu.VMEM((width, rows_all), BF16)] * 3
        + [pltpu.VMEM((rows_all, width), BF16)]
        + [pltpu.VMEM((LANES, width), F32), pltpu.VMEM((LANES, ff), F32)]
        + [pltpu.VMEM(weights, BF16)]
        + [pltpu.VMEM(shape, BF16) for shape in leaving]
        + [pltpu.SemaphoreType.DMA((3,)), pltpu.SemaphoreType.DMA((2 + 4 * ff // width,))]
    )


def mid_kernel(
    experts,
    head,
    x_ref,
    dy_ref,
    gate_ref,
    mixed_ref,
    vector_ref,
    core_ref,
    weight_ref,
    out_ref,
    grad_mid_ref,
    grad_mixed_ref,
    side_ref,
    *rest,
):
    owners = weight_ref.shape[0]
    count = 2 if owners > 1 else 1
    leaving, rest = rest[:count], rest[count:]
    active_ref, grad_ref, dy_t_ref, second_t_ref, routed_t_ref, att_ref = rest[:6]
    acc_vec, acc_upb, kept_ref = rest[6:9]
    staged, (in_sems, out_sems) = rest[9 : 9 + count], rest[9 + count :]
    step, last = pl.program_id(0), pl.num_programs(0) - 1
    rows, width = x_ref.shape
    inner = experts * head
    own_rows = width // owners
    ff = active_ref.shape[1]
    ff_rows = ff // owners
    blocks = ff // width
    up_at, out_at = ff_rows, ff_rows + blocks * own_rows

    spans = ((out_at, out_at + own_rows), (0, ff_rows), (up_at, out_at))
    loads = [
        pltpu.make_async_copy(
            weight_ref.at[:, low:high, :], kept_ref.at[:, low:high, :], in_sems.at[at]
        )
        for at, (low, high) in enumerate(spans)
    ]

    @pl.when(step == 0)
    def _():
        for load in loads:
            load.start()
        acc_vec[...] = jnp.zeros_like(acc_vec)
        acc_upb[...] = jnp.zeros_like(acc_upb)
        loads[0].wait()

    gain, shift = vector_ref[1:2, :width], vector_ref[2:3, :width]
    down_bias = vector_ref[3:4, :width]
    gate_one, gate_two = gate_ref[:, 0:1], gate_ref[:, 1:2]
    first, second = gate_ref[:, 2:3].astype(jnp.int32), gate_ref[:, 3:4].astype(jnp.int32)
    owner = lax.div(lanes_of(rows, inner), head)
    unfold = unfold_matrix(inner, head, head)
    fold = fold_matrix(inner, head, head)
    wo = kept_ref[:, out_at : out_at + own_rows, :].reshape(inner, width)
    mixed_one, mixed_two = mixed_ref[0], mixed_ref[1]
    routed_one = dot_nn((gate_one * mixed_one).astype(BF16), unfold)
    routed_two = dot_nn((gate_two * mixed_two).astype(BF16), unfold)
    routed = jnp.where(
        owner == first, routed_one, jnp.where(owner == second, routed_two, 0.0)
    )
    routed = routed.astype(BF16)
    middle = x_ref[...].astype(F32) + dot_nn(routed, wo)
    normed, inv_dev = normalize(middle)
    second_low = (normed * gain + shift).astype(BF16)
    dy = dy_ref[...]
    dy_wide = dy.astype(F32)
    here = pl.ds(pl.multiple_of(step * rows, rows), rows)
    second_t_ref[:, here] = second_low.T
    dy_t_ref[:, here] = dy.T
    routed_t_ref[:, here] = routed.T
    per_block = width // ff_rows if owners > 1 else 1

    @pl.when(step == 0)
    def _():
        loads[1].wait()
        loads[2].wait()

    def down_block(at):
        if owners > 1:
            block = kept_ref[at * per_block : (at + 1) * per_block, :ff_rows, :]
            return block.reshape(width, width)
        return kept_ref[0, at * width : (at + 1) * width, :]

    def up_block(at):
        low = up_at + at * own_rows
        return kept_ref[:, low : low + own_rows, :].reshape(width, width)

    def ahead(at):
        lo = at * width
        pre_act = dot_nn(second_low, up_block(at)) + vector_ref[0:1, lo : lo + width]
        return pre_act, dot_nt(dy, down_block(at)).astype(BF16)

    ready = ahead(0)
    for at in range(blocks):
        lo = at * width
        pre_act, grad_active = ready
        if at + 1 < blocks:
            ready = ahead(at + 1)
        sigma = jax.nn.sigmoid(pre_act)
        active = (pre_act * sigma).astype(BF16)
        slope = sigma * (1.0 + pre_act * (1.0 - sigma))
        grad_low = (grad_active.astype(F32) * slope).astype(BF16)
        active_ref[here, lo : lo + width] = active
        grad_ref[here, lo : lo + width] = grad_low
        acc_upb[8:9, lo : lo + width] += jnp.sum(grad_low.astype(F32), 0, keepdims=True)

    down_all = jnp.concatenate([down_block(at) for at in range(blocks)], 0)
    up_all = jnp.concatenate([up_block(at) for at in range(blocks)], 1)
    out_ref[...] = (middle + down_bias + dot_nn(active_ref[here, :], down_all)).astype(BF16)
    gsec = dot_nt(grad_ref[here, :], up_all)
    acc_vec[0:1] += jnp.sum(gsec * normed, 0, keepdims=True)
    acc_vec[1:2] += jnp.sum(gsec, 0, keepdims=True)
    acc_vec[2:3] += jnp.sum(dy_wide, 0, keepdims=True)
    grad_mid = dy_wide + norm_back(gsec, gain, normed, inv_dev)
    grad_att = grad_mid.astype(BF16)
    grad_mid_ref[...] = grad_att
    att_ref[here, :] = grad_att
    grad_routed = dot_nt(grad_att, wo).astype(BF16)
    zero = jnp.zeros_like(grad_routed)
    picked_one = dot_nn(jnp.where(owner == first, grad_routed, zero), fold)
    picked_two = dot_nn(jnp.where(owner == second, grad_routed, zero), fold)
    grad_mixed_one = (gate_one * picked_one).astype(BF16)
    grad_mixed_two = (gate_two * picked_two).astype(BF16)
    grad_mixed_ref[0] = grad_mixed_one
    grad_mixed_ref[1] = grad_mixed_two
    spread_one = lax.broadcasted_iota(jnp.int32, (2 * LANES, 2 * LANES), 0) // LANES
    spread_two = lax.broadcasted_iota(jnp.int32, (2 * LANES, 2 * LANES), 1) // LANES
    sums = summed_by(
        jnp.concatenate([picked_one * mixed_one, picked_two * mixed_two], 1),
        spread_one == spread_two,
    )
    grad_one, grad_two = sums[:, :LANES], sums[:, LANES:]
    source = lax.broadcasted_iota(jnp.int32, (2 * LANES, LANES), 0) // LANES
    target = lax.broadcasted_iota(jnp.int32, (2 * LANES, LANES), 1)
    inners = summed_by(
        jnp.concatenate(
            [grad_mixed_one.astype(F32) * mixed_one, grad_mixed_two.astype(F32) * mixed_two], 1
        ),
        target == head + source,
    )
    common = gate_one * grad_one + gate_two * grad_two
    lane = lanes_of(rows, LANES)
    side = jnp.where(lane == first, gate_one * (grad_one - common), inners)
    side = jnp.where(lane == second, gate_two * (grad_two - common), side)
    side = jnp.where(lane == head + 2, gate_ref[:, 2:3], side)
    side_ref[...] = jnp.where(lane == head + 3, gate_ref[:, 3:4], side)

    @pl.when(step == last)
    def _():
        leaves = []

        def put(value, columns, row, count, group):
            if owners == 1:
                staged[0][0, row : row + value.shape[0], columns] = value
                return
            seqs = staged[0].shape[1]
            by_core = value.reshape(value.shape[0] // (2 * seqs * count), 2, seqs, count, -1)
            planes = by_core.shape[0]
            other = core_ref[0] == 1
            low, high = by_core[:, 0], by_core[:, 1]
            where = (slice(group * planes, (group + 1) * planes), slice(None), slice(row, row + count))
            staged[0][where + (columns,)] = jnp.where(other, high, low)
            staged[1][where + (columns,)] = jnp.where(other, low, high)

        def leave(where):
            for source, target in zip(staged, leaving):
                copy = pltpu.make_async_copy(
                    source.at[where], target.at[where], out_sems.at[len(leaves)]
                )
                copy.start()
                leaves.append(copy)

        everything = slice(None)

        def weight_block(at, carry):
            columns = pl.ds(pl.multiple_of(at * width, width), width)
            turned = dot_nn(dy_t_ref[...], active_ref[:, columns]).T.astype(BF16)
            straight = dot_nn(second_t_ref[...], grad_ref[:, columns]).astype(BF16)
            low = up_at + at * own_rows
            if owners == 1:
                staged[0][0, pl.ds(at * width, width), :] = turned
                staged[0][0, pl.ds(low, width), :] = straight
                return carry
            seqs = staged[0].shape[1]
            other = core_ref[0] == 1
            for value, rows_each, planes in ((turned, ff_rows, 1), (straight, own_rows, blocks)):
                by_core = value.reshape(-1, 2, seqs, rows_each, width)
                first_half, second_half = by_core[:, 0], by_core[:, 1]
                if planes == 1:
                    count = by_core.shape[0]
                    where = (pl.ds(at * count, count), everything, slice(0, ff_rows))
                else:
                    low = pl.multiple_of(up_at + at * own_rows, own_rows)
                    where = (everything, everything, pl.ds(low, own_rows))
                staged[0][where] = jnp.where(other, second_half, first_half)
                staged[1][where] = jnp.where(other, first_half, second_half)
                for copy in block_copies(at, planes > 1):
                    copy.start()
            return carry

        def block_copies(at, straight):
            count = staged[0].shape[0] // blocks
            if straight:
                low = pl.multiple_of(up_at + at * own_rows, own_rows)
                where = (everything, everything, pl.ds(low, own_rows))
            else:
                where = (pl.ds(at * count, count), everything, slice(0, ff_rows))
            base = 2 + 4 * at + 2 * int(straight)
            return [
                pltpu.make_async_copy(source.at[where], target.at[where], out_sems.at[base + side])
                for side, (source, target) in enumerate(zip(staged, leaving))
            ]

        def block_waits(at, carry):
            for straight in (False, True):
                for copy in block_copies(at, straight):
                    copy.wait()
            return carry

        lax.fori_loop(0, blocks, weight_block, 0)
        if owners == 1:
            leave((slice(0, 1), slice(0, out_at)))
        d_out = dot_nn(routed_t_ref[...], att_ref[...])
        put(d_out.astype(BF16), everything, out_at, own_rows, 0)
        vectors_turned = acc_vec[...].T
        extra = acc_upb[...].T
        if owners > 1:
            extra = extra.reshape(owners, blocks, own_rows, LANES)
        for at in range(blocks):
            if owners > 1:
                part = extra[:, at].reshape(width, LANES)
            else:
                part = extra[at * width : (at + 1) * width]
            if at == 0:
                part = part + vectors_turned
            columns = slice(at * LANES, (at + 1) * LANES)
            put(part.astype(BF16), columns, out_at + own_rows, own_rows, 0)
        ending = slice(out_at, out_at + 2 * own_rows)
        leave((slice(0, 1), ending) if owners == 1 else (everything, everything, ending))
        for copy in leaves:
            copy.wait()
        if owners > 1:
            lax.fori_loop(0, blocks, block_waits, 0)


def attend_back_kernel(
    reach, head, first_seq, chained, bounds_ref, q_ref, grad_ref, side_ref, lse_ref, start_ref, *rest
):
    pieces = rest[:reach]
    rest = rest[reach + chained :]
    grad_q_ref, leave_ref, kv_buf, acc_kv, acc_q = rest
    seq = first_seq + pl.program_id(0)
    local = pieces[0].shape[1]
    half = local // 2
    for at in range(reach - 1):
        kv_buf[at] = pieces[at][0]
    acc_kv[...] = jnp.zeros_like(acc_kv)
    acc_q[...] = jnp.zeros_like(acc_q)
    queries = by_halves(q_ref)
    grads = by_halves(grad_ref)
    side = side_ref[...].T
    inner_rows = [side[head + at : head + at + 1] for at in range(2)]
    starts = row_halves(start_ref[0])
    inners = [
        jnp.concatenate([row[:, at * half : (at + 1) * half] for row in inner_rows], 1)
        for at in range(2)
    ]
    log_sums = [lse_ref[0, at : at + 1] for at in range(2)]

    def one_group(group, keyval, keys_turned, mask):
        scores = mask(dot_nt(keyval, queries[group]))
        probs = jnp.exp(scores - log_sums[group])
        grad_probs = dot_nt(keyval, grads[group])
        grad_scores = (probs * (grad_probs - inners[group])).astype(BF16)
        acc_q[group] += dot_nn(keys_turned, grad_scores)
        return dot_nn(grad_scores, queries[group]) + dot_nn(probs.astype(BF16), grads[group])

    def turned_keys(keyval):
        return keyval.T[:head]

    def step(at):
        keyval = kv_buf[at]
        turned = turned_keys(keyval)
        added = []
        for group in range(2):

            def mask(scores):
                return masked(scores, starts[group], at * local)

            added.append(one_group(group, keyval, turned, mask))
        acc_kv[at] += added[0] + added[1]

    over_pieces(step, bounds_ref, seq, reach, local)
    own = pieces[reach - 1][0]
    own_at = (reach - 1) * local
    turned = turned_keys(own)
    for group in range(2):
        keys = half * (group + 1)
        added = one_group(
            group,
            own[:keys],
            turned[:, :keys],
            lambda scores: masked(scores, starts[group], own_at, own_at + group * half),
        )
        acc_kv[reach - 1, :keys] += added
    groups = []
    for group in range(2):
        grad_q = acc_q[group] * (head**-0.5)
        groups.append(jnp.concatenate([grad_q, jnp.zeros_like(grad_q)], 0).T.astype(BF16))
    from_halves(grad_q_ref, groups)
    shards = leave_ref.shape[0]
    me = bounds_ref[bounds_ref.shape[0] - 1]
    for at in range(shards):

        @pl.when((at > me) | (at <= me - reach))
        def _():
            leave_ref[at, 0] = jnp.zeros((local, LANES), BF16)

    for at in range(reach):
        target = me - (reach - 1) + at

        @pl.when(target >= 0)
        def _():
            leave_ref[target, 0] = acc_kv[at].astype(BF16)


def query_grad_kernel(
    experts,
    head,
    hidden_ref,
    grad_q_ref,
    grad_logit_ref,
    weight_ref,
    partial_ref,
    d_query_ref,
    d_router_ref,
    acc_query,
    acc_router,
):
    step, last = pl.program_id(0), pl.num_programs(0) - 1
    rows, width = hidden_ref.shape
    inner = experts * head

    @pl.when(step == 0)
    def _():
        acc_query[...] = jnp.zeros_like(acc_query)
        acc_router[...] = jnp.zeros_like(acc_router)

    side = grad_logit_ref[...]
    first = side[:, head + 2 : head + 3].astype(jnp.int32)
    second = side[:, head + 3 : head + 4].astype(jnp.int32)
    owner = lax.div(lanes_of(rows, inner), head)
    unfold = unfold_matrix(inner, head, 0)
    grad_queries = jnp.where(
        owner == first,
        dot_nn(grad_q_ref[0], unfold),
        jnp.where(owner == second, dot_nn(grad_q_ref[1], unfold), 0.0),
    ).astype(BF16)
    grad_logits = jnp.where(lanes_of(rows, LANES) < experts, side, 0.0)
    logit_high = grad_logits.astype(BF16)
    logit_low = (grad_logits - logit_high.astype(F32)).astype(BF16)
    router = weight_ref[:, inner + LANES :]
    partial_ref[...] = (
        dot_nt(grad_queries, weight_ref[:, :inner])
        + dot_nt(logit_high, router)
        + dot_nt(logit_low, router)
    ).astype(BF16)
    hidden_t = hidden_ref[...].T
    acc_query[...] += dot_nn(hidden_t, grad_queries)
    acc_router[...] += dot_nn(hidden_t, logit_high) + dot_nn(hidden_t, logit_low)

    @pl.when(step == last)
    def _():
        d_query_ref[...] = acc_query[...].astype(BF16)
        d_router_ref[...] = acc_router[...]


def last_kernel(
    experts,
    head,
    parts,
    core_ref,
    x_ref,
    hidden_ref,
    partial_ref,
    grad_mid_ref,
    query_ref,
    router_ref,
    weight_ref,
    *rest,
):
    pieces = rest[: len(parts)]
    grad_in_ref, *leaving, acc_kv, acc_vec, summed_ref = rest[len(parts) :]
    step, last = pl.program_id(0), pl.num_programs(0) - 1
    rows, width = x_ref.shape
    inner = experts * head

    @pl.when(step == 0)
    def _():
        acc_kv[...] = jnp.zeros_like(acc_kv)
        acc_vec[...] = jnp.zeros_like(acc_vec)

    for piece, (low, high) in zip(pieces, parts):

        @pl.when((step >= low) & (step < high))
        def _():
            per_step = piece.shape[1] // (high - low)
            base = (step - low) * per_step
            summed = piece[0, pl.ds(base, per_step)].astype(F32)
            for at in range(1, piece.shape[0]):
                summed = summed + piece[at, pl.ds(base, per_step)].astype(F32)
            summed_ref[...] = summed.astype(BF16).reshape(summed_ref.shape)

    gain = rows_of(weight_ref[:, inner + LANES :], (experts,))[0:1]
    normed, inv_dev = normalize(x_ref[...].astype(F32))
    grad_keyvals = summed_ref[...]
    grad_hidden = partial_ref[...].astype(F32) + dot_nt(grad_keyvals, weight_ref[:, inner : inner + LANES])
    grad_in_ref[...] = grad_mid_ref[...].astype(F32) + norm_back(grad_hidden, gain, normed, inv_dev)
    hidden_t = hidden_ref[...].T
    acc_kv[...] += dot_nn(hidden_t, grad_keyvals)
    acc_vec[experts : experts + 1] += jnp.sum(grad_hidden * normed, 0, keepdims=True)
    acc_vec[experts + 1 : experts + 2] += jnp.sum(grad_hidden, 0, keepdims=True)

    @pl.when(step == last)
    def _():
        extra = router_ref[...] + acc_vec[...].T
        for value, low in (
            (query_ref[...], 0),
            (acc_kv[...].astype(BF16), inner),
            (extra.astype(BF16), inner + LANES),
        ):
            columns = slice(low, low + value.shape[1])
            if len(leaving) == 1:
                leaving[0][:, columns] = value
                continue
            keep_ref, send_ref = leaving
            planes, seqs, own_rows = keep_ref.shape[:3]
            by_core = value.reshape(planes, 2, seqs, own_rows, value.shape[1])
            other = core_ref[0] == 1
            keep_ref[:, :, :, columns] = jnp.where(other, by_core[:, 1], by_core[:, 0])
            send_ref[:, :, :, columns] = jnp.where(other, by_core[:, 0], by_core[:, 1])


def finish_second_kernel(kept_ref, last_ref, down_ref, up_ref, out_ref, up_bias_ref, *vector_refs):
    ff_rows, width = down_ref.shape
    own_rows, ff = up_ref.shape
    blocks = ff // width
    total = kept_ref[...].astype(F32) + last_ref[...].astype(F32)
    down_ref[...] = total[:ff_rows]
    for at in range(blocks):
        low = ff_rows + at * own_rows
        up_ref[:, at * width : (at + 1) * width] = total[low : low + own_rows]
    low = ff_rows + blocks * own_rows
    out_ref[...] = total[low : low + own_rows]
    turned = total[low + own_rows :].T
    up_bias_ref[...] = jnp.concatenate([turned[at * LANES + 8] for at in range(blocks)], 0)
    for at, ref in enumerate(vector_refs):
        ref[...] = turned[at]


def finish_first_kernel(count, *refs):
    query_ref, kv_ref, router_ref, gain_ref, bias_ref = refs[count:]
    total = refs[0][...].astype(F32)
    for ref in refs[1:count]:
        total = total + ref[...].astype(F32)
    inner, pair, experts = query_ref.shape[1], kv_ref.shape[1], router_ref.shape[0]
    query_ref[...] = total[:, :inner]
    kv_ref[...] = total[:, inner : inner + pair]
    turned = total[:, inner + LANES :].T
    router_ref[...] = turned[:experts]
    gain_ref[...] = turned[experts]
    bias_ref[...] = turned[experts + 1]


def whole_spec(shape):
    zeros = (0,) * len(shape)
    return pl.BlockSpec(shape, lambda *_: zeros, pipeline_mode=pl.Buffered(1))


def row_spec(rows, columns):
    return pl.BlockSpec((rows, columns), lambda i, *_: (i, 0))


def pair_spec(rows):
    return pl.BlockSpec((2, rows, LANES), lambda i, *_: (0, i, 0))


def swapped(value, axis, mask):
    count = lax.axis_size(axis)
    return lax.ppermute(value, axis, [(at, at ^ mask) for at in range(count)])


def passed_along(value, axis, steps):
    count = lax.axis_size(axis)
    leading, last = (max(0, -steps), min(count, count - steps))
    return lax.ppermute(value, axis, [(source, source + steps) for source in range(leading, last)])


def spread(shard):
    dp, seq = lax.axis_size("dp"), lax.axis_size("seq")
    along = [shard] + [swapped(shard, "dp", 2 * at) for at in range(1, dp // 2)]
    held = jnp.stack(along)
    held = jnp.stack([held] + [swapped(held, "seq", at) for at in range(1, seq)])
    return held, swapped(held, "dp", 1)


def at_index(value, index, dim):
    return lax.dynamic_index_in_dim(value, index, dim, keepdims=False)


def core_halved(value):
    core = lax.axis_index("dp") % 2
    return at_index(value, core, 1) + swapped(at_index(value, 1 - core, 1), "dp", 1)


def summed_direct(value, dim, axis, scale):
    me = lax.axis_index(axis) // scale
    total = at_index(value, me, dim).astype(F32)
    for at in range(1, value.shape[dim]):
        total = total + swapped(at_index(value, me ^ at, dim), axis, at * scale).astype(F32)
    return total


def together(*values):
    return lax.optimization_barrier(values)


def on_device(
    block_in,
    routes,
    segments,
    cotangent,
    ln1_gain,
    ln1_bias,
    query_weight,
    kv_weight,
    router_weight,
    out_weight,
    ln2_gain,
    ln2_bias,
    up_weight,
    up_bias,
    down_weight,
    down_bias,
):
    micro_count, seq_count, local_len, width = block_in.shape
    full_len = segments.shape[2]
    experts = router_weight.shape[1]
    head = kv_weight.shape[1] // 2
    inner = experts * head
    ff = up_weight.shape[1]
    dp, shards = lax.axis_size("dp"), lax.axis_size("seq")
    devices = dp * shards
    own_rows, ff_rows, blocks = width // devices, ff // devices, ff // width
    aligned = own_rows % 16 == 0
    batch = micro_count * seq_count
    rows_all = batch * local_len
    tile = seq_count * local_len
    longest = full_len * 3 // 4
    reach = min(shards, (longest - 2) // local_len + 2)
    own_shard = lax.axis_index("seq")
    start_pos = own_shard * local_len

    def padded(value, columns):
        return jnp.pad(value, ((0, 0), (0, columns - value.shape[1])))

    a_cols = inner + 2 * LANES
    if aligned:
        packed_a, packed_b = pl.pallas_call(
            pack_kernel,
            out_shape=[
                jax.ShapeDtypeStruct((own_rows, a_cols), BF16),
                jax.ShapeDtypeStruct((ff_rows + (blocks + 1) * own_rows, width), BF16),
            ],
            compiler_params=call_params(),
            name="pack",
        )(
            query_weight,
            kv_weight,
            router_weight.T,
            down_weight,
            up_weight,
            out_weight,
            ln1_gain,
            ln1_bias,
            ln2_gain,
            ln2_bias,
            down_bias,
            up_bias,
        )
    else:
        rows = jnp.concatenate([ln1_gain, ln1_bias, ln2_gain, ln2_bias, down_bias, up_bias])
        rows = rows.reshape(5 + blocks, own_rows)
        extra = padded(jnp.concatenate([router_weight, rows.T], 1), LANES)
        packed_a = jnp.concatenate([query_weight, kv_weight, extra], 1)
        packed_b = jnp.concatenate(
            [down_weight]
            + [up_weight[:, at * width : (at + 1) * width] for at in range(blocks)]
            + [out_weight],
            0,
        )
    mine_a, mate_a = spread(packed_a)
    place = jnp.stack(
        [lax.axis_index("dp") // 2, lax.axis_index("dp") % 2, lax.axis_index("seq")]
    ).astype(jnp.int32)
    place_a = place
    if not aligned:
        held = jnp.moveaxis(jnp.stack([mine_a, mate_a]), 2, 0)
        for dim, at in ((0, 0), (1, 1), (2, 2)):
            order = jnp.arange(held.shape[dim], dtype=jnp.int32) ^ place[at]
            held = jnp.take(held, order, axis=dim)
        held = held.reshape(2, width // 2, a_cols)
        mine_a, mate_a = held[:1, None], held[1:, None]
        place_a = jnp.zeros_like(place)
    group_b = lax.all_gather(packed_b, ("dp", "seq"), axis=0, tiled=False)
    up_at, out_at = ff_rows, ff_rows + blocks * own_rows
    if aligned:
        weights = group_b
    else:
        up_all = group_b[:, up_at:out_at].reshape(devices, blocks, own_rows, width)
        weights = jnp.concatenate(
            [
                group_b[:, :ff_rows].reshape(ff, width),
                jnp.moveaxis(up_all, 0, 1).reshape(ff, width),
                group_b[:, out_at:].reshape(width, width),
            ],
            0,
        )[None]

    tokens = block_in.reshape(rows_all, width)
    grad_out = cotangent.reshape(rows_all, width)
    route_rows = routes.reshape(rows_all, 2)

    seg_rows = segments.reshape(batch, full_len)
    seg_local = lax.dynamic_slice_in_dim(seg_rows, start_pos, local_len, 1)
    doc_start = jnp.sum(
        (seg_rows[:, None, :] < seg_local[:, :, None]).astype(jnp.int32), -1, dtype=jnp.int32
    )
    doc_start = jnp.maximum(doc_start - (own_shard - (reach - 1)) * local_len, 0)
    bounds = jnp.concatenate([doc_start[:, 0], own_shard.reshape(1).astype(jnp.int32)])
    starts = doc_start.reshape(batch, 1, local_len)

    steps = micro_count
    hidden, keyvals, group_a = pl.pallas_call(
        functools.partial(keyval_kernel, experts, head),
        grid=(steps,),
        in_specs=[
            pl.BlockSpec(memory_space=pltpu.SMEM),
            row_spec(tile, width),
            whole_spec(mine_a.shape),
            whole_spec(mate_a.shape),
        ],
        out_specs=[row_spec(tile, width), row_spec(tile, LANES), whole_spec((width, a_cols))],
        out_shape=[
            jax.ShapeDtypeStruct((rows_all, width), BF16),
            jax.ShapeDtypeStruct((rows_all, LANES), BF16),
            jax.ShapeDtypeStruct((width, a_cols), BF16),
        ],
        scratch_shapes=[
            pltpu.VMEM((2 * mine_a.shape[0] * mine_a.shape[1],) + mine_a.shape[2:], BF16)
        ],
        compiler_params=call_params(),
        cost_estimate=cost(2 * rows_all * width * LANES, rows_all * width * 4),
        name="keyval",
    )(place_a, tokens, mine_a, mate_a)

    own_pieces = keyvals.reshape(batch, local_len, LANES)
    pieces = [own_pieces] + [passed_along(own_pieces, "seq", back) for back in range(1, reach)]
    pieces = pieces[::-1]

    queries, gates = pl.pallas_call(
        functools.partial(query_kernel, experts, head),
        grid=(steps,),
        in_specs=[row_spec(tile, width), row_spec(tile, 2), whole_spec((width, a_cols))],
        out_specs=[pair_spec(tile), row_spec(tile, LANES)],
        out_shape=[
            jax.ShapeDtypeStruct((2, rows_all, LANES), BF16),
            jax.ShapeDtypeStruct((rows_all, LANES), F32),
        ],
        compiler_params=call_params(),
        cost_estimate=cost(2 * rows_all * width * (a_cols + 512), rows_all * width * 4),
        name="query",
    )(hidden, route_rows, group_a)

    columns = group_a[:, inner + LANES :].astype(F32)
    small = jnp.pad(columns[:, experts + 2 : experts + 5].T, ((0, 4), (0, ff - width)))
    up_row = columns[:, experts + 5 : experts + 5 + blocks]
    up_row = jnp.swapaxes(up_row.reshape(devices, own_rows, blocks), 1, 2).reshape(1, ff)
    vectors = jnp.concatenate([up_row, small], 0)

    piece_spec = pl.BlockSpec((1, local_len, LANES), lambda b, *_: (b, 0, 0))
    q_spec = pl.BlockSpec((2, local_len, LANES), lambda b, *_: (0, b, 0))
    start_spec = pl.BlockSpec((1, 1, local_len), lambda b, *_: (b, 0, 0))
    lse_spec = pl.BlockSpec((1, 2, local_len), lambda b, *_: (b, 0, 0))
    pairs = rows_all * full_len
    mixed, lse = pl.pallas_call(
        functools.partial(attend_kernel, reach, head),
        grid_spec=pltpu.PrefetchScalarGridSpec(
            num_scalar_prefetch=1,
            grid=(batch,),
            in_specs=[q_spec, start_spec] + [piece_spec] * reach,
            out_specs=[q_spec, lse_spec],
            scratch_shapes=[
                pltpu.VMEM((reach, local_len, LANES), BF16),
                pltpu.VMEM((2, local_len), F32),
                pltpu.VMEM((2, local_len), F32),
                pltpu.VMEM((2, head, local_len), F32),
            ],
        ),
        out_shape=[
            jax.ShapeDtypeStruct((2, rows_all, LANES), F32),
            jax.ShapeDtypeStruct((batch, 2, local_len), F32),
        ],
        compiler_params=call_params(),
        cost_estimate=cost(4 * pairs * LANES, rows_all * LANES * 16, pairs),
        name="attend",
    )(bounds, queries, starts, *pieces)

    grad_rows = ff_rows + (blocks + 2) * own_rows if aligned else ff + (blocks + 2) * width
    core_index = (lax.axis_index("dp") % 2).reshape(1).astype(jnp.int32)
    if aligned:
        leaving = [(dp // 2, shards, grad_rows, width)] * 2
    else:
        leaving = [(1, grad_rows, width)]
    block_out, grad_mid, grad_mixed, side, *grads_b = pl.pallas_call(
        functools.partial(mid_kernel, experts, head),
        grid=(steps,),
        in_specs=[
            row_spec(tile, width),
            row_spec(tile, width),
            row_spec(tile, LANES),
            pair_spec(tile),
            whole_spec((8, ff)),
            pl.BlockSpec(memory_space=pltpu.SMEM),
        ]
        + [pl.BlockSpec(memory_space=pl.ANY)],
        out_specs=[
            row_spec(tile, width),
            row_spec(tile, width),
            pair_spec(tile),
            row_spec(tile, LANES),
        ]
        + [pl.BlockSpec(memory_space=pl.ANY)] * len(leaving),
        out_shape=[
            jax.ShapeDtypeStruct((rows_all, width), BF16),
            jax.ShapeDtypeStruct((rows_all, width), BF16),
            jax.ShapeDtypeStruct((2, rows_all, LANES), BF16),
            jax.ShapeDtypeStruct((rows_all, LANES), F32),
        ]
        + [jax.ShapeDtypeStruct(shape, BF16) for shape in leaving],
        scratch_shapes=mid_scratch(rows_all, width, ff, weights.shape, leaving),
        compiler_params=call_params(),
        cost_estimate=cost(6 * rows_all * width * (2 * ff + width), rows_all * width * 16),
        name="mid",
    )(tokens, grad_out, gates, mixed, vectors, core_index, weights)

    if not aligned:
        parts = grads_b[0][0]
        down_part = parts[:ff].reshape(devices, ff_rows, width)
        up_part = parts[ff : 2 * ff].reshape(blocks, devices, own_rows, width)
        up_part = jnp.moveaxis(up_part, 0, 1).reshape(devices, blocks * own_rows, width)
        out_part = parts[2 * ff : 2 * ff + width].reshape(devices, own_rows, width)
        tail = parts[2 * ff + width :]
        rows_up = tail.reshape(width, blocks, LANES)[:, :, 8].T.reshape(devices, own_rows, blocks)
        rows_vec = tail[:, :8].reshape(devices, own_rows, 8)
        rows_up = jnp.moveaxis(rows_up.reshape(devices, blocks, own_rows), 1, 2)
        tail = jnp.zeros((devices, own_rows, blocks, LANES), BF16)
        tail = tail.at[:, :, :, 8].set(rows_up).at[:, :, 0, :8].set(rows_vec)
        tail = tail.reshape(devices, own_rows, width)
        packed = jnp.concatenate([down_part, up_part, out_part, tail], 1)
        packed = packed.reshape((dp // 2, 2, shards) + packed.shape[1:])
        grads_b = [at_index(packed, core_index[0], 1), at_index(packed, 1 - core_index[0], 1)]

    keep, send = grads_b
    bits, z_bits = shards.bit_length() - 1, (dp // 2).bit_length() - 1
    along_x = [("seq", 1 << at) for at in range(bits // 2)]
    along_y = [("seq", 1 << at) for at in range(bits // 2, bits)]
    along_z = [("dp", 2 << at) for at in range(z_bits)]
    near, far = along_z[:1], along_z[1:]
    dims = along_z[::-1] + along_y[::-1] + along_x[::-1]
    orders = [along_x + along_y + near, along_y + near + along_x, near + along_x + along_y]
    third = -(-keep.shape[2] // 24) * 8 if keep.shape[2] % 8 == 0 else -(-keep.shape[2] // 3)
    cuts = [0, third, 2 * third, keep.shape[2]]
    held = keep + swapped(send, "dp", 1)
    held = held.reshape((2,) * len(dims) + held.shape[2:])
    parts = [
        (held[..., low:high, :], dims, order)
        for low, high, order in zip(cuts[:-1], cuts[1:], orders)
    ]

    def send_parts(parts):
        stays, arrives = [], []
        for value, left, order in parts:
            axis, mask = order[0]
            dim, bit = left.index(order[0]), (lax.axis_index(axis) // mask) % 2
            left = left[:dim] + left[dim + 1 :]
            stays.append((at_index(value, bit, dim), left, order[1:]))
            arrives.append(swapped(at_index(value, 1 - bit, dim), axis, mask))
        return stays, arrives

    def behind(parts, other):
        *values, other = together(*[value for value, _, _ in parts], other)
        return [(value,) + part[1:] for value, part in zip(values, parts)], other

    def joined(parts, arrives):
        return [(part[0] + piece,) + part[1:] for part, piece in zip(parts, arrives)]

    leave_spec = pl.BlockSpec((shards, 1, local_len, LANES), lambda b, *_: (0, b, 0, 0))

    parts, arrives = send_parts(parts)
    parts, bounds_now = behind(parts, bounds)
    grad_queries = None
    returned = []
    splits = [0, max(1, micro_count - 1), micro_count] if micro_count > 1 else [0, 1]
    for micro, stop in zip(splits[:-1], splits[1:]):
        count = (stop - micro) * seq_count

        def at_micro(block, dims, base=micro * seq_count):
            if dims == "b":
                return pl.BlockSpec(block, lambda b, *_: (base + b, 0, 0))
            return pl.BlockSpec(block, lambda b, *_: (0, base + b, 0))

        q_at = at_micro((2, local_len, LANES), "q")
        in_specs = [
            q_at,
            q_at,
            pl.BlockSpec(
                (local_len, LANES), lambda b, *_, base=micro * seq_count: (base + b, 0)
            ),
            at_micro((1, 2, local_len), "b"),
            at_micro((1, 1, local_len), "b"),
        ]
        in_specs += [at_micro((1, local_len, LANES), "b")] * reach
        operands = in_hbm(queries, grad_mixed, side, lse, starts, *pieces)
        aliases = {}
        if micro:
            in_specs.append(pl.BlockSpec(memory_space=pl.ANY))
            operands += in_hbm(grad_queries)
            aliases = {len(operands): 0}
        grad_queries, leave = pl.pallas_call(
            functools.partial(
                attend_back_kernel, reach, head, micro * seq_count, int(micro > 0)
            ),
            grid_spec=pltpu.PrefetchScalarGridSpec(
                num_scalar_prefetch=1,
                grid=(count,),
                in_specs=in_specs,
                out_specs=[q_at, leave_spec],
                scratch_shapes=[
                    pltpu.VMEM((reach, local_len, LANES), BF16),
                    pltpu.VMEM((reach, local_len, LANES), F32),
                    pltpu.VMEM((2, head, local_len), F32),
                ],
            ),
            out_shape=[
                pltpu.HBM((2, rows_all, LANES), BF16),
                jax.ShapeDtypeStruct((shards, count, local_len, LANES), BF16),
            ],
            input_output_aliases=aliases,
            compiler_params=call_params(28),
            cost_estimate=cost(
                10 * pairs * LANES * count // batch,
                count * local_len * LANES * 32,
                pairs * count // batch,
            ),
            name="attend_back",
        )(bounds_now, *operands)
        returned.append(lax.all_to_all(leave, "seq", 0, 0, tiled=True))
        if parts[0][2]:
            *arrives, grad_queries = together(*arrives, grad_queries)
            parts, arrives = send_parts(joined(parts, arrives))
            if stop < micro_count:
                parts, bounds_now = behind(parts, bounds)
            else:
                parts, side = behind(parts, side)

    partial_hidden, d_query, d_router = pl.pallas_call(
        functools.partial(query_grad_kernel, experts, head),
        grid=(steps,),
        in_specs=[
            row_spec(tile, width),
            pair_spec(tile),
            row_spec(tile, LANES),
            whole_spec((width, a_cols)),
        ],
        out_specs=[
            row_spec(tile, width),
            whole_spec((width, inner)),
            whole_spec((width, LANES)),
        ],
        out_shape=[
            jax.ShapeDtypeStruct((rows_all, width), BF16),
            jax.ShapeDtypeStruct((width, inner), BF16),
            jax.ShapeDtypeStruct((width, LANES), F32),
        ],
        scratch_shapes=[pltpu.VMEM((width, inner), F32), pltpu.VMEM((width, LANES), F32)],
        compiler_params=call_params(28),
        cost_estimate=cost(4 * rows_all * width * a_cols, rows_all * width * 12),
        name="query_grad",
    )(*in_hbm(hidden, grad_queries, side, group_a))
    *arrives, d_router = together(*arrives, d_router)
    parts = joined(parts, arrives)
    while parts[0][2]:
        parts = joined(*send_parts(parts))
    whole = jnp.concatenate([value for value, _, _ in parts], -2)
    parts, arrives = send_parts([(whole, parts[0][1], far)])
    parts, d_router = behind(parts, d_router)
    if aligned:
        small_shapes = [(dp // 2, shards, own_rows, a_cols)] * 2
    else:
        small_shapes = [(width, a_cols)]
    grad_in, *small = pl.pallas_call(
        functools.partial(last_kernel, experts, head, tuple(zip(splits[:-1], splits[1:]))),
        grid=(steps,),
        in_specs=[
            pl.BlockSpec(memory_space=pltpu.SMEM),
            row_spec(tile, width),
            row_spec(tile, width),
            row_spec(tile, width),
            row_spec(tile, width),
            whole_spec((width, inner)),
            whole_spec((width, LANES)),
            whole_spec((width, a_cols)),
        ]
        + [whole_spec(piece.shape) for piece in returned],
        out_specs=[row_spec(tile, width)] + [whole_spec(shape) for shape in small_shapes],
        out_shape=[
            jax.ShapeDtypeStruct((rows_all, width), F32),
        ]
        + [jax.ShapeDtypeStruct(shape, BF16) for shape in small_shapes],
        scratch_shapes=[
            pltpu.VMEM((width, LANES), F32),
            pltpu.VMEM((LANES, width), F32),
            pltpu.VMEM((tile, LANES), BF16),
        ],
        compiler_params=call_params(28),
        cost_estimate=cost(4 * rows_all * width * LANES, rows_all * width * 16),
        name="last",
    )(
        core_index,
        *in_hbm(tokens, hidden),
        partial_hidden,
        *in_hbm(grad_mid, d_query),
        d_router,
        *in_hbm(group_a, *returned),
    )
    if not aligned:
        by_core = small[0].reshape(dp // 2, 2, shards, own_rows, a_cols)
        small = [at_index(by_core, core_index[0], 1), at_index(by_core, 1 - core_index[0], 1)]
    keep_small, send_small = small
    *arrives, send_small = together(*arrives, send_small)
    while parts[0][2]:
        parts, arrives = send_parts(joined(parts, arrives))
    own_b = (parts[0][0], arrives[0])
    held = keep_small + swapped(send_small, "dp", 1)
    held = summed_direct(held, 1, "seq", 1).astype(BF16)
    z_me = lax.axis_index("dp") // 2
    ends = [at_index(held, z_me, 0)]
    ends += [swapped(at_index(held, z_me ^ at, 0), "dp", 2 * at) for at in range(1, dp // 2)]

    out_at_b, tail_at = ff_rows + blocks * own_rows, ff_rows + (blocks + 1) * own_rows
    if aligned:
        vector_shape = jax.ShapeDtypeStruct((own_rows,), F32)
        grad_down, grad_up, grad_out_weight, grad_up_bias, *second_vectors = pl.pallas_call(
            finish_second_kernel,
            out_shape=[
                jax.ShapeDtypeStruct((ff_rows, width), F32),
                jax.ShapeDtypeStruct((own_rows, ff), F32),
                jax.ShapeDtypeStruct((own_rows, width), F32),
                jax.ShapeDtypeStruct((ff_rows,), F32),
            ]
            + [vector_shape] * 3,
            compiler_params=call_params(),
            name="finish_second",
        )(*own_b)
        grad_query, grad_kv, grad_router, *first_vectors = pl.pallas_call(
            functools.partial(finish_first_kernel, len(ends)),
            out_shape=[
                jax.ShapeDtypeStruct((own_rows, inner), F32),
                jax.ShapeDtypeStruct((own_rows, 2 * head), F32),
                jax.ShapeDtypeStruct((experts, own_rows), F32),
            ]
            + [vector_shape] * 2,
            compiler_params=call_params(),
            name="finish_first",
        )(*ends)
        grad_router = grad_router.T
    else:
        own_b = own_b[0].astype(F32) + own_b[1].astype(F32)
        total = sum([piece.astype(F32) for piece in ends])
        ends = own_b[tail_at:]
        grad_up = jnp.concatenate(
            [
                own_b[ff_rows + at * own_rows : ff_rows + (at + 1) * own_rows]
                for at in range(blocks)
            ],
            1,
        )
        grad_up_bias = jnp.concatenate([ends[:, at * LANES + 8] for at in range(blocks)])
        grad_down, grad_out_weight = own_b[:ff_rows], own_b[out_at_b:tail_at]
        second_vectors = [ends[:, at] for at in range(3)]
        grad_query, grad_kv = total[:, :inner], total[:, inner : inner + 2 * head]
        total = total[:, inner + LANES :]
        grad_router = total[:, :experts]
        first_vectors = [total[:, experts], total[:, experts + 1]]
    return (
        block_out.reshape(block_in.shape),
        grad_in.reshape(block_in.shape),
        first_vectors[0],
        first_vectors[1],
        grad_query,
        grad_kv,
        grad_router,
        grad_out_weight,
        second_vectors[0],
        second_vectors[1],
        grad_up,
        grad_up_bias,
        grad_down,
        second_vectors[2],
    )


def solution(mesh):
    rows = P(("dp", "seq"), None)
    vector = P(("dp", "seq"))
    data = P(None, "dp", "seq", None)
    weights = (
        vector,
        vector,
        rows,
        rows,
        rows,
        rows,
        vector,
        vector,
        rows,
        vector,
        rows,
        vector,
    )
    return jax.shard_map(
        on_device,
        mesh=mesh,
        in_specs=(data, data, P(None, "dp", None), data) + weights,
        out_specs=(data, data) + weights,
        check_vma=False,
    )
```

```python
import functools

import jax
import jax.numpy as jnp
from jax import lax
from jax.experimental import pallas as pl
from jax.experimental.pallas import tpu as pltpu
from jax.sharding import PartitionSpec as P

EPS = 1e-05
LANES = 128
MIB = 1024 * 1024
BF16 = jnp.bfloat16
F32 = jnp.float32


def call_params(mib=56):
    return pltpu.CompilerParams(vmem_limit_bytes=mib * MIB)


def in_hbm(*values):
    return [pltpu.with_memory_space_constraint(value, pltpu.HBM) for value in values]


def cost(flops, bytes_accessed, transcendentals=0):
    return pl.CostEstimate(
        flops=int(flops), bytes_accessed=int(bytes_accessed), transcendentals=int(transcendentals)
    )


def dot_nn(left, right):
    return lax.dot_general(left, right, (((1,), (0,)), ((), ())), preferred_element_type=F32)


def dot_nt(left, right):
    return lax.dot_general(left, right, (((1,), (1,)), ((), ())), preferred_element_type=F32)


def lanes_of(rows, width):
    return lax.broadcasted_iota(jnp.int32, (rows, width), 1)


def fold_matrix(width, head, shift):
    source = lax.broadcasted_iota(jnp.int32, (width, LANES), 0)
    target = lax.broadcasted_iota(jnp.int32, (width, LANES), 1)
    return jnp.where(target == shift + lax.rem(source, head), 1.0, 0.0).astype(BF16)


def unfold_matrix(width, head, shift):
    source = lax.broadcasted_iota(jnp.int32, (LANES, width), 1)
    target = lax.broadcasted_iota(jnp.int32, (LANES, width), 0)
    return jnp.where(target == shift + lax.rem(source, head), 1.0, 0.0).astype(BF16)


def rows_of(columns, picked):
    row = lax.broadcasted_iota(jnp.int32, (8, LANES), 0)
    lane = lax.broadcasted_iota(jnp.int32, (8, LANES), 1)
    chosen = jnp.zeros((8, LANES), F32)
    for at, column in enumerate(picked):
        chosen = jnp.where((row == at) & (lane == column), 1.0, chosen)
    return dot_nt(chosen.astype(BF16), columns)


def normalize(values):
    centered = values - jnp.mean(values, -1, keepdims=True)
    inv_dev = lax.rsqrt(jnp.mean(centered * centered, -1, keepdims=True) + EPS)
    return centered * inv_dev, inv_dev


def norm_back(grad, gain, normed, inv_dev):
    scaled = grad * gain
    return inv_dev * (
        scaled
        - jnp.mean(scaled, -1, keepdims=True)
        - normed * jnp.mean(scaled * normed, -1, keepdims=True)
    )


def pack_kernel(query_ref, kv_ref, router_ref, down_ref, up_ref, out_ref, *rest):
    *vector_refs, up_bias_ref, first_ref, second_ref = rest
    own_rows, width = query_ref.shape
    first_ref[:, :width] = query_ref[...]
    first_ref[:, width : width + LANES] = kv_ref[...]
    rows = [router_ref[...].astype(F32)]
    rows += [ref[...].astype(F32).reshape(1, own_rows) for ref in vector_refs]
    bias = up_bias_ref[...].astype(F32).reshape(1, up_bias_ref.shape[0])
    rows += [
        bias[:, at * own_rows : (at + 1) * own_rows] for at in range(bias.shape[1] // own_rows)
    ]
    count = router_ref.shape[0] + len(rows) - 1
    rows.append(jnp.zeros((32 - count, own_rows), F32))
    rows = jnp.concatenate(rows, 0).astype(BF16)
    row = lax.broadcasted_iota(jnp.int32, (32, LANES), 0)
    lane = lax.broadcasted_iota(jnp.int32, (32, LANES), 1)
    chosen = jnp.where(lane == row, 1.0, 0.0).astype(BF16)
    turned = lax.dot_general(rows, chosen, (((0,), (0,)), ((), ())), preferred_element_type=F32)
    first_ref[:, width + LANES :] = turned.astype(BF16)
    ff_rows = down_ref.shape[0]
    second_ref[:ff_rows] = down_ref[...]
    blocks = up_ref.shape[1] // width
    for at in range(blocks):
        low = ff_rows + at * own_rows
        second_ref[low : low + own_rows] = up_ref[:, at * width : (at + 1) * width]
    second_ref[ff_rows + blocks * own_rows :] = out_ref[...]


def in_order(place_ref, parts, put):
    z_me, core_me, seq_me = place_ref[0], place_ref[1], place_ref[2]
    for core, part in enumerate(parts):
        for seq in range(part.shape[0]):
            for z in range(part.shape[1]):
                dp_at = (z_me ^ z) * 2 + (core_me ^ core)
                put(dp_at * part.shape[0] + (seq_me ^ seq), part[seq, z])


def keyval_kernel(experts, head, place_ref, x_ref, mine_ref, mate_ref, *rest):
    hidden_ref, kv_ref, weight_ref, blocks_ref = rest

    @pl.when(pl.program_id(0) == 0)
    def _():
        def put(device, block):
            blocks_ref[device] = block

        in_order(place_ref, (mine_ref, mate_ref), put)
        weight_ref[...] = blocks_ref[...].reshape(weight_ref.shape)

    inner = experts * head
    vectors = rows_of(weight_ref[:, inner + LANES :], (experts, experts + 1))
    normed, _ = normalize(x_ref[...].astype(F32))
    hidden = (normed * vectors[0:1] + vectors[1:2]).astype(BF16)
    hidden_ref[...] = hidden
    kv_ref[...] = dot_nn(hidden, weight_ref[:, inner : inner + LANES]).astype(BF16)


def query_kernel(experts, head, hidden_ref, routes_ref, weight_ref, q_ref, gate_ref):
    inner = experts * head
    hidden = hidden_ref[...]
    rows = hidden.shape[0]
    logits = dot_nn(hidden, weight_ref[:, inner + LANES :])
    lane = lanes_of(rows, LANES)
    first, second = routes_ref[:, 0:1], routes_ref[:, 1:2]
    logit_one = jnp.sum(jnp.where(lane == first, logits, 0.0), -1, keepdims=True)
    logit_two = jnp.sum(jnp.where(lane == second, logits, 0.0), -1, keepdims=True)
    peak = jnp.maximum(logit_one, logit_two)
    exp_one = jnp.exp(logit_one - peak)
    exp_two = jnp.exp(logit_two - peak)
    total = exp_one + exp_two
    gates = jnp.where(lane == 0, exp_one / total, jnp.where(lane == 1, exp_two / total, 0.0))
    gates = jnp.where(lane == 2, first.astype(F32), gates)
    gate_ref[...] = jnp.where(lane == 3, second.astype(F32), gates)
    queries = (dot_nn(hidden, weight_ref[:, :inner]) * (head**-0.5)).astype(BF16)
    owner = lax.div(lanes_of(rows, inner), head)
    fold = fold_matrix(inner, head, 0)
    zero = jnp.zeros_like(queries)
    q_ref[0] = dot_nn(jnp.where(owner == first, queries, zero), fold).astype(BF16)
    q_ref[1] = dot_nn(jnp.where(owner == second, queries, zero), fold).astype(BF16)


def masked(scores, start, key_at, query_at=None):
    keys = key_at + lax.broadcasted_iota(jnp.int32, scores.shape, 0)
    seen = keys >= start
    if query_at is not None:
        lane = lax.broadcasted_iota(jnp.int32, (1, scores.shape[1]), 1)
        seen = seen & (keys <= query_at + lax.rem(lane, scores.shape[1] // 2))
    return jnp.where(seen, scores, -1e30)


def by_halves(ref):
    half = ref.shape[1] // 2
    return [
        jnp.concatenate([ref[0, at * half : (at + 1) * half], ref[1, at * half : (at + 1) * half]], 0)
        for at in range(2)
    ]


def from_halves(ref, groups):
    half = ref.shape[1] // 2
    for at, group in enumerate(groups):
        ref[0, at * half : (at + 1) * half] = group[:half]
        ref[1, at * half : (at + 1) * half] = group[half:]


def row_halves(row):
    half = row.shape[1] // 2
    return [
        jnp.concatenate([row[:, at * half : (at + 1) * half]] * 2, 1) for at in range(2)
    ]


def over_pieces(step, bounds_ref, seq, reach, local):
    low = jnp.minimum(bounds_ref[seq] // local, reach - 1)

    def body(at, carry):
        step(at)
        return carry

    lax.fori_loop(low, reach - 1, body, 0)


def attend_kernel(reach, head, bounds_ref, q_ref, start_ref, *rest):
    pieces = rest[:reach]
    mixed_ref, lse_ref, kv_buf, peak_ref, total_ref, acc_ref = rest[reach:]
    seq = pl.program_id(0)
    local = pieces[0].shape[1]
    half = local // 2
    for at in range(reach - 1):
        kv_buf[at] = pieces[at][0]
    queries = by_halves(q_ref)
    starts = row_halves(start_ref[0])
    peak_ref[...] = jnp.full_like(peak_ref, -1e30)
    total_ref[...] = jnp.zeros_like(total_ref)
    acc_ref[...] = jnp.zeros_like(acc_ref)

    def turned_values(keyval):
        return keyval.T[head:]

    def accumulate(group, scores, values):
        old = peak_ref[group : group + 1]
        peak = jnp.maximum(old, jnp.max(scores, 0, keepdims=True))
        fade = jnp.exp(old - peak)
        expo = jnp.exp(scores - peak)
        total_ref[group : group + 1] = total_ref[group : group + 1] * fade + jnp.sum(
            expo, 0, keepdims=True
        )
        acc_ref[group] = acc_ref[group] * fade + dot_nn(values, expo.astype(BF16))
        peak_ref[group : group + 1] = peak

    def step(at):
        keyval = kv_buf[at]
        values = turned_values(keyval)
        for group in range(2):
            scores = masked(dot_nt(keyval, queries[group]), starts[group], at * local)
            accumulate(group, scores, values)

    over_pieces(step, bounds_ref, seq, reach, local)
    own = pieces[reach - 1][0]
    own_at = (reach - 1) * local
    values = turned_values(own)
    for group in range(2):
        keys = half * (group + 1)
        scores = masked(
            dot_nt(own[:keys], queries[group]), starts[group], own_at, own_at + group * half
        )
        accumulate(group, scores, values[:, :keys])
    groups = []
    for group in range(2):
        mixed = acc_ref[group] / total_ref[group : group + 1]
        groups.append(jnp.concatenate([jnp.zeros_like(mixed), mixed], 0).T)
    from_halves(mixed_ref, groups)
    lse_ref[0] = peak_ref[...] + jnp.log(total_ref[...])


def summed_by(values, chosen):
    matrix = jnp.where(chosen, 1.0, 0.0).astype(BF16)
    high = values.astype(BF16)
    low = (values - high.astype(F32)).astype(BF16)
    return dot_nn(high, matrix) + dot_nn(low, matrix)


def mid_scratch(rows_all, width, ff, weights, leaving):
    return (
        [pltpu.VMEM((rows_all, ff), BF16)] * 2
        + [pltpu.VMEM((width, rows_all), BF16)] * 3
        + [pltpu.VMEM((rows_all, width), BF16)]
        + [pltpu.VMEM((LANES, width), F32), pltpu.VMEM((LANES, ff), F32)]
        + [pltpu.VMEM(weights, BF16)]
        + [pltpu.VMEM(shape, BF16) for shape in leaving]
        + [pltpu.SemaphoreType.DMA((3,)), pltpu.SemaphoreType.DMA((2 + 4 * ff // width,))]
    )


def mid_kernel(
    experts,
    head,
    x_ref,
    dy_ref,
    gate_ref,
    mixed_ref,
    vector_ref,
    core_ref,
    weight_ref,
    out_ref,
    grad_mid_ref,
    grad_mixed_ref,
    side_ref,
    *rest,
):
    owners = weight_ref.shape[0]
    count = 2 if owners > 1 else 1
    leaving, rest = rest[:count], rest[count:]
    active_ref, grad_ref, dy_t_ref, second_t_ref, routed_t_ref, att_ref = rest[:6]
    acc_vec, acc_upb, kept_ref = rest[6:9]
    staged, (in_sems, out_sems) = rest[9 : 9 + count], rest[9 + count :]
    step, last = pl.program_id(0), pl.num_programs(0) - 1
    rows, width = x_ref.shape
    inner = experts * head
    own_rows = width // owners
    ff = active_ref.shape[1]
    ff_rows = ff // owners
    blocks = ff // width
    up_at, out_at = ff_rows, ff_rows + blocks * own_rows

    spans = ((out_at, out_at + own_rows), (0, ff_rows), (up_at, out_at))
    loads = [
        pltpu.make_async_copy(
            weight_ref.at[:, low:high, :], kept_ref.at[:, low:high, :], in_sems.at[at]
        )
        for at, (low, high) in enumerate(spans)
    ]

    @pl.when(step == 0)
    def _():
        for load in loads:
            load.start()
        acc_vec[...] = jnp.zeros_like(acc_vec)
        acc_upb[...] = jnp.zeros_like(acc_upb)
        loads[0].wait()

    gain, shift = vector_ref[1:2, :width], vector_ref[2:3, :width]
    down_bias = vector_ref[3:4, :width]
    gate_one, gate_two = gate_ref[:, 0:1], gate_ref[:, 1:2]
    first, second = gate_ref[:, 2:3].astype(jnp.int32), gate_ref[:, 3:4].astype(jnp.int32)
    owner = lax.div(lanes_of(rows, inner), head)
    unfold = unfold_matrix(inner, head, head)
    fold = fold_matrix(inner, head, head)
    wo = kept_ref[:, out_at : out_at + own_rows, :].reshape(inner, width)
    mixed_one, mixed_two = mixed_ref[0], mixed_ref[1]
    routed_one = dot_nn((gate_one * mixed_one).astype(BF16), unfold)
    routed_two = dot_nn((gate_two * mixed_two).astype(BF16), unfold)
    routed = jnp.where(
        owner == first, routed_one, jnp.where(owner == second, routed_two, 0.0)
    )
    routed = routed.astype(BF16)
    middle = x_ref[...].astype(F32) + dot_nn(routed, wo)
    normed, inv_dev = normalize(middle)
    second_low = (normed * gain + shift).astype(BF16)
    dy = dy_ref[...]
    dy_wide = dy.astype(F32)
    here = pl.ds(pl.multiple_of(step * rows, rows), rows)
    second_t_ref[:, here] = second_low.T
    dy_t_ref[:, here] = dy.T
    routed_t_ref[:, here] = routed.T
    per_block = width // ff_rows if owners > 1 else 1

    @pl.when(step == 0)
    def _():
        loads[1].wait()
        loads[2].wait()

    def down_block(at):
        if owners > 1:
            block = kept_ref[at * per_block : (at + 1) * per_block, :ff_rows, :]
            return block.reshape(width, width)
        return kept_ref[0, at * width : (at + 1) * width, :]

    def up_block(at):
        low = up_at + at * own_rows
        return kept_ref[:, low : low + own_rows, :].reshape(width, width)

    def ahead(at):
        lo = at * width
        pre_act = dot_nn(second_low, up_block(at)) + vector_ref[0:1, lo : lo + width]
        return pre_act, dot_nt(dy, down_block(at)).astype(BF16)

    ready = ahead(0)
    branch = middle + down_bias
    gsec = jnp.zeros_like(middle)
    for at in range(blocks):
        lo = at * width
        pre_act, grad_active = ready
        if at + 1 < blocks:
            ready = ahead(at + 1)
        sigma = jax.nn.sigmoid(pre_act)
        active = (pre_act * sigma).astype(BF16)
        slope = sigma * (1.0 + pre_act * (1.0 - sigma))
        grad_low = (grad_active.astype(F32) * slope).astype(BF16)
        active_ref[here, lo : lo + width] = active
        grad_ref[here, lo : lo + width] = grad_low
        branch = branch + dot_nn(active, down_block(at))
        gsec = gsec + dot_nt(grad_low, up_block(at))
        acc_upb[8:9, lo : lo + width] += jnp.sum(grad_low.astype(F32), 0, keepdims=True)

    out_ref[...] = branch.astype(BF16)
    acc_vec[0:1] += jnp.sum(gsec * normed, 0, keepdims=True)
    acc_vec[1:2] += jnp.sum(gsec, 0, keepdims=True)
    acc_vec[2:3] += jnp.sum(dy_wide, 0, keepdims=True)
    grad_mid = dy_wide + norm_back(gsec, gain, normed, inv_dev)
    grad_att = grad_mid.astype(BF16)
    grad_mid_ref[...] = grad_att
    att_ref[here, :] = grad_att
    grad_routed = dot_nt(grad_att, wo).astype(BF16)
    zero = jnp.zeros_like(grad_routed)
    picked_one = dot_nn(jnp.where(owner == first, grad_routed, zero), fold)
    picked_two = dot_nn(jnp.where(owner == second, grad_routed, zero), fold)
    grad_mixed_one = (gate_one * picked_one).astype(BF16)
    grad_mixed_two = (gate_two * picked_two).astype(BF16)
    grad_mixed_ref[0] = grad_mixed_one
    grad_mixed_ref[1] = grad_mixed_two
    spread_one = lax.broadcasted_iota(jnp.int32, (2 * LANES, 2 * LANES), 0) // LANES
    spread_two = lax.broadcasted_iota(jnp.int32, (2 * LANES, 2 * LANES), 1) // LANES
    sums = summed_by(
        jnp.concatenate([picked_one * mixed_one, picked_two * mixed_two], 1),
        spread_one == spread_two,
    )
    grad_one, grad_two = sums[:, :LANES], sums[:, LANES:]
    source = lax.broadcasted_iota(jnp.int32, (2 * LANES, LANES), 0) // LANES
    target = lax.broadcasted_iota(jnp.int32, (2 * LANES, LANES), 1)
    inners = summed_by(
        jnp.concatenate(
            [grad_mixed_one.astype(F32) * mixed_one, grad_mixed_two.astype(F32) * mixed_two], 1
        ),
        target == head + source,
    )
    common = gate_one * grad_one + gate_two * grad_two
    lane = lanes_of(rows, LANES)
    side = jnp.where(lane == first, gate_one * (grad_one - common), inners)
    side = jnp.where(lane == second, gate_two * (grad_two - common), side)
    side = jnp.where(lane == head + 2, gate_ref[:, 2:3], side)
    side_ref[...] = jnp.where(lane == head + 3, gate_ref[:, 3:4], side)

    @pl.when(step == last)
    def _():
        leaves = []

        def put(value, columns, row, count, group):
            if owners == 1:
                staged[0][0, row : row + value.shape[0], columns] = value
                return
            seqs = staged[0].shape[1]
            by_core = value.reshape(value.shape[0] // (2 * seqs * count), 2, seqs, count, -1)
            planes = by_core.shape[0]
            other = core_ref[0] == 1
            low, high = by_core[:, 0], by_core[:, 1]
            where = (slice(group * planes, (group + 1) * planes), slice(None), slice(row, row + count))
            staged[0][where + (columns,)] = jnp.where(other, high, low)
            staged[1][where + (columns,)] = jnp.where(other, low, high)

        def leave(where):
            for source, target in zip(staged, leaving):
                copy = pltpu.make_async_copy(
                    source.at[where], target.at[where], out_sems.at[len(leaves)]
                )
                copy.start()
                leaves.append(copy)

        everything = slice(None)

        def weight_block(at, carry):
            columns = pl.ds(pl.multiple_of(at * width, width), width)
            turned = dot_nn(dy_t_ref[...], active_ref[:, columns]).T.astype(BF16)
            straight = dot_nn(second_t_ref[...], grad_ref[:, columns]).astype(BF16)
            low = up_at + at * own_rows
            if owners == 1:
                staged[0][0, pl.ds(at * width, width), :] = turned
                staged[0][0, pl.ds(low, width), :] = straight
                return carry
            seqs = staged[0].shape[1]
            other = core_ref[0] == 1
            for value, rows_each, planes in ((turned, ff_rows, 1), (straight, own_rows, blocks)):
                by_core = value.reshape(-1, 2, seqs, rows_each, width)
                first_half, second_half = by_core[:, 0], by_core[:, 1]
                if planes == 1:
                    count = by_core.shape[0]
                    where = (pl.ds(at * count, count), everything, slice(0, ff_rows))
                else:
                    low = pl.multiple_of(up_at + at * own_rows, own_rows)
                    where = (everything, everything, pl.ds(low, own_rows))
                staged[0][where] = jnp.where(other, second_half, first_half)
                staged[1][where] = jnp.where(other, first_half, second_half)
                for copy in block_copies(at, planes > 1):
                    copy.start()
            return carry

        def block_copies(at, straight):
            count = staged[0].shape[0] // blocks
            if straight:
                low = pl.multiple_of(up_at + at * own_rows, own_rows)
                where = (everything, everything, pl.ds(low, own_rows))
            else:
                where = (pl.ds(at * count, count), everything, slice(0, ff_rows))
            base = 2 + 4 * at + 2 * int(straight)
            return [
                pltpu.make_async_copy(source.at[where], target.at[where], out_sems.at[base + side])
                for side, (source, target) in enumerate(zip(staged, leaving))
            ]

        def block_waits(at, carry):
            for straight in (False, True):
                for copy in block_copies(at, straight):
                    copy.wait()
            return carry

        lax.fori_loop(0, blocks, weight_block, 0)
        if owners == 1:
            leave((slice(0, 1), slice(0, out_at)))
        d_out = dot_nn(routed_t_ref[...], att_ref[...])
        put(d_out.astype(BF16), everything, out_at, own_rows, 0)
        vectors_turned = acc_vec[...].T
        extra = acc_upb[...].T
        if owners > 1:
            extra = extra.reshape(owners, blocks, own_rows, LANES)
        for at in range(blocks):
            if owners > 1:
                part = extra[:, at].reshape(width, LANES)
            else:
                part = extra[at * width : (at + 1) * width]
            if at == 0:
                part = part + vectors_turned
            columns = slice(at * LANES, (at + 1) * LANES)
            put(part.astype(BF16), columns, out_at + own_rows, own_rows, 0)
        ending = slice(out_at, out_at + 2 * own_rows)
        leave((slice(0, 1), ending) if owners == 1 else (everything, everything, ending))
        for copy in leaves:
            copy.wait()
        if owners > 1:
            lax.fori_loop(0, blocks, block_waits, 0)


def attend_back_kernel(
    reach, head, first_seq, chained, bounds_ref, q_ref, grad_ref, side_ref, lse_ref, start_ref, *rest
):
    pieces = rest[:reach]
    rest = rest[reach + chained :]
    grad_q_ref, leave_ref, kv_buf, acc_kv, acc_q = rest
    seq = first_seq + pl.program_id(0)
    local = pieces[0].shape[1]
    half = local // 2
    for at in range(reach - 1):
        kv_buf[at] = pieces[at][0]
    acc_kv[...] = jnp.zeros_like(acc_kv)
    acc_q[...] = jnp.zeros_like(acc_q)
    queries = by_halves(q_ref)
    grads = by_halves(grad_ref)
    side = side_ref[...].T
    inner_rows = [side[head + at : head + at + 1] for at in range(2)]
    starts = row_halves(start_ref[0])
    inners = [
        jnp.concatenate([row[:, at * half : (at + 1) * half] for row in inner_rows], 1)
        for at in range(2)
    ]
    log_sums = [lse_ref[0, at : at + 1] for at in range(2)]

    def one_group(group, keyval, keys_turned, mask):
        scores = mask(dot_nt(keyval, queries[group]))
        probs = jnp.exp(scores - log_sums[group])
        grad_probs = dot_nt(keyval, grads[group])
        grad_scores = (probs * (grad_probs - inners[group])).astype(BF16)
        acc_q[group] += dot_nn(keys_turned, grad_scores)
        return dot_nn(grad_scores, queries[group]) + dot_nn(probs.astype(BF16), grads[group])

    def turned_keys(keyval):
        return keyval.T[:head]

    def step(at):
        keyval = kv_buf[at]
        turned = turned_keys(keyval)
        added = []
        for group in range(2):

            def mask(scores):
                return masked(scores, starts[group], at * local)

            added.append(one_group(group, keyval, turned, mask))
        acc_kv[at] += added[0] + added[1]

    over_pieces(step, bounds_ref, seq, reach, local)
    own = pieces[reach - 1][0]
    own_at = (reach - 1) * local
    turned = turned_keys(own)
    for group in range(2):
        keys = half * (group + 1)
        added = one_group(
            group,
            own[:keys],
            turned[:, :keys],
            lambda scores: masked(scores, starts[group], own_at, own_at + group * half),
        )
        acc_kv[reach - 1, :keys] += added
    groups = []
    for group in range(2):
        grad_q = acc_q[group] * (head**-0.5)
        groups.append(jnp.concatenate([grad_q, jnp.zeros_like(grad_q)], 0).T.astype(BF16))
    from_halves(grad_q_ref, groups)
    shards = leave_ref.shape[0]
    me = bounds_ref[bounds_ref.shape[0] - 1]
    for at in range(shards):

        @pl.when((at > me) | (at <= me - reach))
        def _():
            leave_ref[at, 0] = jnp.zeros((local, LANES), BF16)

    for at in range(reach):
        target = me - (reach - 1) + at

        @pl.when(target >= 0)
        def _():
            leave_ref[target, 0] = acc_kv[at].astype(BF16)


def query_grad_kernel(
    experts,
    head,
    hidden_ref,
    grad_q_ref,
    grad_logit_ref,
    weight_ref,
    partial_ref,
    d_query_ref,
    d_router_ref,
    acc_query,
    acc_router,
):
    step, last = pl.program_id(0), pl.num_programs(0) - 1
    rows, width = hidden_ref.shape
    inner = experts * head

    @pl.when(step == 0)
    def _():
        acc_query[...] = jnp.zeros_like(acc_query)
        acc_router[...] = jnp.zeros_like(acc_router)

    side = grad_logit_ref[...]
    first = side[:, head + 2 : head + 3].astype(jnp.int32)
    second = side[:, head + 3 : head + 4].astype(jnp.int32)
    owner = lax.div(lanes_of(rows, inner), head)
    unfold = unfold_matrix(inner, head, 0)
    grad_queries = jnp.where(
        owner == first,
        dot_nn(grad_q_ref[0], unfold),
        jnp.where(owner == second, dot_nn(grad_q_ref[1], unfold), 0.0),
    ).astype(BF16)
    grad_logits = jnp.where(lanes_of(rows, LANES) < experts, side, 0.0)
    logit_high = grad_logits.astype(BF16)
    logit_low = (grad_logits - logit_high.astype(F32)).astype(BF16)
    router = weight_ref[:, inner + LANES :]
    partial_ref[...] = (
        dot_nt(grad_queries, weight_ref[:, :inner])
        + dot_nt(logit_high, router)
        + dot_nt(logit_low, router)
    ).astype(BF16)
    hidden_t = hidden_ref[...].T
    acc_query[...] += dot_nn(hidden_t, grad_queries)
    acc_router[...] += dot_nn(hidden_t, logit_high) + dot_nn(hidden_t, logit_low)

    @pl.when(step == last)
    def _():
        d_query_ref[...] = acc_query[...].astype(BF16)
        d_router_ref[...] = acc_router[...]


def last_kernel(
    experts,
    head,
    parts,
    core_ref,
    x_ref,
    hidden_ref,
    partial_ref,
    grad_mid_ref,
    query_ref,
    router_ref,
    weight_ref,
    *rest,
):
    pieces = rest[: len(parts)]
    grad_in_ref, *leaving, acc_kv, acc_vec, summed_ref = rest[len(parts) :]
    step, last = pl.program_id(0), pl.num_programs(0) - 1
    rows, width = x_ref.shape
    inner = experts * head

    @pl.when(step == 0)
    def _():
        acc_kv[...] = jnp.zeros_like(acc_kv)
        acc_vec[...] = jnp.zeros_like(acc_vec)

    for piece, (low, high) in zip(pieces, parts):

        @pl.when((step >= low) & (step < high))
        def _():
            per_step = piece.shape[1] // (high - low)
            base = (step - low) * per_step
            summed = piece[0, pl.ds(base, per_step)].astype(F32)
            for at in range(1, piece.shape[0]):
                summed = summed + piece[at, pl.ds(base, per_step)].astype(F32)
            summed_ref[...] = summed.astype(BF16).reshape(summed_ref.shape)

    gain = rows_of(weight_ref[:, inner + LANES :], (experts,))[0:1]
    normed, inv_dev = normalize(x_ref[...].astype(F32))
    grad_keyvals = summed_ref[...]
    grad_hidden = partial_ref[...].astype(F32) + dot_nt(grad_keyvals, weight_ref[:, inner : inner + LANES])
    grad_in_ref[...] = grad_mid_ref[...].astype(F32) + norm_back(grad_hidden, gain, normed, inv_dev)
    hidden_t = hidden_ref[...].T
    acc_kv[...] += dot_nn(hidden_t, grad_keyvals)
    acc_vec[experts : experts + 1] += jnp.sum(grad_hidden * normed, 0, keepdims=True)
    acc_vec[experts + 1 : experts + 2] += jnp.sum(grad_hidden, 0, keepdims=True)

    @pl.when(step == last)
    def _():
        extra = router_ref[...] + acc_vec[...].T
        for value, low in (
            (query_ref[...], 0),
            (acc_kv[...].astype(BF16), inner),
            (extra.astype(BF16), inner + LANES),
        ):
            columns = slice(low, low + value.shape[1])
            if len(leaving) == 1:
                leaving[0][:, columns] = value
                continue
            keep_ref, send_ref = leaving
            planes, seqs, own_rows = keep_ref.shape[:3]
            by_core = value.reshape(planes, 2, seqs, own_rows, value.shape[1])
            other = core_ref[0] == 1
            keep_ref[:, :, :, columns] = jnp.where(other, by_core[:, 1], by_core[:, 0])
            send_ref[:, :, :, columns] = jnp.where(other, by_core[:, 0], by_core[:, 1])


def finish_second_kernel(kept_ref, last_ref, down_ref, up_ref, out_ref, up_bias_ref, *vector_refs):
    ff_rows, width = down_ref.shape
    own_rows, ff = up_ref.shape
    blocks = ff // width
    total = kept_ref[...].astype(F32) + last_ref[...].astype(F32)
    down_ref[...] = total[:ff_rows]
    for at in range(blocks):
        low = ff_rows + at * own_rows
        up_ref[:, at * width : (at + 1) * width] = total[low : low + own_rows]
    low = ff_rows + blocks * own_rows
    out_ref[...] = total[low : low + own_rows]
    turned = total[low + own_rows :].T
    up_bias_ref[...] = jnp.concatenate([turned[at * LANES + 8] for at in range(blocks)], 0)
    for at, ref in enumerate(vector_refs):
        ref[...] = turned[at]


def finish_first_kernel(count, *refs):
    query_ref, kv_ref, router_ref, gain_ref, bias_ref = refs[count:]
    total = refs[0][...].astype(F32)
    for ref in refs[1:count]:
        total = total + ref[...].astype(F32)
    inner, pair, experts = query_ref.shape[1], kv_ref.shape[1], router_ref.shape[0]
    query_ref[...] = total[:, :inner]
    kv_ref[...] = total[:, inner : inner + pair]
    turned = total[:, inner + LANES :].T
    router_ref[...] = turned[:experts]
    gain_ref[...] = turned[experts]
    bias_ref[...] = turned[experts + 1]


def whole_spec(shape):
    zeros = (0,) * len(shape)
    return pl.BlockSpec(shape, lambda *_: zeros, pipeline_mode=pl.Buffered(1))


def row_spec(rows, columns):
    return pl.BlockSpec((rows, columns), lambda i, *_: (i, 0))


def pair_spec(rows):
    return pl.BlockSpec((2, rows, LANES), lambda i, *_: (0, i, 0))


def swapped(value, axis, mask):
    count = lax.axis_size(axis)
    return lax.ppermute(value, axis, [(at, at ^ mask) for at in range(count)])


def passed_along(value, axis, steps):
    count = lax.axis_size(axis)
    leading, last = (max(0, -steps), min(count, count - steps))
    return lax.ppermute(value, axis, [(source, source + steps) for source in range(leading, last)])


def spread(shard):
    dp, seq = lax.axis_size("dp"), lax.axis_size("seq")
    along = [shard] + [swapped(shard, "dp", 2 * at) for at in range(1, dp // 2)]
    held = jnp.stack(along)
    held = jnp.stack([held] + [swapped(held, "seq", at) for at in range(1, seq)])
    return held, swapped(held, "dp", 1)


def at_index(value, index, dim):
    return lax.dynamic_index_in_dim(value, index, dim, keepdims=False)


def core_halved(value):
    core = lax.axis_index("dp") % 2
    return at_index(value, core, 1) + swapped(at_index(value, 1 - core, 1), "dp", 1)


def summed_direct(value, dim, axis, scale):
    me = lax.axis_index(axis) // scale
    total = at_index(value, me, dim).astype(F32)
    for at in range(1, value.shape[dim]):
        total = total + swapped(at_index(value, me ^ at, dim), axis, at * scale).astype(F32)
    return total


def together(*values):
    return lax.optimization_barrier(values)


def on_device(
    block_in,
    routes,
    segments,
    cotangent,
    ln1_gain,
    ln1_bias,
    query_weight,
    kv_weight,
    router_weight,
    out_weight,
    ln2_gain,
    ln2_bias,
    up_weight,
    up_bias,
    down_weight,
    down_bias,
):
    micro_count, seq_count, local_len, width = block_in.shape
    full_len = segments.shape[2]
    experts = router_weight.shape[1]
    head = kv_weight.shape[1] // 2
    inner = experts * head
    ff = up_weight.shape[1]
    dp, shards = lax.axis_size("dp"), lax.axis_size("seq")
    devices = dp * shards
    own_rows, ff_rows, blocks = width // devices, ff // devices, ff // width
    aligned = own_rows % 16 == 0
    batch = micro_count * seq_count
    rows_all = batch * local_len
    tile = seq_count * local_len
    longest = full_len * 3 // 4
    reach = min(shards, (longest - 2) // local_len + 2)
    own_shard = lax.axis_index("seq")
    start_pos = own_shard * local_len

    def padded(value, columns):
        return jnp.pad(value, ((0, 0), (0, columns - value.shape[1])))

    a_cols = inner + 2 * LANES
    if aligned:
        packed_a, packed_b = pl.pallas_call(
            pack_kernel,
            out_shape=[
                jax.ShapeDtypeStruct((own_rows, a_cols), BF16),
                jax.ShapeDtypeStruct((ff_rows + (blocks + 1) * own_rows, width), BF16),
            ],
            compiler_params=call_params(),
            name="pack",
        )(
            query_weight,
            kv_weight,
            router_weight.T,
            down_weight,
            up_weight,
            out_weight,
            ln1_gain,
            ln1_bias,
            ln2_gain,
            ln2_bias,
            down_bias,
            up_bias,
        )
    else:
        rows = jnp.concatenate([ln1_gain, ln1_bias, ln2_gain, ln2_bias, down_bias, up_bias])
        rows = rows.reshape(5 + blocks, own_rows)
        extra = padded(jnp.concatenate([router_weight, rows.T], 1), LANES)
        packed_a = jnp.concatenate([query_weight, kv_weight, extra], 1)
        packed_b = jnp.concatenate(
            [down_weight]
            + [up_weight[:, at * width : (at + 1) * width] for at in range(blocks)]
            + [out_weight],
            0,
        )
    mine_a, mate_a = spread(packed_a)
    place = jnp.stack(
        [lax.axis_index("dp") // 2, lax.axis_index("dp") % 2, lax.axis_index("seq")]
    ).astype(jnp.int32)
    place_a = place
    if not aligned:
        held = jnp.moveaxis(jnp.stack([mine_a, mate_a]), 2, 0)
        for dim, at in ((0, 0), (1, 1), (2, 2)):
            order = jnp.arange(held.shape[dim], dtype=jnp.int32) ^ place[at]
            held = jnp.take(held, order, axis=dim)
        held = held.reshape(2, width // 2, a_cols)
        mine_a, mate_a = held[:1, None], held[1:, None]
        place_a = jnp.zeros_like(place)
    group_b = lax.all_gather(packed_b, ("dp", "seq"), axis=0, tiled=False)
    up_at, out_at = ff_rows, ff_rows + blocks * own_rows
    if aligned:
        weights = group_b
    else:
        up_all = group_b[:, up_at:out_at].reshape(devices, blocks, own_rows, width)
        weights = jnp.concatenate(
            [
                group_b[:, :ff_rows].reshape(ff, width),
                jnp.moveaxis(up_all, 0, 1).reshape(ff, width),
                group_b[:, out_at:].reshape(width, width),
            ],
            0,
        )[None]

    tokens = block_in.reshape(rows_all, width)
    grad_out = cotangent.reshape(rows_all, width)
    route_rows = routes.reshape(rows_all, 2)

    seg_rows = segments.reshape(batch, full_len)
    seg_local = lax.dynamic_slice_in_dim(seg_rows, start_pos, local_len, 1)
    doc_start = jnp.sum(
        (seg_rows[:, None, :] < seg_local[:, :, None]).astype(jnp.int32), -1, dtype=jnp.int32
    )
    doc_start = jnp.maximum(doc_start - (own_shard - (reach - 1)) * local_len, 0)
    bounds = jnp.concatenate([doc_start[:, 0], own_shard.reshape(1).astype(jnp.int32)])
    starts = doc_start.reshape(batch, 1, local_len)

    steps = micro_count
    hidden, keyvals, group_a = pl.pallas_call(
        functools.partial(keyval_kernel, experts, head),
        grid=(steps,),
        in_specs=[
            pl.BlockSpec(memory_space=pltpu.SMEM),
            row_spec(tile, width),
            whole_spec(mine_a.shape),
            whole_spec(mate_a.shape),
        ],
        out_specs=[row_spec(tile, width), row_spec(tile, LANES), whole_spec((width, a_cols))],
        out_shape=[
            jax.ShapeDtypeStruct((rows_all, width), BF16),
            jax.ShapeDtypeStruct((rows_all, LANES), BF16),
            jax.ShapeDtypeStruct((width, a_cols), BF16),
        ],
        scratch_shapes=[
            pltpu.VMEM((2 * mine_a.shape[0] * mine_a.shape[1],) + mine_a.shape[2:], BF16)
        ],
        compiler_params=call_params(),
        cost_estimate=cost(2 * rows_all * width * LANES, rows_all * width * 4),
        name="keyval",
    )(place_a, tokens, mine_a, mate_a)

    own_pieces = keyvals.reshape(batch, local_len, LANES)
    pieces = [own_pieces] + [passed_along(own_pieces, "seq", back) for back in range(1, reach)]
    pieces = pieces[::-1]

    queries, gates = pl.pallas_call(
        functools.partial(query_kernel, experts, head),
        grid=(steps,),
        in_specs=[row_spec(tile, width), row_spec(tile, 2), whole_spec((width, a_cols))],
        out_specs=[pair_spec(tile), row_spec(tile, LANES)],
        out_shape=[
            jax.ShapeDtypeStruct((2, rows_all, LANES), BF16),
            jax.ShapeDtypeStruct((rows_all, LANES), F32),
        ],
        compiler_params=call_params(),
        cost_estimate=cost(2 * rows_all * width * (a_cols + 512), rows_all * width * 4),
        name="query",
    )(hidden, route_rows, group_a)

    columns = group_a[:, inner + LANES :].astype(F32)
    small = jnp.pad(columns[:, experts + 2 : experts + 5].T, ((0, 4), (0, ff - width)))
    up_row = columns[:, experts + 5 : experts + 5 + blocks]
    up_row = jnp.swapaxes(up_row.reshape(devices, own_rows, blocks), 1, 2).reshape(1, ff)
    vectors = jnp.concatenate([up_row, small], 0)

    piece_spec = pl.BlockSpec((1, local_len, LANES), lambda b, *_: (b, 0, 0))
    q_spec = pl.BlockSpec((2, local_len, LANES), lambda b, *_: (0, b, 0))
    start_spec = pl.BlockSpec((1, 1, local_len), lambda b, *_: (b, 0, 0))
    lse_spec = pl.BlockSpec((1, 2, local_len), lambda b, *_: (b, 0, 0))
    pairs = rows_all * full_len
    mixed, lse = pl.pallas_call(
        functools.partial(attend_kernel, reach, head),
        grid_spec=pltpu.PrefetchScalarGridSpec(
            num_scalar_prefetch=1,
            grid=(batch,),
            in_specs=[q_spec, start_spec] + [piece_spec] * reach,
            out_specs=[q_spec, lse_spec],
            scratch_shapes=[
                pltpu.VMEM((reach, local_len, LANES), BF16),
                pltpu.VMEM((2, local_len), F32),
                pltpu.VMEM((2, local_len), F32),
                pltpu.VMEM((2, head, local_len), F32),
            ],
        ),
        out_shape=[
            jax.ShapeDtypeStruct((2, rows_all, LANES), F32),
            jax.ShapeDtypeStruct((batch, 2, local_len), F32),
        ],
        compiler_params=call_params(),
        cost_estimate=cost(4 * pairs * LANES, rows_all * LANES * 16, pairs),
        name="attend",
    )(bounds, queries, starts, *pieces)

    grad_rows = ff_rows + (blocks + 2) * own_rows if aligned else ff + (blocks + 2) * width
    core_index = (lax.axis_index("dp") % 2).reshape(1).astype(jnp.int32)
    if aligned:
        leaving = [(dp // 2, shards, grad_rows, width)] * 2
    else:
        leaving = [(1, grad_rows, width)]
    block_out, grad_mid, grad_mixed, side, *grads_b = pl.pallas_call(
        functools.partial(mid_kernel, experts, head),
        grid=(steps,),
        in_specs=[
            row_spec(tile, width),
            row_spec(tile, width),
            row_spec(tile, LANES),
            pair_spec(tile),
            whole_spec((8, ff)),
            pl.BlockSpec(memory_space=pltpu.SMEM),
        ]
        + [pl.BlockSpec(memory_space=pl.ANY)],
        out_specs=[
            row_spec(tile, width),
            row_spec(tile, width),
            pair_spec(tile),
            row_spec(tile, LANES),
        ]
        + [pl.BlockSpec(memory_space=pl.ANY)] * len(leaving),
        out_shape=[
            jax.ShapeDtypeStruct((rows_all, width), BF16),
            jax.ShapeDtypeStruct((rows_all, width), BF16),
            jax.ShapeDtypeStruct((2, rows_all, LANES), BF16),
            jax.ShapeDtypeStruct((rows_all, LANES), F32),
        ]
        + [jax.ShapeDtypeStruct(shape, BF16) for shape in leaving],
        scratch_shapes=mid_scratch(rows_all, width, ff, weights.shape, leaving),
        compiler_params=call_params(),
        cost_estimate=cost(6 * rows_all * width * (2 * ff + width), rows_all * width * 16),
        name="mid",
    )(tokens, grad_out, gates, mixed, vectors, core_index, weights)

    if not aligned:
        parts = grads_b[0][0]
        down_part = parts[:ff].reshape(devices, ff_rows, width)
        up_part = parts[ff : 2 * ff].reshape(blocks, devices, own_rows, width)
        up_part = jnp.moveaxis(up_part, 0, 1).reshape(devices, blocks * own_rows, width)
        out_part = parts[2 * ff : 2 * ff + width].reshape(devices, own_rows, width)
        tail = parts[2 * ff + width :]
        rows_up = tail.reshape(width, blocks, LANES)[:, :, 8].T.reshape(devices, own_rows, blocks)
        rows_vec = tail[:, :8].reshape(devices, own_rows, 8)
        rows_up = jnp.moveaxis(rows_up.reshape(devices, blocks, own_rows), 1, 2)
        tail = jnp.zeros((devices, own_rows, blocks, LANES), BF16)
        tail = tail.at[:, :, :, 8].set(rows_up).at[:, :, 0, :8].set(rows_vec)
        tail = tail.reshape(devices, own_rows, width)
        packed = jnp.concatenate([down_part, up_part, out_part, tail], 1)
        packed = packed.reshape((dp // 2, 2, shards) + packed.shape[1:])
        grads_b = [at_index(packed, core_index[0], 1), at_index(packed, 1 - core_index[0], 1)]

    keep, send = grads_b
    bits, z_bits = shards.bit_length() - 1, (dp // 2).bit_length() - 1
    along_x = [("seq", 1 << at) for at in range(bits // 2)]
    along_y = [("seq", 1 << at) for at in range(bits // 2, bits)]
    along_z = [("dp", 2 << at) for at in range(z_bits)]
    near, far = along_z[:1], along_z[1:]
    dims = along_z[::-1] + along_y[::-1] + along_x[::-1]
    orders = [along_x + along_y + near, along_y + near + along_x, near + along_x + along_y]
    third = -(-keep.shape[2] // 24) * 8 if keep.shape[2] % 8 == 0 else -(-keep.shape[2] // 3)
    cuts = [0, third, 2 * third, keep.shape[2]]
    held = keep + swapped(send, "dp", 1)
    held = held.reshape((2,) * len(dims) + held.shape[2:])
    parts = [
        (held[..., low:high, :], dims, order)
        for low, high, order in zip(cuts[:-1], cuts[1:], orders)
    ]

    def send_parts(parts):
        stays, arrives = [], []
        for value, left, order in parts:
            axis, mask = order[0]
            dim, bit = left.index(order[0]), (lax.axis_index(axis) // mask) % 2
            left = left[:dim] + left[dim + 1 :]
            stays.append((at_index(value, bit, dim), left, order[1:]))
            arrives.append(swapped(at_index(value, 1 - bit, dim), axis, mask))
        return stays, arrives

    def behind(parts, other):
        *values, other = together(*[value for value, _, _ in parts], other)
        return [(value,) + part[1:] for value, part in zip(values, parts)], other

    def joined(parts, arrives):
        return [(part[0] + piece,) + part[1:] for part, piece in zip(parts, arrives)]

    leave_spec = pl.BlockSpec((shards, 1, local_len, LANES), lambda b, *_: (0, b, 0, 0))

    parts, arrives = send_parts(parts)
    parts, bounds_now = behind(parts, bounds)
    grad_queries = None
    returned = []
    splits = [0, max(1, micro_count - 1), micro_count] if micro_count > 1 else [0, 1]
    for micro, stop in zip(splits[:-1], splits[1:]):
        count = (stop - micro) * seq_count

        def at_micro(block, dims, base=micro * seq_count):
            if dims == "b":
                return pl.BlockSpec(block, lambda b, *_: (base + b, 0, 0))
            return pl.BlockSpec(block, lambda b, *_: (0, base + b, 0))

        q_at = at_micro((2, local_len, LANES), "q")
        in_specs = [
            q_at,
            q_at,
            pl.BlockSpec(
                (local_len, LANES), lambda b, *_, base=micro * seq_count: (base + b, 0)
            ),
            at_micro((1, 2, local_len), "b"),
            at_micro((1, 1, local_len), "b"),
        ]
        in_specs += [at_micro((1, local_len, LANES), "b")] * reach
        operands = in_hbm(queries, grad_mixed, side, lse, starts, *pieces)
        aliases = {}
        if micro:
            in_specs.append(pl.BlockSpec(memory_space=pl.ANY))
            operands += in_hbm(grad_queries)
            aliases = {len(operands): 0}
        grad_queries, leave = pl.pallas_call(
            functools.partial(
                attend_back_kernel, reach, head, micro * seq_count, int(micro > 0)
            ),
            grid_spec=pltpu.PrefetchScalarGridSpec(
                num_scalar_prefetch=1,
                grid=(count,),
                in_specs=in_specs,
                out_specs=[q_at, leave_spec],
                scratch_shapes=[
                    pltpu.VMEM((reach, local_len, LANES), BF16),
                    pltpu.VMEM((reach, local_len, LANES), F32),
                    pltpu.VMEM((2, head, local_len), F32),
                ],
            ),
            out_shape=[
                pltpu.HBM((2, rows_all, LANES), BF16),
                jax.ShapeDtypeStruct((shards, count, local_len, LANES), BF16),
            ],
            input_output_aliases=aliases,
            compiler_params=call_params(28),
            cost_estimate=cost(
                10 * pairs * LANES * count // batch,
                count * local_len * LANES * 32,
                pairs * count // batch,
            ),
            name="attend_back",
        )(bounds_now, *operands)
        returned.append(lax.all_to_all(leave, "seq", 0, 0, tiled=True))
        if parts[0][2]:
            *arrives, grad_queries = together(*arrives, grad_queries)
            parts, arrives = send_parts(joined(parts, arrives))
            if stop < micro_count:
                parts, bounds_now = behind(parts, bounds)
            else:
                parts, side = behind(parts, side)

    partial_hidden, d_query, d_router = pl.pallas_call(
        functools.partial(query_grad_kernel, experts, head),
        grid=(steps,),
        in_specs=[
            row_spec(tile, width),
            pair_spec(tile),
            row_spec(tile, LANES),
            whole_spec((width, a_cols)),
        ],
        out_specs=[
            row_spec(tile, width),
            whole_spec((width, inner)),
            whole_spec((width, LANES)),
        ],
        out_shape=[
            jax.ShapeDtypeStruct((rows_all, width), BF16),
            jax.ShapeDtypeStruct((width, inner), BF16),
            jax.ShapeDtypeStruct((width, LANES), F32),
        ],
        scratch_shapes=[pltpu.VMEM((width, inner), F32), pltpu.VMEM((width, LANES), F32)],
        compiler_params=call_params(28),
        cost_estimate=cost(4 * rows_all * width * a_cols, rows_all * width * 12),
        name="query_grad",
    )(*in_hbm(hidden, grad_queries, side, group_a))
    *arrives, d_router = together(*arrives, d_router)
    parts = joined(parts, arrives)
    while parts[0][2]:
        parts = joined(*send_parts(parts))
    whole = jnp.concatenate([value for value, _, _ in parts], -2)
    parts, arrives = send_parts([(whole, parts[0][1], far)])
    parts, d_router = behind(parts, d_router)
    if aligned:
        small_shapes = [(dp // 2, shards, own_rows, a_cols)] * 2
    else:
        small_shapes = [(width, a_cols)]
    grad_in, *small = pl.pallas_call(
        functools.partial(last_kernel, experts, head, tuple(zip(splits[:-1], splits[1:]))),
        grid=(steps,),
        in_specs=[
            pl.BlockSpec(memory_space=pltpu.SMEM),
            row_spec(tile, width),
            row_spec(tile, width),
            row_spec(tile, width),
            row_spec(tile, width),
            whole_spec((width, inner)),
            whole_spec((width, LANES)),
            whole_spec((width, a_cols)),
        ]
        + [whole_spec(piece.shape) for piece in returned],
        out_specs=[row_spec(tile, width)] + [whole_spec(shape) for shape in small_shapes],
        out_shape=[
            jax.ShapeDtypeStruct((rows_all, width), F32),
        ]
        + [jax.ShapeDtypeStruct(shape, BF16) for shape in small_shapes],
        scratch_shapes=[
            pltpu.VMEM((width, LANES), F32),
            pltpu.VMEM((LANES, width), F32),
            pltpu.VMEM((tile, LANES), BF16),
        ],
        compiler_params=call_params(28),
        cost_estimate=cost(4 * rows_all * width * LANES, rows_all * width * 16),
        name="last",
    )(
        core_index,
        *in_hbm(tokens, hidden),
        partial_hidden,
        *in_hbm(grad_mid, d_query),
        d_router,
        *in_hbm(group_a, *returned),
    )
    if not aligned:
        by_core = small[0].reshape(dp // 2, 2, shards, own_rows, a_cols)
        small = [at_index(by_core, core_index[0], 1), at_index(by_core, 1 - core_index[0], 1)]
    keep_small, send_small = small
    *arrives, send_small = together(*arrives, send_small)
    while parts[0][2]:
        parts, arrives = send_parts(joined(parts, arrives))
    own_b = (parts[0][0], arrives[0])
    held = keep_small + swapped(send_small, "dp", 1)
    held = summed_direct(held, 1, "seq", 1).astype(BF16)
    z_me = lax.axis_index("dp") // 2
    ends = [at_index(held, z_me, 0)]
    ends += [swapped(at_index(held, z_me ^ at, 0), "dp", 2 * at) for at in range(1, dp // 2)]

    out_at_b, tail_at = ff_rows + blocks * own_rows, ff_rows + (blocks + 1) * own_rows
    if aligned:
        vector_shape = jax.ShapeDtypeStruct((own_rows,), F32)
        grad_down, grad_up, grad_out_weight, grad_up_bias, *second_vectors = pl.pallas_call(
            finish_second_kernel,
            out_shape=[
                jax.ShapeDtypeStruct((ff_rows, width), F32),
                jax.ShapeDtypeStruct((own_rows, ff), F32),
                jax.ShapeDtypeStruct((own_rows, width), F32),
                jax.ShapeDtypeStruct((ff_rows,), F32),
            ]
            + [vector_shape] * 3,
            compiler_params=call_params(),
            name="finish_second",
        )(*own_b)
        grad_query, grad_kv, grad_router, *first_vectors = pl.pallas_call(
            functools.partial(finish_first_kernel, len(ends)),
            out_shape=[
                jax.ShapeDtypeStruct((own_rows, inner), F32),
                jax.ShapeDtypeStruct((own_rows, 2 * head), F32),
                jax.ShapeDtypeStruct((experts, own_rows), F32),
            ]
            + [vector_shape] * 2,
            compiler_params=call_params(),
            name="finish_first",
        )(*ends)
        grad_router = grad_router.T
    else:
        own_b = own_b[0].astype(F32) + own_b[1].astype(F32)
        total = sum([piece.astype(F32) for piece in ends])
        ends = own_b[tail_at:]
        grad_up = jnp.concatenate(
            [
                own_b[ff_rows + at * own_rows : ff_rows + (at + 1) * own_rows]
                for at in range(blocks)
            ],
            1,
        )
        grad_up_bias = jnp.concatenate([ends[:, at * LANES + 8] for at in range(blocks)])
        grad_down, grad_out_weight = own_b[:ff_rows], own_b[out_at_b:tail_at]
        second_vectors = [ends[:, at] for at in range(3)]
        grad_query, grad_kv = total[:, :inner], total[:, inner : inner + 2 * head]
        total = total[:, inner + LANES :]
        grad_router = total[:, :experts]
        first_vectors = [total[:, experts], total[:, experts + 1]]
    return (
        block_out.reshape(block_in.shape),
        grad_in.reshape(block_in.shape),
        first_vectors[0],
        first_vectors[1],
        grad_query,
        grad_kv,
        grad_router,
        grad_out_weight,
        second_vectors[0],
        second_vectors[1],
        grad_up,
        grad_up_bias,
        grad_down,
        second_vectors[2],
    )


def solution(mesh):
    rows = P(("dp", "seq"), None)
    vector = P(("dp", "seq"))
    data = P(None, "dp", "seq", None)
    weights = (
        vector,
        vector,
        rows,
        rows,
        rows,
        rows,
        vector,
        vector,
        rows,
        vector,
        rows,
        vector,
    )
    return jax.shard_map(
        on_device,
        mesh=mesh,
        in_specs=(data, data, P(None, "dp", None), data) + weights,
        out_specs=(data, data) + weights,
        check_vma=False,
    )
```
